32 devices in a mesh: seq: 16 (over z, y, core), mp: 2 (over x).
Axes of the slice: x: 2, y: 2, z: 4, core: 2. Of those that a mesh axis runs over, the one named last changes fastest.
Arguments:
- tokens: float32 [8192, 1024], P('seq'), may hold values from -6 to 6
- window_state: float32 [2, 1024, 16], P(None, ('seq', 'mp')), may hold values from -6 to 6
- norm1_gain: float32 [1024], replicated, may hold values from 0.5 to 1.5
- norm1_bias: float32 [1024], replicated, may hold values from -3 to 3
- in_coef: float32 [1024, 16], P(('seq', 'mp')), may hold values from -0.375 to 0.375
- out_coef: float32 [1024, 16], P(('seq', 'mp')), may hold values from -4 to 4
- decay_rate: float32 [1024, 16], P(('seq', 'mp')), may hold values from 6.1035156e-05 to 0.04
- skip_gain: float32 [1024], P(('seq', 'mp')), may hold values from 0.5 to 1.5
- qkv_weight: bfloat16 [3, 1024, 1024], P(None, None, 'mp'), may hold values from -0.1875 to 0.1875
- out_weight: bfloat16 [1024, 1024], P('mp'), may hold values from -0.75 to 0.75
- norm2_gain: float32 [1024], replicated, may hold values from 0.5 to 1.5
- norm2_bias: float32 [1024], replicated, may hold values from -3 to 3
- up_weight: bfloat16 [1024, 4096], P(None, 'mp'), may hold values from -0.1875 to 0.1875
- up_bias: float32 [4096], P('mp'), may hold values from -3 to 3
- down_weight: bfloat16 [4096, 1024], P('mp'), may hold values from -0.1875 to 0.1875
- down_bias: float32 [1024], replicated, may hold values from -3 to 3
- cotangent: float32 [8192, 1024], P('seq'), may hold values from -6 to 6
Outputs:
- result: float32 [8192, 1024], P('seq')
- grad_tokens: float32 [8192, 1024], P('seq')
- grad_norm1_gain: float32 [1024], replicated
- grad_norm1_bias: float32 [1024], replicated
- grad_in_coef: float32 [1024, 16], P(('seq', 'mp'))
- grad_out_coef: float32 [1024, 16], P(('seq', 'mp'))
- grad_decay_rate: float32 [1024, 16], P(('seq', 'mp'))
- grad_skip_gain: float32 [1024], P(('seq', 'mp'))
- grad_qkv_weight: float32 [3, 1024, 1024], P(None, None, 'mp')
- grad_out_weight: float32 [1024, 1024], P('mp')
- grad_norm2_gain: float32 [1024], replicated
- grad_norm2_bias: float32 [1024], replicated
- grad_up_weight: float32 [1024, 4096], P(None, 'mp')
- grad_up_bias: float32 [4096], P('mp')
- grad_down_weight: float32 [4096, 1024], P('mp')
- grad_down_bias: float32 [1024], replicated
The draws below stay inside these ranges and needn't reach their ends.
All inputs are finite; a program needn't handle non-finite values.
Results may differ from the reference program's by a relative error of at most 0.002.
Values sent between devices are 32-bit elements; how exact they have to be, the bound alone decides.
No kernel may reach another device: no remote copies, remote signals or barrier semaphores. Data moves between devices by JAX's collectives and lax.ppermute only.
A program may use at most 192 MiB of HBM per device.

```python
import math
import jax
import jax.numpy as jnp
from jax import lax

D = 1024
HEADS = 8
HDIM = 128
STATE = 16
FF = 4096
BLOCK = 512
CTX = 128
LEN = 4096
TOKENS = 8192
NSEQ = 2


def block_scale(key, extent, cuts, low, largest):
    def one(dim, shards_of):
        steps = jax.random.uniform(jax.random.fold_in(jax.random.fold_in(key, 6), dim), (shards_of,), jnp.float32, low / len(cuts), largest / len(cuts))
        return jnp.repeat(jnp.exp(steps), extent[dim] // shards_of).reshape((-1,) + (1,) * (len(extent) - dim - 1))

    level = one(*cuts[0])
    for cut in cuts[1:]:
        level = level * one(*cut)
    return level


def gaussian(own_key, shape, scale, reach, shards=(), kind=jnp.bfloat16):
    drawn = jax.random.normal(own_key, shape, jnp.float32) * scale
    if len(shards) > 0:
        drawn = block_scale(own_key, shape, shards, -0.22, 0.18) * drawn
    return jnp.clip(drawn, min=-reach, max=reach).astype(kind)


def setup_inputs(seed: int = 0) -> dict:
    arg_keys = jax.random.split(jax.random.key(seed), 18)
    tokens = gaussian(arg_keys[0], (TOKENS, D), 1.0, 6.0, ((0, 16),), jnp.float32)
    window_state = gaussian(arg_keys[1], (NSEQ, D, STATE), 1.0, 6.0, ((1, 32),), jnp.float32)
    norm1_gain = jnp.clip(1.0 + 0.1 * jax.random.normal(arg_keys[2], (D,), jnp.float32), 0.5, 1.5)
    norm1_bias = gaussian(arg_keys[3], (D,), 0.5, 3.0, (), jnp.float32)
    in_coef = gaussian(arg_keys[4], (D, STATE), (1.5 / LEN ** 0.5), 0.375, ((0, 32),), jnp.float32)
    out_coef = gaussian(arg_keys[5], (D, STATE), 0.25, 4.0, ((0, 32),), jnp.float32)
    decay_rate = jnp.clip(jnp.exp(math.log(0.04) - 6.4851847 * jax.random.uniform(arg_keys[6], (D, STATE), jnp.float32) ** block_scale(arg_keys[6], (D, STATE), ((0, 32),), -0.2, 0.2)), 6.103515625e-05, 0.04)
    skip_gain = jnp.clip(0.5 + 1.0 * jax.random.uniform(arg_keys[7], (D,), jnp.float32) ** block_scale(arg_keys[7], (D,), ((0, 32),), -0.2, 0.2), 0.5, 1.5)
    qkv_weight = gaussian(arg_keys[8], (3, D, D), D ** -0.5, 0.1875, ((2, 2),))
    out_weight = gaussian(arg_keys[9], (D, D), (D // 16) ** -0.5, 0.75, ((0, 2),))
    norm2_gain = jnp.clip(1.0 + 0.1 * jax.random.normal(arg_keys[10], (D,), jnp.float32), 0.5, 1.5)
    norm2_bias = gaussian(arg_keys[11], (D,), 0.5, 3.0, (), jnp.float32)
    up_weight = gaussian(arg_keys[12], (D, FF), D ** -0.5, 0.1875, ((1, 2),))
    up_bias = gaussian(arg_keys[13], (FF,), 0.5, 3.0, ((0, 2),), jnp.float32)
    down_weight = gaussian(arg_keys[14], (FF, D), (FF // 4) ** -0.5, 0.1875, ((0, 2),))
    down_bias = gaussian(arg_keys[15], (D,), 0.5, 3.0, (), jnp.float32)
    cotangent = gaussian(arg_keys[16], (TOKENS, D), 1.0, 6.0, ((0, 16),), jnp.float32)
    return {"tokens": tokens, "window_state": window_state, "norm1_gain": norm1_gain, "norm1_bias": norm1_bias, "in_coef": in_coef, "out_coef": out_coef, "decay_rate": decay_rate, "skip_gain": skip_gain, "qkv_weight": qkv_weight, "out_weight": out_weight, "norm2_gain": norm2_gain, "norm2_bias": norm2_bias, "up_weight": up_weight, "up_bias": up_bias, "down_weight": down_weight, "down_bias": down_bias, "cotangent": cotangent}


@jax.custom_vjp
def low(v):
    return lax.optimization_barrier(v.astype(jnp.bfloat16)).astype(jnp.float32)

@jax.custom_vjp
def low_back(v):
    return v

def low_keep(v):
    return (low(v), None)

def low_pass(kept, grad):
    return (grad,)

def back_keep(v):
    return (v, None)

def back_low(kept, grad):
    return (low(grad),)
low.defvjp(low_keep, low_pass)
low_back.defvjp(back_keep, back_low)

def layer_norm(value, gain, bias):
    center = value - lax.optimization_barrier(jnp.mean(value, axis=-1, keepdims=True))
    spread = lax.optimization_barrier(jnp.mean(center * center, axis=-1, keepdims=True))
    return center * lax.rsqrt(spread + 1e-05) * gain + bias

def ssm_sequence(normed, state, in_coef, out_coef, decay_rate, skip_gain):
    steps_t = jnp.arange(LEN).astype(jnp.float32)[:, None]
    kernel = jnp.zeros((LEN, D), jnp.float32)
    start = jnp.zeros((LEN, D), jnp.float32)
    for index in range(STATE):
        fading = jnp.exp(-decay_rate[:, index] * steps_t)
        kernel = kernel + in_coef[:, index] * out_coef[:, index] * fading
        start = start + out_coef[:, index] * state[:, index] * (fading * jnp.exp(-decay_rate[:, index]))
    spectrum = jnp.fft.rfft(normed, n=2 * LEN, axis=0) * jnp.fft.rfft(kernel, n=2 * LEN, axis=0)
    conv = jnp.fft.irfft(spectrum, n=2 * LEN, axis=0)[:LEN]
    return conv + skip_gain * normed + start

def attend(normed, states, qkv, out_w):
    blocks = LEN // BLOCK
    highest = lax.Precision.HIGHEST
    padded = jnp.concatenate([jnp.zeros((CTX, D), jnp.float32), states], 0)[:LEN]
    context = padded.reshape(blocks, BLOCK, D)[:, :CTX]
    query = jnp.dot(normed, qkv[0], precision=highest).reshape(blocks, BLOCK, HEADS, HDIM)
    key_self = jnp.dot(normed, qkv[1], precision=highest).reshape(blocks, BLOCK, HEADS, HDIM)
    value_self = jnp.dot(normed, qkv[2], precision=highest).reshape(blocks, BLOCK, HEADS, HDIM)
    key_ctx = jnp.einsum('bcd,de->bce', context, qkv[1], precision=highest).reshape(blocks, CTX, HEADS, HDIM)
    value_ctx = jnp.einsum('bcd,de->bce', context, qkv[2], precision=highest).reshape(blocks, CTX, HEADS, HDIM)
    keys = jnp.concatenate([key_ctx, key_self], 1)
    values = jnp.concatenate([value_ctx, value_self], 1)
    scores = jnp.einsum('bqhe,bkhe->bhqk', query, keys, precision=highest) * HDIM ** (-0.5)
    rows_q = jnp.arange(BLOCK)[:, None]
    cols_k = jnp.arange(CTX + BLOCK)[None, :]
    ctx_ok = (jnp.arange(blocks) > 0)[:, None, None, None]
    allowed = jnp.where(cols_k < CTX, ctx_ok, (cols_k - CTX <= rows_q)[None, None])
    scores = jnp.where(allowed, scores, -1e+30)
    probs = jax.nn.softmax(scores, axis=-1)
    heads = jnp.einsum('bhqk,bkhe->bqhe', probs, values, precision=highest).reshape(LEN, D)
    return jnp.dot(heads, out_w, precision=highest)

def reference(tokens, window_state, norm1_gain, norm1_bias, in_coef, out_coef, decay_rate, skip_gain, qkv_weight, out_weight, norm2_gain, norm2_bias, up_weight, up_bias, down_weight, down_bias, cotangent):
    highest = lax.Precision.HIGHEST

    def forward(rows_all, gain1, bias1, coef_in, coef_out, rates, skips, qkv, out_w, gain2, bias2, up_w, up_b, down_w, down_b):

        def one_sequence(pair):
            rows, state = pair
            normed = layer_norm(rows, gain1, bias1)
            states = ssm_sequence(normed, state, coef_in, coef_out, rates, skips)
            mixed = rows + attend(normed, states, qkv, out_w)
            normed2 = layer_norm(mixed, gain2, bias2)
            hidden = jax.nn.gelu(jnp.dot(normed2, up_w, precision=highest) + up_b, approximate=False)
            return mixed + jnp.dot(hidden, down_w, precision=highest) + down_b
        outs = lax.map(jax.checkpoint(one_sequence), (rows_all.reshape(NSEQ, LEN, D), window_state))
        return outs.reshape(TOKENS, D)
    result, pull = jax.vjp(forward, tokens, norm1_gain, norm1_bias, in_coef, out_coef, decay_rate, skip_gain, qkv_weight.astype(jnp.float32), out_weight.astype(jnp.float32), norm2_gain, norm2_bias, up_weight.astype(jnp.float32), up_bias, down_weight.astype(jnp.float32), down_bias)
    grads = pull(cotangent)
    return (result, grads[0], grads[1], grads[2], grads[3], grads[4], grads[5], grads[6], grads[7], grads[8], grads[9], grads[10], grads[11], grads[12], grads[13], grads[14])
```

```python
import functools
import math

import jax
import jax.numpy as jnp
from jax import lax
from jax.experimental import pallas as pl
from jax.experimental.pallas import tpu as pltpu
from jax.sharding import PartitionSpec as P

HDIM = 128
BLOCK = 512
CTX = 128
LEN = 4096
EPS = 1e-05
HIGH = lax.Precision.HIGH


def mm(left, right, dims=((1,), (0,))):
    return lax.dot_general(
        left, right, (dims, ((), ())), precision=HIGH, preferred_element_type=jnp.float32
    )


def norm_parts(value):
    center = value - jnp.mean(value, axis=-1, keepdims=True)
    spread = jnp.mean(center * center, axis=-1, keepdims=True)
    rate = lax.rsqrt(spread + EPS)
    return center * rate, rate


def norm_back(grad, unit, rate, gain):
    scaled = grad * gain
    inner = jnp.mean(scaled * unit, axis=-1, keepdims=True)
    return rate * (scaled - jnp.mean(scaled, axis=-1, keepdims=True) - unit * inner)


def swap_bit(value, axis, bit):
    size = lax.axis_size(axis)
    return lax.ppermute(value, axis, [(i, i ^ (1 << bit)) for i in range(size)])


def bits_of(count):
    return count.bit_length() - 1


def shift_to(value, axis, distance):
    size = lax.axis_size(axis)
    route = [(i, i + distance) for i in range(size) if 0 <= i + distance < size]
    return lax.ppermute(value, axis, route)


def gather_all(piece):
    rows = piece.shape[0]
    mp_size, seq_size = lax.axis_size("mp"), lax.axis_size("seq")
    me = lax.axis_index("seq") * mp_size + lax.axis_index("mp")
    block, low = piece, 0
    for bit in range(bits_of(mp_size * seq_size)):
        axis, own = ("mp", bit) if bit < bits_of(mp_size) else ("seq", bit - bits_of(mp_size))
        other = swap_bit(block, axis, own)
        upper = (me >> bit) & 1
        block = jnp.where(
            upper == 1, jnp.concatenate([other, block], 0), jnp.concatenate([block, other], 0)
        )
    return block


def scatter_sum(whole):
    mp_size, seq_size = lax.axis_size("mp"), lax.axis_size("seq")
    me = lax.axis_index("seq") * mp_size + lax.axis_index("mp")
    block = whole
    for bit in reversed(range(bits_of(mp_size * seq_size))):
        axis, own = ("mp", bit) if bit < bits_of(mp_size) else ("seq", bit - bits_of(mp_size))
        half = block.reshape(2, block.shape[0] // 2, block.shape[1])
        upper = (me >> bit) & 1
        keep = lax.dynamic_index_in_dim(half, upper, 0, keepdims=False)
        give = lax.dynamic_index_in_dim(half, 1 - upper, 0, keepdims=False)
        block = keep + swap_bit(give, axis, own)
    return block


def sum_seq_small(value):
    for bit in range(bits_of(lax.axis_size("seq"))):
        value = value + swap_bit(value, "seq", bit)
    return value


def chip_order(count):
    if count <= 2:
        return list(range(count))
    return list(range(0, count, 2)) + list(range(count - 1 - count % 2, 0, -2))


def ring_route(count):
    order = chip_order(count)
    route = []
    for i in range(count):
        here, there = order[i], order[(i + 1) % count]
        route.append((2 * here, 2 * there))
        route.append((2 * there + 1, 2 * here + 1))
    return route


def pick(value, index):
    return lax.dynamic_index_in_dim(value, index, 0, keepdims=False)


def ring_sum(streams):
    count = lax.axis_size("seq") // 2
    order = chip_order(count)
    places = [0] * count
    for i, chip in enumerate(order):
        places[chip] = i
    me = lax.axis_index("seq")
    core = me % 2
    here = jnp.array(places, jnp.int32)[me // 2]
    place = jnp.where(core == 0, here, (count - here) % count)
    mirror = (count - place) % count
    route = ring_route(count)
    halves = []
    for value in streams:
        rows, cols = value.shape
        split = value.reshape(2, rows // 2, cols)
        mine = pick(split, core) + swap_bit(pick(split, 1 - core), "seq", 0)
        halves.append(mine.reshape(count, rows // 2 // count, cols))
    held = [pick(half, place) for half in halves]
    for step in range(count - 1):
        got = [lax.ppermute(part, "seq", route) for part in held]
        spot = (place + 2 * count - 1 - step) % count
        held = [new + pick(half, spot) for new, half in zip(got, halves)]
    outs = [jnp.zeros((2, count) + part.shape, part.dtype) for part in held]

    def put(whole, part, which, spot):
        return lax.dynamic_update_slice(whole, part[None, None], (which, spot % count, 0, 0))

    for step in range(count):
        spot, far = place + 1 - step + count, mirror + 1 - step + count
        outs = [put(whole, part, core, spot) for whole, part in zip(outs, held)]
        others = [swap_bit(part, "seq", 0) for part in held]
        outs = [put(whole, part, 1 - core, far) for whole, part in zip(outs, others)]
        if step < count - 1:
            held = [lax.ppermute(part, "seq", route) for part in held]
    return [whole.reshape(value.shape) for whole, value in zip(outs, streams)]


def summary_kernel(x_ref, fade_ref, h_ref, p_ref):
    fade = fade_ref[...]
    states = fade.shape[0]

    def octet(i, carry):
        h, p = carry
        tile = x_ref[pl.ds(pl.multiple_of(i * 8, 8), 8), :]
        for r in range(8):
            row = jnp.broadcast_to(tile[r : r + 1, :], fade.shape)
            p = fade * (p + h)
            h = fade * h + row
        return h, p

    zero = jnp.zeros(fade.shape, jnp.float32)
    h, p = lax.fori_loop(0, x_ref.shape[0] // 8, octet, (zero, zero))
    h_ref[...] = h
    p_ref[...] = p


def tail_kernel(x_ref, fade_ref, gate_ref, skip_ref, first_ref, y_ref):
    fade, gate, skip = fade_ref[...], gate_ref[...], skip_ref[...]

    def octet(i, u):
        base = pl.multiple_of(i * 8, 8)
        tile = x_ref[pl.ds(base, 8), :]
        rows = []
        for r in range(8):
            row = tile[r : r + 1, :]
            u = fade * u + gate * jnp.broadcast_to(row, fade.shape)
            rows.append(jnp.sum(u, axis=0, keepdims=True) + skip * row)
        y_ref[pl.ds(base, 8), :] = jnp.concatenate(rows, 0)
        return u

    lax.fori_loop(0, x_ref.shape[0] // 8, octet, first_ref[...])


def tail_back_kernel(
    x_ref, d_ref, fade_ref, gate_ref, skip_ref, q_ref, r_ref, dh_ref, dp_ref, dskip_ref, dx_ref
):
    fade, gate, skip = fade_ref[...], gate_ref[...], skip_ref[...]
    octets = x_ref.shape[0] // 8
    zero = jnp.zeros(fade.shape, jnp.float32)

    def forward(i, carry):
        h, p, dh, dp = carry
        base = pl.multiple_of(i * 8, 8)
        tile, grads = x_ref[pl.ds(base, 8), :], d_ref[pl.ds(base, 8), :]
        for r in range(8):
            p = fade * (p + h)
            h = fade * h + jnp.broadcast_to(tile[r : r + 1, :], fade.shape)
            grad = jnp.broadcast_to(grads[r : r + 1, :], fade.shape)
            dh = dh + grad * h
            dp = dp + grad * p
        return h, p, dh, dp

    _, _, dh, dp = lax.fori_loop(0, octets, forward, (zero, zero, zero, zero))
    dh_ref[...] = dh
    dp_ref[...] = dp
    dskip_ref[...] = jnp.sum(x_ref[...] * d_ref[...], axis=0, keepdims=True)

    def backward(k, carry):
        q, r_sum = carry
        base = pl.multiple_of((octets - 1 - k) * 8, 8)
        grads = d_ref[pl.ds(base, 8), :]
        rows = [None] * 8
        for r in reversed(range(8)):
            r_sum = fade * (r_sum + q)
            grad = grads[r : r + 1, :]
            q = fade * q + jnp.broadcast_to(grad, fade.shape)
            rows[r] = jnp.sum(gate * q, axis=0, keepdims=True) + skip * grad
        dx_ref[pl.ds(base, 8), :] = jnp.concatenate(rows, 0)
        return q, r_sum

    q, r_sum = lax.fori_loop(0, octets, backward, (zero, zero))
    q_ref[...] = q
    r_ref[...] = r_sum


def spread_kernel(first_ref, fade_ref, y_ref):
    fade = fade_ref[...]
    octets = y_ref.shape[0] // 8

    def octet(k, v):
        base = pl.multiple_of((octets - 1 - k) * 8, 8)
        rows = [None] * 8
        for r in reversed(range(8)):
            v = fade * v
            rows[r] = jnp.sum(v, axis=0, keepdims=True)
        y_ref[pl.ds(base, 8), :] = jnp.concatenate(rows, 0)
        return v

    lax.fori_loop(0, octets, octet, first_ref[...])


def by_channels(kernel, ins, outs, flops):
    width = ins[0].shape[1]
    cut = 512 if width % 512 == 0 else width

    def spec(rows):
        return pl.BlockSpec((rows, cut), lambda i: (0, i))

    moved = sum(a.size for a in ins) + sum(r * width for r in outs)
    return pl.pallas_call(
        kernel,
        grid=(width // cut,),
        in_specs=[spec(a.shape[0]) for a in ins],
        out_specs=[spec(r) for r in outs],
        out_shape=[jax.ShapeDtypeStruct((r, width), jnp.float32) for r in outs],
        cost_estimate=pl.CostEstimate(flops=flops, bytes_accessed=4 * moved, transcendentals=0),
    )(*ins)


def attend(query, keys, values, allowed):
    rows, inner = query.shape
    heads = inner // HDIM
    outs, kept = [], []
    for head in range(heads):
        cols = slice(head * HDIM, (head + 1) * HDIM)
        scores = mm(query[:, cols], keys[:, cols], ((1,), (1,))) * HDIM ** (-0.5)
        scores = jnp.where(allowed, scores, -1e30)
        top = jnp.max(scores, axis=-1, keepdims=True)
        weight = jnp.exp(scores - top)
        probs = weight / jnp.sum(weight, axis=-1, keepdims=True)
        outs.append(mm(probs, values[:, cols]))
        kept.append(probs)
    return jnp.concatenate(outs, 1), kept


def attend_back(grad, query, keys, values, outs, kept):
    heads = len(kept)
    dq, dk, dv = [], [], []
    for head in range(heads):
        cols = slice(head * HDIM, (head + 1) * HDIM)
        probs, g = kept[head], grad[:, cols]
        dprobs = mm(g, values[:, cols], ((1,), (1,)))
        inner = jnp.sum(g * outs[:, cols], axis=-1, keepdims=True)
        dscores = probs * (dprobs - inner) * HDIM ** (-0.5)
        dq.append(mm(dscores, keys[:, cols]))
        dk.append(mm(dscores, query[:, cols], ((0,), (0,))))
        dv.append(mm(probs, g, ((0,), (0,))))
    return jnp.concatenate(dq, 1), jnp.concatenate(dk, 1), jnp.concatenate(dv, 1)


def per_device(
    tokens,
    window_state,
    norm1_gain,
    norm1_bias,
    in_coef,
    out_coef,
    decay_rate,
    skip_gain,
    qkv_weight,
    out_weight,
    norm2_gain,
    norm2_bias,
    up_weight,
    up_bias,
    down_weight,
    down_bias,
    cotangent,
):
    place_seq = lax.axis_index("seq")
    rows, width = tokens.shape
    channels, states = in_coef.shape
    windows = window_state.shape[0]
    per_window = LEN // rows
    block = place_seq % per_window
    window = place_seq // per_window
    has_ctx = block > 0

    qkv = qkv_weight.astype(jnp.float32)
    out_own = out_weight.astype(jnp.float32)
    up = up_weight.astype(jnp.float32)
    down = down_weight.astype(jnp.float32)

    packed = jnp.concatenate(
        [decay_rate, in_coef, out_coef, skip_gain[:, None]] + [window_state[w] for w in range(windows)],
        1,
    )
    used = packed.shape[1]
    packed = jnp.pad(packed, ((0, 0), (0, -used % 128)))
    coefs = jnp.transpose(gather_all(packed))
    decay = coefs[:states]
    c_in = coefs[states : 2 * states]
    c_out = coefs[2 * states : 3 * states]
    skip = coefs[3 * states : 3 * states + 1]
    carried = lax.dynamic_slice_in_dim(coefs, 3 * states + 1 + window * states, states, 0)
    fade = jnp.exp(-decay)

    tail_tokens = shift_to(tokens[rows - CTX :], "seq", 1)

    unit1, rate1 = norm_parts(tokens)
    normed = unit1 * norm1_gain + norm1_bias
    tail_unit, _ = norm_parts(tail_tokens)
    tail = jnp.where(has_ctx, tail_unit * norm1_gain + norm1_bias, 0.0)
    segment = jnp.concatenate([tail, normed[: rows - CTX]], 0)

    sum_h, sum_p = by_channels(summary_kernel, [segment, fade], [states, states], 5 * segment.size * states)
    length = float(rows)
    before = jnp.zeros((2, states, width), jnp.float32)
    total = jnp.stack([sum_h, sum_p])

    def shifted(pair, steps):
        gone = jnp.exp(-decay * steps)
        return jnp.stack([gone * pair[0], gone * (pair[1] + steps * pair[0])])

    for bit in range(bits_of(per_window)):
        other = swap_bit(total, "seq", bit)
        upper = ((block >> bit) & 1) == 1
        behind = (block & ((1 << bit) - 1)).astype(jnp.float32) * length
        before = jnp.where(upper, shifted(other, behind) + before, before)
        left = jnp.where(upper, other, total)
        right = jnp.where(upper, total, other)
        total = shifted(left, length * (1 << bit)) + right
    past_h, past_p = before[0], before[1]
    start_t = jnp.maximum(block * rows - CTX, 0).astype(jnp.float32)
    gate = c_in * c_out
    first = c_out * (c_in * past_h + carried * jnp.exp(-decay * start_t))
    (context,) = by_channels(
        tail_kernel, [tail, fade, gate, skip, first], [CTX], 5 * CTX * width * states
    )

    query = mm(normed, qkv[0])
    key_self = mm(normed, qkv[1])
    value_self = mm(normed, qkv[2])
    key_ctx = mm(context, qkv[1])
    value_ctx = mm(context, qkv[2])
    keys = jnp.concatenate([key_ctx, key_self], 0)
    values = jnp.concatenate([value_ctx, value_self], 0)
    rows_q = jnp.arange(rows)[:, None]
    cols_k = jnp.arange(CTX + rows)[None, :]
    allowed = jnp.where(cols_k < CTX, has_ctx, cols_k - CTX <= rows_q)
    heads, kept = attend(query, keys, values, allowed)
    attn_part = mm(heads, out_own)
    mixed = tokens + (attn_part + swap_bit(attn_part, "mp", 0))

    unit2, rate2 = norm_parts(mixed)
    normed2 = unit2 * norm2_gain + norm2_bias
    pre = mm(normed2, up) + up_bias
    cdf = 0.5 * lax.erfc(pre * (-(0.5**0.5)))
    hidden = pre * cdf
    slope = cdf + pre * (jnp.exp(-0.5 * pre * pre) * (1.0 / math.sqrt(2.0 * math.pi)))
    grad_pre = mm(cotangent, down, ((1,), (1,))) * slope
    grad_down = mm(hidden, cotangent, ((0,), (0,)))
    grad_normed2_part = mm(grad_pre, up, ((1,), (1,)))
    grad_up = mm(normed2, grad_pre, ((0,), (0,)))
    grad_up_bias = jnp.sum(grad_pre, axis=0)
    grad_down_bias = jnp.sum(cotangent, axis=0)
    feed_part = mm(hidden, down)
    result = mixed + (feed_part + swap_bit(feed_part, "mp", 0)) + down_bias
    grad_up_sum, grad_down_sum = ring_sum([grad_up, grad_down])

    grad_normed2 = grad_normed2_part + swap_bit(grad_normed2_part, "mp", 0)
    grad_gain2 = jnp.sum(grad_normed2 * unit2, axis=0)
    grad_bias2 = jnp.sum(grad_normed2, axis=0)
    grad_mixed = cotangent + norm_back(grad_normed2, unit2, rate2, norm2_gain)

    grad_heads = mm(grad_mixed, out_own, ((1,), (1,)))
    grad_out_t = mm(grad_mixed, heads, ((0,), (0,)))
    dq, dk, dv = attend_back(grad_heads, query, keys, values, heads, kept)
    grad_context = mm(dk[:CTX], qkv[1], ((1,), (1,))) + mm(dv[:CTX], qkv[2], ((1,), (1,)))
    grad_context = jnp.where(has_ctx, grad_context, 0.0)
    grad_normed_part = (
        mm(dq, qkv[0], ((1,), (1,)))
        + mm(dk[CTX:], qkv[1], ((1,), (1,)))
        + mm(dv[CTX:], qkv[2], ((1,), (1,)))
    )
    grad_q = mm(normed, dq, ((0,), (0,)))
    seen = jnp.concatenate([context, normed], 0)
    grad_k = mm(seen, dk, ((0,), (0,)))
    grad_v = mm(seen, dv, ((0,), (0,)))
    (attn_sum,) = ring_sum([jnp.concatenate([grad_q, grad_k, grad_v, grad_out_t], 1)])
    inner = grad_q.shape[1]
    grad_qkv_sum = jnp.stack([attn_sum[:, i * inner : (i + 1) * inner] for i in range(3)])
    grad_out_sum = jnp.transpose(attn_sum[:, 3 * inner :])

    sum_q, sum_r, part_h, part_p, part_skip, grad_tail = by_channels(
        tail_back_kernel,
        [tail, grad_context, fade, gate, skip],
        [states, states, states, states, 1, CTX],
        20 * CTX * width * states,
    )
    along_h = fade * past_h * sum_q + part_h
    along_p = fade * (past_h * (sum_r + sum_q) + past_p * sum_q) + part_p
    faded = jnp.exp(-decay * (start_t + 1.0))
    part_in = c_out * along_h
    part_out = c_in * along_h + carried * faded * sum_q
    part_decay = -gate * along_p - c_out * carried * faded * ((start_t + 1.0) * sum_q + sum_r)
    stacked = jnp.concatenate([part_in, part_out, part_decay, part_skip], 0)
    stacked = jnp.pad(stacked, ((0, -stacked.shape[0] % 128), (0, 0)))
    own = scatter_sum(jnp.transpose(stacked))
    grad_in = own[:, :states]
    grad_out_coef = own[:, states : 2 * states]
    grad_decay = own[:, 2 * states : 3 * states]
    grad_skip = own[:, 3 * states]

    after = jnp.zeros((states, width), jnp.float32)
    total_q = sum_q
    for bit in range(bits_of(per_window)):
        other = swap_bit(total_q, "seq", bit)
        upper = ((block >> bit) & 1) == 1
        ahead = ((1 << bit) - 1 - (block & ((1 << bit) - 1))).astype(jnp.float32) * length
        after = jnp.where(upper, after, after + jnp.exp(-decay * ahead) * other)
        left = jnp.where(upper, other, total_q)
        right = jnp.where(upper, total_q, other)
        total_q = left + jnp.exp(-decay * (length * (1 << bit))) * right
    (grad_segment,) = by_channels(
        spread_kernel, [gate * after, fade], [rows], 4 * rows * width * states
    )
    to_last = jnp.where(has_ctx, grad_segment[:CTX] + grad_tail, 0.0)
    from_next = shift_to(to_last, "seq", -1)
    grad_states = jnp.concatenate([grad_segment[CTX:], from_next], 0)

    grad_normed_half = grad_normed_part + grad_states
    grad_normed = grad_normed_half + swap_bit(grad_normed_half, "mp", 0)
    grad_gain1 = jnp.sum(grad_normed * unit1, axis=0)
    grad_bias1 = jnp.sum(grad_normed, axis=0)
    grad_tokens = grad_mixed + norm_back(grad_normed, unit1, rate1, norm1_gain)

    early = sum_seq_small(
        jnp.concatenate([grad_gain2, grad_bias2, grad_down_bias, grad_up_bias]).reshape(-1, width)
    )
    late = sum_seq_small(jnp.stack([grad_gain1, grad_bias1]))
    return (
        result,
        grad_tokens,
        late[0],
        late[1],
        grad_in,
        grad_out_coef,
        grad_decay,
        grad_skip,
        grad_qkv_sum,
        grad_out_sum,
        early[0],
        early[1],
        grad_up_sum,
        early[3:].reshape(-1),
        grad_down_sum,
        early[2],
    )


def solution(mesh):
    owner = P(("seq", "mp"), None)
    return jax.shard_map(
        per_device,
        mesh=mesh,
        in_specs=(
            P("seq", None),
            P(None, ("seq", "mp"), None),
            P(),
            P(),
            owner,
            owner,
            owner,
            P(("seq", "mp")),
            P(None, None, "mp"),
            P("mp", None),
            P(),
            P(),
            P(None, "mp"),
            P("mp"),
            P("mp", None),
            P(),
            P("seq", None),
        ),
        out_specs=(
            P("seq", None),
            P("seq", None),
            P(),
            P(),
            owner,
            owner,
            owner,
            P(("seq", "mp")),
            P(None, None, "mp"),
            P("mp", None),
            P(),
            P(),
            P(None, "mp"),
            P("mp"),
            P("mp", None),
            P(),
        ),
        check_vma=False,
    )
```

```python
import functools
import math

import jax
import jax.numpy as jnp
from jax import lax
from jax.experimental import pallas as pl
from jax.experimental.pallas import tpu as pltpu
from jax.sharding import PartitionSpec as P

HDIM = 128
BLOCK = 512
CTX = 128
LEN = 4096
EPS = 1e-05
HIGH = lax.Precision.HIGH


def mm(left, right, dims=((1,), (0,))):
    return lax.dot_general(
        left, right, (dims, ((), ())), precision=HIGH, preferred_element_type=jnp.float32
    )


def norm_parts(value):
    center = value - jnp.mean(value, axis=-1, keepdims=True)
    spread = jnp.mean(center * center, axis=-1, keepdims=True)
    rate = lax.rsqrt(spread + EPS)
    return center * rate, rate


def norm_back(grad, unit, rate, gain):
    scaled = grad * gain
    inner = jnp.mean(scaled * unit, axis=-1, keepdims=True)
    return rate * (scaled - jnp.mean(scaled, axis=-1, keepdims=True) - unit * inner)


def swap_bit(value, axis, bit):
    size = lax.axis_size(axis)
    return lax.ppermute(value, axis, [(i, i ^ (1 << bit)) for i in range(size)])


def bits_of(count):
    return count.bit_length() - 1


def shift_to(value, axis, distance):
    size = lax.axis_size(axis)
    route = [(i, i + distance) for i in range(size) if 0 <= i + distance < size]
    return lax.ppermute(value, axis, route)


def after(value, *others):
    return lax.optimization_barrier((value,) + others)[0]


def gather_all(piece):
    rows = piece.shape[0]
    mp_size, seq_size = lax.axis_size("mp"), lax.axis_size("seq")
    me = lax.axis_index("seq") * mp_size + lax.axis_index("mp")
    block, low = piece, 0
    for bit in range(bits_of(mp_size * seq_size)):
        axis, own = ("mp", bit) if bit < bits_of(mp_size) else ("seq", bit - bits_of(mp_size))
        other = swap_bit(block, axis, own)
        upper = (me >> bit) & 1
        block = jnp.where(
            upper == 1, jnp.concatenate([other, block], 0), jnp.concatenate([block, other], 0)
        )
    return block


def scatter_sum(whole):
    mp_size, seq_size = lax.axis_size("mp"), lax.axis_size("seq")
    me = lax.axis_index("seq") * mp_size + lax.axis_index("mp")
    block = whole
    for bit in reversed(range(bits_of(mp_size * seq_size))):
        axis, own = ("mp", bit) if bit < bits_of(mp_size) else ("seq", bit - bits_of(mp_size))
        half = block.reshape(2, block.shape[0] // 2, block.shape[1])
        upper = (me >> bit) & 1
        keep = lax.dynamic_index_in_dim(half, upper, 0, keepdims=False)
        give = lax.dynamic_index_in_dim(half, 1 - upper, 0, keepdims=False)
        block = keep + swap_bit(give, axis, own)
    return block


def sum_seq_small(value):
    for bit in range(bits_of(lax.axis_size("seq"))):
        value = value + swap_bit(value, "seq", bit)
    return value


def trade_chips(value, distance):
    size = lax.axis_size("seq")
    return lax.ppermute(value, "seq", [(i, i ^ (2 * distance)) for i in range(size)])


def chip_order(count):
    if count <= 2:
        return list(range(count))
    return list(range(0, count, 2)) + list(range(count - 1 - count % 2, 0, -2))


def ring_route(count):
    order = chip_order(count)
    route = []
    for i in range(count):
        here, there = order[i], order[(i + 1) % count]
        route.append((2 * here, 2 * there))
        route.append((2 * there + 1, 2 * here + 1))
    return route


def ring_spot():
    count = lax.axis_size("seq") // 2
    places = [0] * count
    for i, chip in enumerate(chip_order(count)):
        places[chip] = i
    me = lax.axis_index("seq")
    here = jnp.array(places, jnp.int32)[me // 2]
    return jnp.where(me % 2 == 0, here, (count - here) % count)


def unset(shape):
    return pl.pallas_call(
        lambda out: None,
        out_shape=jax.ShapeDtypeStruct(shape, jnp.float32),
        out_specs=pl.BlockSpec(memory_space=pl.ANY),
    )()


def ring_reduce(parts, gate=()):
    count = lax.axis_size("seq") // 2
    place, route = ring_spot(), ring_route(count)
    rows = parts[0].shape[0] // count

    def chunk(spot):
        cut = [lax.dynamic_slice_in_dim(p, spot * rows, rows, 0) for p in parts]
        return cut[0] if len(cut) == 1 else jnp.concatenate(cut, 1)

    held = chunk(place)
    if gate:
        held = after(held, *gate)
    for step in range(count - 1):
        got = lax.ppermute(held, "seq", route)
        held = got + chunk((place + 2 * count - 1 - step) % count)
    return held


def ring_spread(held, outs, split):
    count = lax.axis_size("seq") // 2
    place, route = ring_spot(), ring_route(count)
    core = lax.axis_index("seq") % 2
    mirror = (count - place) % count
    rows = held.shape[0]

    def put(outs, part, which, spot):
        row = which * (count * rows) + spot % count * rows
        new = []
        for out, (low, high, lead) in zip(outs, split):
            cut = part[:, low:high]
            if lead is None:
                new.append(lax.dynamic_update_slice(out, cut, (row, 0)))
            else:
                new.append(lax.dynamic_update_slice(out, cut[None], (lead, row, 0)))
        return new

    for step in range(count):
        spot, far = place + 1 - step + count, mirror + 1 - step + count
        other = swap_bit(held, "seq", 0)
        outs = put(outs, held, core, spot)
        outs = put(outs, other, 1 - core, far)
        if step < count - 1:
            held = lax.ppermute(held, "seq", route)
    return outs, held


def chip_sum(left, right, first=None):
    core = lax.axis_index("seq") % 2

    def half(which):
        total = None
        for l, r in zip(left, right):
            cut = lax.dynamic_slice_in_dim(l, which * (l.shape[1] // 2), l.shape[1] // 2, 1)
            part = mm(cut, r, ((0,), (0,)))
            total = part if total is None else total + part
        return total

    give = half(1 - core)
    got = swap_bit(give, "seq", 0)
    return half(core) + got


def rows8(shape):
    return lax.broadcasted_iota(jnp.int32, shape, 0).astype(jnp.float32)


def octets_of(decay_ref):
    states, lanes = decay_ref.shape
    rates = [jnp.broadcast_to(decay_ref[n : n + 1, :], (8, lanes)) for n in range(states)]
    return rates, [jnp.exp(-8.0 * rate) for rate in rates]


def summary_kernel(tail_ref, x_ref, decay_ref, h_ref):
    states, lanes = decay_ref.shape
    rates, jump = octets_of(decay_ref)

    def run(ref):
        def step(i, acc):
            tile = ref[pl.ds(pl.multiple_of(i * 8, 8), 8), :]
            return tuple(j * a + tile for j, a in zip(jump, acc))

        return step

    acc = (tail_ref[:8, :] * 0.0,) * states
    acc = lax.fori_loop(0, tail_ref.shape[0] // 8, run(tail_ref), acc)
    acc = lax.fori_loop(0, (x_ref.shape[0] - tail_ref.shape[0]) // 8, run(x_ref), acc)
    left = 7.0 - rows8((8, lanes))
    for n in range(states):
        h_ref[n : n + 1, :] = jnp.sum(acc[n] * jnp.exp(-rates[n] * left), axis=0, keepdims=True)


def moment_kernel(tail_ref, x_ref, decay_ref, p_ref):
    states, lanes = decay_ref.shape
    rates, jump = octets_of(decay_ref)

    def run(ref):
        def step(i, carry):
            acc, lag = carry
            tile = ref[pl.ds(pl.multiple_of(i * 8, 8), 8), :]
            lag = tuple(j * (b + a) for j, a, b in zip(jump, acc, lag))
            acc = tuple(j * a + tile for j, a in zip(jump, acc))
            return acc, lag

        return step

    zeros = (tail_ref[:8, :] * 0.0,) * states
    carry = lax.fori_loop(0, tail_ref.shape[0] // 8, run(tail_ref), (zeros, zeros))
    acc, lag = lax.fori_loop(0, (x_ref.shape[0] - tail_ref.shape[0]) // 8, run(x_ref), carry)
    left = 7.0 - rows8((8, lanes))
    for n in range(states):
        total = (8.0 * lag[n] + left * acc[n]) * jnp.exp(-rates[n] * left)
        p_ref[n : n + 1, :] = jnp.sum(total, axis=0, keepdims=True)


def carry_kernel(near_ref, first_ref, decay_ref, y_ref):
    states, lanes = decay_ref.shape
    rates, jump = octets_of(decay_ref)
    ahead = rows8((8, lanes)) + 1.0
    start = tuple(
        jnp.broadcast_to(first_ref[n : n + 1, :], (8, lanes)) * jnp.exp(-rates[n] * ahead)
        for n in range(states)
    )

    def step(i, modes):
        base = pl.multiple_of(i * 8, 8)
        y_ref[pl.ds(base, 8), :] = near_ref[pl.ds(base, 8), :] + sum(modes)
        return tuple(j * m for j, m in zip(jump, modes))

    lax.fori_loop(0, y_ref.shape[0] // 8, step, start)


def spread_kernel(first_ref, decay_ref, y_ref):
    states, lanes = decay_ref.shape
    rates, jump = octets_of(decay_ref)
    ahead = 8.0 - rows8((8, lanes))
    count = y_ref.shape[0] // 8
    start = tuple(
        jnp.broadcast_to(first_ref[n : n + 1, :], (8, lanes)) * jnp.exp(-rates[n] * ahead)
        for n in range(states)
    )

    def step(i, modes):
        y_ref[pl.ds(pl.multiple_of((count - 1 - i) * 8, 8), 8), :] = sum(modes)
        return tuple(j * m for j, m in zip(jump, modes))

    lax.fori_loop(0, count, step, start)


def near_kernel(x_ref, fade_ref, gate_ref, skip_ref, y_ref):
    fade, gate, skip = fade_ref[...], gate_ref[...], skip_ref[...]

    def octet(i, u):
        base = pl.multiple_of(i * 8, 8)
        tile = x_ref[pl.ds(base, 8), :]
        rows = []
        for r in range(8):
            row = tile[r : r + 1, :]
            u = fade * u + gate * jnp.broadcast_to(row, fade.shape)
            rows.append(jnp.sum(u, axis=0, keepdims=True) + skip * row)
        y_ref[pl.ds(base, 8), :] = jnp.concatenate(rows, 0)
        return u

    lax.fori_loop(0, x_ref.shape[0] // 8, octet, jnp.zeros(fade.shape, jnp.float32))


def tail_back_kernel(
    x_ref, d_ref, fade_ref, gate_ref, skip_ref, q_ref, r_ref, dh_ref, dp_ref, dskip_ref, dx_ref
):
    fade, gate, skip = fade_ref[...], gate_ref[...], skip_ref[...]
    octets = x_ref.shape[0] // 8
    zero = jnp.zeros(fade.shape, jnp.float32)

    def forward(i, carry):
        h, p, dh, dp = carry
        base = pl.multiple_of(i * 8, 8)
        tile, grads = x_ref[pl.ds(base, 8), :], d_ref[pl.ds(base, 8), :]
        for r in range(8):
            p = fade * (p + h)
            h = fade * h + jnp.broadcast_to(tile[r : r + 1, :], fade.shape)
            grad = jnp.broadcast_to(grads[r : r + 1, :], fade.shape)
            dh = dh + grad * h
            dp = dp + grad * p
        return h, p, dh, dp

    _, _, dh, dp = lax.fori_loop(0, octets, forward, (zero, zero, zero, zero))
    dh_ref[...] = dh
    dp_ref[...] = dp
    dskip_ref[...] = jnp.sum(x_ref[...] * d_ref[...], axis=0, keepdims=True)

    def backward(k, carry):
        q, r_sum = carry
        base = pl.multiple_of((octets - 1 - k) * 8, 8)
        grads = d_ref[pl.ds(base, 8), :]
        rows = [None] * 8
        for r in reversed(range(8)):
            r_sum = fade * (r_sum + q)
            grad = grads[r : r + 1, :]
            q = fade * q + jnp.broadcast_to(grad, fade.shape)
            rows[r] = jnp.sum(gate * q, axis=0, keepdims=True) + skip * grad
        dx_ref[pl.ds(base, 8), :] = jnp.concatenate(rows, 0)
        return q, r_sum

    q, r_sum = lax.fori_loop(0, octets, backward, (zero, zero))
    q_ref[...] = q
    r_ref[...] = r_sum


def by_channels(kernel, ins, outs, flops, cut=512):
    width = ins[0].shape[1]
    cut = cut if width % cut == 0 else width

    def spec(rows):
        return pl.BlockSpec((rows, cut), lambda i: (0, i))

    moved = sum(a.size for a in ins) + sum(r * width for r in outs)
    return pl.pallas_call(
        kernel,
        grid=(width // cut,),
        in_specs=[spec(a.shape[0]) for a in ins],
        out_specs=[spec(r) for r in outs],
        out_shape=[jax.ShapeDtypeStruct((r, width), jnp.float32) for r in outs],
        cost_estimate=pl.CostEstimate(flops=flops, bytes_accessed=4 * moved, transcendentals=0),
    )(*ins)


def cut(value):
    top = value.astype(jnp.bfloat16)
    return top, (value - top.astype(jnp.float32)).astype(jnp.bfloat16)


def dot3(left, right, dims):
    def one(a, b):
        return lax.dot_general(a, b, (dims, ((), ())), preferred_element_type=jnp.float32)

    return one(left[0], right[1]) + one(left[1], right[0]) + one(left[0], right[0])


NT = ((1,), (1,))
NN = ((1,), (0,))
TN = ((0,), (0,))
TILE = 256
SCALE = HDIM ** (-0.5)


def causal(shape, first_row):
    row = lax.broadcasted_iota(jnp.int32, shape, 0) + first_row
    return lax.broadcasted_iota(jnp.int32, shape, 1) <= row


def self_kernel(q_ref, k_ref, v_ref, acc_ref, top_ref, sum_ref):
    rows = q_ref.shape[0]
    k, v = cut(k_ref[...]), cut(v_ref[...])
    for first in range(0, rows, TILE):
        span = slice(first, first + TILE)
        seen = first + TILE
        q = cut(q_ref[span, :] * SCALE)
        scores = dot3(q, (k[0][:seen], k[1][:seen]), NT)
        scores = jnp.where(causal(scores.shape, first), scores, -1e30)
        top = jnp.max(scores, axis=1, keepdims=True)
        weight = jnp.exp(scores - top)
        acc_ref[span, :] = dot3(cut(weight), (v[0][:seen], v[1][:seen]), NN)
        top_ref[span, :] = jnp.broadcast_to(top, (TILE, HDIM))
        sum_ref[span, :] = jnp.broadcast_to(jnp.sum(weight, axis=1, keepdims=True), (TILE, HDIM))


def ctx_kernel(ok_ref, q_ref, k_ref, v_ref, acc_ref, top_ref, sum_ref, out_ref, log_ref):
    ok = ok_ref[0] > 0
    q = cut(q_ref[...] * SCALE)
    scores = dot3(q, cut(k_ref[...]), NT)
    scores = jnp.where(ok, scores, -1e30)
    top = jnp.maximum(top_ref[...], jnp.max(scores, axis=1, keepdims=True))
    weight = jnp.where(ok, jnp.exp(scores - top[:, :1]), 0.0)
    ease = jnp.exp(top_ref[...] - top)
    total = sum_ref[...] * ease + jnp.sum(weight, axis=1, keepdims=True)
    out_ref[...] = (acc_ref[...] * ease + dot3(cut(weight), cut(v_ref[...]), NN)) / total
    log_ref[...] = top + jnp.log(total)


def back_kernel(
    ok_ref, q_ref, k_ref, v_ref, kc_ref, vc_ref, o0_ref, o1_ref, l0_ref, l1_ref, g0_ref, g1_ref,
    dq_ref, dk_ref, dv_ref, dkc_ref, dvc_ref,
):
    ok = ok_ref[0] > 0
    rows = q_ref.shape[0]
    tiles = (rows + TILE - 1) // TILE
    k, v, kc, vc = cut(k_ref[...]), cut(v_ref[...]), cut(kc_ref[...]), cut(vc_ref[...])
    for tile in reversed(range(tiles)):
        first = tile * TILE
        seen = first + TILE
        o, log, g = (
            (o0_ref, l0_ref, g0_ref) if first < rows // 2 else (o1_ref, l1_ref, g1_ref)
        )
        local = slice(first % (rows // 2), first % (rows // 2) + TILE)
        grad = g[local, :]
        q = cut(q_ref[first:seen, :] * SCALE)
        grad2 = cut(grad)
        inner = jnp.sum(grad * o[local, :], axis=1, keepdims=True)
        mark = log[local, :][:, :1]
        ks, vs = (k[0][:seen], k[1][:seen]), (v[0][:seen], v[1][:seen])
        probs = dot3(q, ks, NT)
        probs = jnp.where(causal(probs.shape, first), jnp.exp(probs - mark), 0.0)
        probs_c = jnp.where(ok, jnp.exp(dot3(q, kc, NT) - mark), 0.0)
        ds = cut(probs * (dot3(grad2, vs, NT) - inner))
        ds_c = cut(probs_c * (dot3(grad2, vc, NT) - inner))
        probs, probs_c = cut(probs), cut(probs_c)
        dq_ref[first:seen, :] = (dot3(ds, ks, NN) + dot3(ds_c, kc, NN)) * SCALE
        dk, dv = dot3(ds, q, TN), dot3(probs, grad2, TN)
        dkc, dvc = dot3(ds_c, q, TN), dot3(probs_c, grad2, TN)
        if tile == tiles - 1:
            dk_ref[...], dv_ref[...], dkc_ref[...], dvc_ref[...] = dk, dv, dkc, dvc
        else:
            dk_ref[:seen, :] += dk
            dv_ref[:seen, :] += dv
            dkc_ref[...] += dkc
            dvc_ref[...] += dvc


def by_heads(kernel, ins, outs, scalars=(), firsts=None, flops=0):
    heads = ins[0][0].shape[1] // HDIM
    specs = [pl.BlockSpec(memory_space=pltpu.SMEM) for _ in scalars]
    for _, rows, at in ins:
        specs.append(pl.BlockSpec((rows, HDIM), lambda h, at=at: (at, h)))
    moved = sum(r * HDIM * heads for _, r, _ in ins) + sum(outs) * HDIM * heads
    return pl.pallas_call(
        kernel,
        grid=(heads,),
        in_specs=specs,
        out_specs=[pl.BlockSpec((r, HDIM), lambda h: (0, h)) for r in outs],
        out_shape=[jax.ShapeDtypeStruct((r, heads * HDIM), jnp.float32) for r in outs],
        cost_estimate=pl.CostEstimate(flops=flops, bytes_accessed=4 * moved, transcendentals=0),
        compiler_params=pltpu.CompilerParams(vmem_limit_bytes=40 << 20),
    )(*scalars, *[a for a, _, _ in ins])


def per_device(
    tokens,
    window_state,
    norm1_gain,
    norm1_bias,
    in_coef,
    out_coef,
    decay_rate,
    skip_gain,
    qkv_weight,
    out_weight,
    norm2_gain,
    norm2_bias,
    up_weight,
    up_bias,
    down_weight,
    down_bias,
    cotangent,
):
    place_seq = lax.axis_index("seq")
    core = place_seq % 2
    rows, width = tokens.shape
    states = in_coef.shape[1]
    windows = window_state.shape[0]
    per_window = LEN // rows
    block = place_seq % per_window
    window = place_seq // per_window
    has_ctx = block > 0
    ok = has_ctx.astype(jnp.int32).reshape(1)
    half = rows // 2

    qkv = qkv_weight.astype(jnp.float32)
    out_own = out_weight.astype(jnp.float32)
    up = up_weight.astype(jnp.float32)
    down = down_weight.astype(jnp.float32)

    decay = jnp.transpose(gather_all(decay_rate))
    packed = jnp.concatenate(
        [in_coef, out_coef, skip_gain[:, None]] + [window_state[w] for w in range(windows)], 1
    )
    coefs = jnp.transpose(gather_all(packed))
    c_in = coefs[:states]
    c_out = coefs[states : 2 * states]
    skip = coefs[2 * states : 2 * states + 1]
    carried = lax.dynamic_slice_in_dim(coefs, 2 * states + 1 + window * states, states, 0)
    gate = c_in * c_out
    fade = jnp.exp(-decay)

    tail_tokens = shift_to(tokens[rows - CTX :], "seq", 1)

    inner = out_own.shape[0]
    sent = lax.dynamic_slice_in_dim(out_own, core * (inner // 2), inner // 2, 0)
    across = swap_bit(sent, "mp", 0)
    beside = swap_bit(across, "seq", 0)
    out_far = jnp.where(
        core == 0, jnp.concatenate([across, beside], 0), jnp.concatenate([beside, across], 0)
    )

    unit1, rate1 = norm_parts(tokens)
    normed = unit1 * norm1_gain + norm1_bias
    tail_unit, _ = norm_parts(tail_tokens)
    tail = jnp.where(has_ctx, tail_unit * norm1_gain + norm1_bias, 0.0)

    length = float(rows)
    chips = per_window // 2
    chip = block // 2
    (sum_h,) = by_channels(summary_kernel, [tail, normed, decay], [states], 2 * rows * width * states, 128)

    def faded(steps):
        return jnp.exp(-decay * steps)

    def pair_order(value):
        other = swap_bit(value, "seq", 0)
        return jnp.where(core == 0, value, other), jnp.where(core == 0, other, value)

    first_h, second_h = pair_order(sum_h)
    both_h = faded(length) * first_h + second_h
    far_h = [trade_chips(both_h, d) for d in range(1, chips)]
    past_h = jnp.zeros_like(sum_h)
    for d in range(1, chips):
        there = chip ^ d
        gap = jnp.maximum(chip - 1 - there, 0).astype(jnp.float32) * (2.0 * length)
        past_h = past_h + jnp.where(there < chip, faded(gap) * far_h[d - 1], 0.0)
    past_h = jnp.where(core == 0, past_h, faded(length) * past_h + first_h)

    start_t = jnp.maximum(block * rows - CTX, 0).astype(jnp.float32)
    first = c_out * (c_in * past_h + carried * faded(start_t))
    (near,) = by_channels(near_kernel, [tail, fade, gate, skip], [CTX], 5 * CTX * width * states)
    (context,) = by_channels(carry_kernel, [near, first, decay], [CTX], 2 * CTX * width * states, 128)

    query = mm(normed, qkv[0])
    key = mm(normed, qkv[1])
    value = mm(normed, qkv[2])
    acc, top, total = by_heads(
        self_kernel, [(a, rows, 0) for a in (query, key, value)], [rows] * 3,
        flops=2 * 6 * rows * rows * inner,
    )
    grad_hidden = mm(cotangent, down, NT)
    context = after(context, acc, grad_hidden)
    key_ctx = mm(context, qkv[1])
    value_ctx = mm(context, qkv[2])
    heads, logs, far = [], [], []
    for part in range(2):
        o, l = by_heads(
            ctx_kernel,
            [(query, half, part), (key_ctx, CTX, 0), (value_ctx, CTX, 0)]
            + [(a, half, part) for a in (acc, top, total)],
            [half, half],
            scalars=(ok,),
            flops=2 * 6 * half * CTX * inner,
        )
        if part:
            o = after(o, heads[0])
        heads.append(o)
        logs.append(l)
        far.append(swap_bit(o, "mp", 0))

    unit2, rate2, mixed, normed2, hidden, slope = [], [], [], [], [], []
    for part in range(2):
        span = slice(part * half, (part + 1) * half)
        m = tokens[span] + (mm(heads[part], out_own) + mm(far[part], out_far))
        u, r = norm_parts(m)
        n = u * norm2_gain + norm2_bias
        pre = mm(n, up) + up_bias
        cdf = 0.5 + 0.5 * lax.erf(pre * (0.5**0.5))
        bell = jnp.exp(-0.5 * pre * pre) * (1.0 / math.sqrt(2.0 * math.pi))
        mixed.append(m)
        unit2.append(u)
        rate2.append(r)
        normed2.append(n)
        hidden.append(pre * cdf)
        slope.append(grad_hidden[span] * (cdf + pre * bell))
    cots = [cotangent[:half], cotangent[half:]]
    down_half = chip_sum(hidden, cots)
    grad_pre = [after(s, down_half) for s in slope]
    part2 = [mm(g, up, NT) for g in grad_pre]
    sums2 = [p + swap_bit(p, "mp", 0) for p in part2]
    up_half = chip_sum(normed2, [after(g, part2[1]) for g in grad_pre])
    feed = jnp.concatenate([mm(after(h, up_half), down) for h in hidden], 0)
    result = jnp.concatenate(mixed, 0) + (feed + swap_bit(after(feed, *sums2), "mp", 0)) + down_bias
    grad_up_bias = jnp.sum(grad_pre[0], axis=0) + jnp.sum(grad_pre[1], axis=0)
    grad_down_bias = jnp.sum(cotangent, axis=0)

    held_down = ring_reduce([down_half])
    held_up = ring_reduce([up_half])
    (grad_down,), last_down = ring_spread(held_down, [unset(down.shape)], [(0, width, None)])
    (grad_up,), last_up = ring_spread(held_up, [unset(up.shape)], [(0, up.shape[1], None)])

    grad_mixed, grad_heads = [], []
    gain2, bias2 = 0.0, 0.0
    for part in range(2):
        g = sums2[part]
        gain2 = gain2 + jnp.sum(g * unit2[part], axis=0)
        bias2 = bias2 + jnp.sum(g, axis=0)
        grad_mixed.append(cots[part] + norm_back(g, unit2[part], rate2[part], norm2_gain))
        grad_heads.append(mm(grad_mixed[part], out_own, NT))

    dq, dk, dv, dk_ctx, dv_ctx = by_heads(
        back_kernel,
        [(query, rows, 0), (key, rows, 0), (value, rows, 0), (key_ctx, CTX, 0), (value_ctx, CTX, 0)]
        + [(a, half, 0) for a in heads + logs + grad_heads],
        [rows, rows, rows, CTX, CTX],
        scalars=(ok,),
        flops=2 * 15 * rows * (rows + CTX) * inner,
    )
    dkv = jnp.concatenate([dk, dv], 1)
    dkv_ctx = jnp.concatenate([dk_ctx, dv_ctx], 1)
    q_half = chip_sum([normed], [dq])
    kv_half = chip_sum([context, normed], [dkv_ctx, dkv])
    out_half = chip_sum(grad_mixed, heads)
    grad_context = mm(dk_ctx, qkv[1], NT) + mm(dv_ctx, qkv[2], NT)
    grad_context = jnp.where(has_ctx, grad_context, 0.0)
    grad_normed_part = mm(dq, qkv[0], NT) + mm(dk, qkv[1], NT) + mm(dv, qkv[2], NT)

    gates = (last_down, last_up)
    held_qo = ring_reduce([q_half, out_half], gates)
    held_kv = ring_reduce([kv_half], gates)
    grad_qkv = unset((3, width, inner))
    (grad_qkv, grad_out_t), _ = ring_spread(
        held_qo, [grad_qkv, unset((width, inner))], [(0, inner, 0), (inner, 2 * inner, None)]
    )
    (key_out, value_out), _ = ring_spread(
        held_kv, [unset((width, inner)), unset((width, inner))], [(0, inner, None), (inner, 2 * inner, None)]
    )
    grad_qkv = lax.dynamic_update_slice(grad_qkv, key_out[None], (1, 0, 0))
    grad_qkv = lax.dynamic_update_slice(grad_qkv, value_out[None], (2, 0, 0))
    grad_out = jnp.transpose(grad_out_t)

    (sum_p,) = by_channels(moment_kernel, [tail, after(normed, dq), decay], [states], 4 * rows * width * states, 128)
    first_p, second_p = pair_order(sum_p)
    both_p = faded(length) * (first_p + length * first_h) + second_p
    past_p = jnp.zeros_like(sum_p)
    for d in range(1, chips):
        there = chip ^ d
        gap = jnp.maximum(chip - 1 - there, 0).astype(jnp.float32) * (2.0 * length)
        moved = faded(gap) * (trade_chips(both_p, d) + gap * far_h[d - 1])
        past_p = past_p + jnp.where(there < chip, moved, 0.0)
    chip_h = jnp.zeros_like(sum_p)
    for d in range(1, chips):
        there = chip ^ d
        gap = jnp.maximum(chip - 1 - there, 0).astype(jnp.float32) * (2.0 * length)
        chip_h = chip_h + jnp.where(there < chip, faded(gap) * far_h[d - 1], 0.0)
    past_p = jnp.where(core == 0, past_p, faded(length) * (past_p + length * chip_h) + first_p)

    sum_q, sum_r, part_h, part_p, part_skip, grad_tail = by_channels(
        tail_back_kernel,
        [tail, grad_context, fade, gate, skip],
        [states, states, states, states, 1, CTX],
        20 * CTX * width * states,
    )
    along_h = fade * past_h * sum_q + part_h
    along_p = fade * (past_h * (sum_r + sum_q) + past_p * sum_q) + part_p
    gone = faded(start_t + 1.0)
    part_in = c_out * along_h
    part_out = c_in * along_h + carried * gone * sum_q
    part_decay = -gate * along_p - c_out * carried * gone * ((start_t + 1.0) * sum_q + sum_r)
    stacked = jnp.concatenate([part_in, part_out, part_decay, part_skip], 0)
    stacked = jnp.pad(stacked, ((0, -stacked.shape[0] % 128), (0, 0)))
    own = scatter_sum(jnp.transpose(stacked))
    grad_in = own[:, :states]
    grad_out_coef = own[:, states : 2 * states]
    grad_decay = own[:, 2 * states : 3 * states]
    grad_skip = own[:, 3 * states]

    first_q, second_q = pair_order(sum_q)
    both_q = first_q + faded(length) * second_q
    later = jnp.zeros_like(sum_q)
    for d in range(1, chips):
        there = chip ^ d
        gap = jnp.maximum(there - 1 - chip, 0).astype(jnp.float32) * (2.0 * length)
        later = later + jnp.where(there > chip, faded(gap) * trade_chips(both_q, d), 0.0)
    later = jnp.where(core == 1, later, second_q + faded(length) * later)
    (grad_segment,) = by_channels(
        spread_kernel, [gate * later, decay], [rows], 2 * rows * width * states, 128
    )
    to_last = jnp.where(has_ctx, grad_segment[:CTX] + grad_tail, 0.0)
    from_next = shift_to(to_last, "seq", -1)
    grad_states = jnp.concatenate([grad_segment[CTX:], from_next], 0)

    grad_normed_half = grad_normed_part + grad_states
    grad_normed = grad_normed_half + swap_bit(grad_normed_half, "mp", 0)
    grad_gain1 = jnp.sum(grad_normed * unit1, axis=0)
    grad_bias1 = jnp.sum(grad_normed, axis=0)
    grad_tokens = jnp.concatenate(grad_mixed, 0) + norm_back(grad_normed, unit1, rate1, norm1_gain)

    small = sum_seq_small(
        jnp.concatenate(
            [gain2, bias2, grad_down_bias, grad_gain1, grad_bias1, grad_up_bias]
        ).reshape(-1, width)
    )
    return (
        result,
        grad_tokens,
        small[3],
        small[4],
        grad_in,
        grad_out_coef,
        grad_decay,
        grad_skip,
        grad_qkv,
        grad_out,
        small[0],
        small[1],
        grad_up,
        small[5:].reshape(-1),
        grad_down,
        small[2],
    )


def solution(mesh):
    owner = P(("seq", "mp"), None)
    return jax.shard_map(
        per_device,
        mesh=mesh,
        in_specs=(
            P("seq", None),
            P(None, ("seq", "mp"), None),
            P(),
            P(),
            owner,
            owner,
            owner,
            P(("seq", "mp")),
            P(None, None, "mp"),
            P("mp", None),
            P(),
            P(),
            P(None, "mp"),
            P("mp"),
            P("mp", None),
            P(),
            P("seq", None),
        ),
        out_specs=(
            P("seq", None),
            P("seq", None),
            P(),
            P(),
            owner,
            owner,
            owner,
            P(("seq", "mp")),
            P(None, None, "mp"),
            P("mp", None),
            P(),
            P(),
            P(None, "mp"),
            P("mp"),
            P("mp", None),
            P(),
        ),
        check_vma=False,
    )
```

```python
import functools
import math

import jax
import jax.numpy as jnp
from jax import lax
from jax.experimental import pallas as pl
from jax.experimental.pallas import tpu as pltpu
from jax.sharding import PartitionSpec as P

HDIM = 128
BLOCK = 512
CTX = 128
LEN = 4096
EPS = 1e-05
HIGH = lax.Precision.HIGH


def mm(left, right, dims=((1,), (0,))):
    return lax.dot_general(
        left, right, (dims, ((), ())), precision=HIGH, preferred_element_type=jnp.float32
    )


def norm_parts(value):
    center = value - jnp.mean(value, axis=-1, keepdims=True)
    spread = jnp.mean(center * center, axis=-1, keepdims=True)
    rate = lax.rsqrt(spread + EPS)
    return center * rate, rate


def norm_back(grad, unit, rate, gain):
    scaled = grad * gain
    inner = jnp.mean(scaled * unit, axis=-1, keepdims=True)
    return rate * (scaled - jnp.mean(scaled, axis=-1, keepdims=True) - unit * inner)


def swap_bit(value, axis, bit):
    size = lax.axis_size(axis)
    return lax.ppermute(value, axis, [(i, i ^ (1 << bit)) for i in range(size)])


def bits_of(count):
    return count.bit_length() - 1


def shift_in_window(value, distance, per_window):
    size = lax.axis_size("seq")
    route = [(i, i + distance) for i in range(size)]
    inside = [(a, b) for a, b in route if 0 <= b < size and a // per_window == b // per_window]
    return lax.ppermute(value, "seq", inside)


def after(value, *others):
    return lax.optimization_barrier((value,) + others)[0]


def gather_all(piece, gates=()):
    mp_size, seq_size = lax.axis_size("mp"), lax.axis_size("seq")
    me = lax.axis_index("seq") * mp_size + lax.axis_index("mp")
    block, seen = piece, []
    for bit in range(bits_of(mp_size * seq_size)):
        axis, own = ("mp", bit) if bit < bits_of(mp_size) else ("seq", bit - bits_of(mp_size))
        if gates:
            block = after(block, gates[bit])
        other = swap_bit(block, axis, own)
        upper = (me >> bit) & 1
        block = jnp.where(
            upper == 1, jnp.concatenate([other, block], 1), jnp.concatenate([block, other], 1)
        )
        seen.append(block)
    return block, seen


def trade_chips(value, distance):
    size = lax.axis_size("seq")
    return lax.ppermute(value, "seq", [(i, i ^ (2 * distance)) for i in range(size)])


def chip_order(count):
    if count <= 2:
        return list(range(count))
    return list(range(0, count, 2)) + list(range(count - 1 - count % 2, 0, -2))


def ring_route(count):
    order = chip_order(count)
    route = []
    for i in range(count):
        here, there = order[i], order[(i + 1) % count]
        route.append((2 * here, 2 * there))
        route.append((2 * there + 1, 2 * here + 1))
    return route


def ring_spot():
    count = lax.axis_size("seq") // 2
    places = [0] * count
    for i, chip in enumerate(chip_order(count)):
        places[chip] = i
    me = lax.axis_index("seq")
    here = jnp.array(places, jnp.int32)[me // 2]
    return jnp.where(me % 2 == 0, here, (count - here) % count)


def unset(shape):
    return pl.pallas_call(
        lambda out: None,
        out_shape=jax.ShapeDtypeStruct(shape, jnp.float32),
        out_specs=pl.BlockSpec(memory_space=pl.ANY),
    )()


def pick(value, index):
    return lax.dynamic_index_in_dim(value, index, 0, keepdims=False)


class Clock:
    def __init__(self):
        self.last = ()

    def hold(self, value):
        return after(value, *self.last) if self.last else value

    def set(self, *values):
        self.last = values


def assemble_kernel(count, cuts, where_ref, *refs):
    parts, outs, sems = refs[: 2 * count], refs[2 * count : -1], refs[-1]
    copies = []
    for n in range(2 * count):
        which, spot = where_ref[0, n], where_ref[1, n]
        for out, (low, high) in zip(outs, cuts):
            copies.append(
                pltpu.make_async_copy(
                    parts[n].at[low:high], out.at[:, which, spot], sems.at[len(copies)]
                )
            )
    for copy in copies:
        copy.start()
    for copy in copies:
        copy.wait()


class Ring:
    def __init__(self, pieces, outs):
        self.count = lax.axis_size("seq") // 2
        self.place, self.route = ring_spot(), ring_route(self.count)
        self.core = lax.axis_index("seq") % 2
        self.mirror = (self.count - self.place) % self.count
        self.rows, self.cols = pieces[0][0].shape[0] // self.count, pieces[0][0].shape[1]
        self.pieces = [
            [a.reshape(self.count, self.rows, self.cols) for a in addends] for addends in pieces
        ]
        self.outs = outs
        self.step, self.own, self.far = 0, [], []
        self.held = self.chunk(self.place)

    def chunk(self, spot):
        return jnp.stack([sum(pick(a, spot) for a in addends) for addends in self.pieces])

    def turn(self, clock):
        got = clock.hold(lax.ppermute(self.held, "seq", self.route))
        self.step += 1
        if self.step < self.count:
            got = got + self.chunk((self.place + 2 * self.count - self.step) % self.count)
        self.held = got
        if self.step >= self.count - 1:
            self.own.append(got)
            self.far.append(swap_bit(got, "seq", 0))
        clock.set(got)

    def results(self):
        count = self.count
        hops = jnp.arange(count, dtype=jnp.int32)
        spots = jnp.concatenate([self.place + 1 - hops, self.mirror + 1 - hops]) + count
        which = jnp.repeat(jnp.stack([self.core, 1 - self.core]), count)
        where = jnp.stack([which, spots % count]).astype(jnp.int32)
        cuts, low = [], 0
        for size in self.outs:
            cuts.append((low, low + size))
            low += size
        shapes = [(size, 2, count, self.rows, self.cols) for size in self.outs]
        outs = pl.pallas_call(
            functools.partial(assemble_kernel, count, cuts),
            in_specs=[pl.BlockSpec(memory_space=pltpu.SMEM)]
            + [pl.BlockSpec(memory_space=pltpu.VMEM)] * (2 * count),
            out_specs=[pl.BlockSpec(memory_space=pl.ANY)] * len(shapes),
            out_shape=[jax.ShapeDtypeStruct(shape, jnp.float32) for shape in shapes],
            scratch_shapes=[pltpu.SemaphoreType.DMA((2 * count * len(shapes),))],
            cost_estimate=pl.CostEstimate(
                flops=0, bytes_accessed=8 * sum(math.prod(a) for a in shapes), transcendentals=0
            ),
        )(where, *self.own, *self.far)
        return [out.reshape(out.shape[0], -1, self.cols) for out in outs]


def core_half(value, which):
    size = value.shape[1] // 2
    return lax.dynamic_slice_in_dim(value, which * size, size, 1)


def rows8(shape):
    return lax.broadcasted_iota(jnp.int32, shape, 0).astype(jnp.float32)


def tree(values):
    values = list(values)
    while len(values) > 1:
        values = [sum(values[i : i + 2]) for i in range(0, len(values), 2)]
    return values[0]


def groups(decay_ref):
    states, lanes = decay_ref.shape
    for low in range(0, lanes, 128):
        span = slice(low, low + 128)
        rates = [jnp.broadcast_to(decay_ref[n : n + 1, span], (8, 128)) for n in range(states)]
        yield span, rates, [jnp.exp(-8.0 * rate) for rate in rates]


UNROLL = 4


def over_rows(ref, count, span, body, carry):
    def step(i, carry):
        for k in range(UNROLL):
            base = pl.multiple_of((i * UNROLL + k) * 8, 8)
            carry = body(ref[pl.ds(base, 8), span], carry)
        return carry

    return lax.fori_loop(0, count // (8 * UNROLL), step, carry)


def summary_kernel(tail_ref, x_ref, decay_ref, h_ref):
    for span, rates, jump in groups(decay_ref):

        def body(tile, acc):
            return tuple(j * a + tile for j, a in zip(jump, acc))

        acc = (tail_ref[:8, span] * 0.0,) * len(rates)
        acc = over_rows(tail_ref, tail_ref.shape[0], span, body, acc)
        acc = over_rows(x_ref, x_ref.shape[0] - tail_ref.shape[0], span, body, acc)
        left = 7.0 - rows8((8, 128))
        for n, rate in enumerate(rates):
            h_ref[n : n + 1, span] = jnp.sum(acc[n] * jnp.exp(-rate * left), axis=0, keepdims=True)


def moment_kernel(tail_ref, x_ref, decay_ref, p_ref):
    for span, rates, jump in groups(decay_ref):

        def body(tile, carry):
            acc, lag = carry
            lag = tuple(j * (b + a) for j, a, b in zip(jump, acc, lag))
            return tuple(j * a + tile for j, a in zip(jump, acc)), lag

        zeros = (tail_ref[:8, span] * 0.0,) * len(rates)
        carry = over_rows(tail_ref, tail_ref.shape[0], span, body, (zeros, zeros))
        acc, lag = over_rows(x_ref, x_ref.shape[0] - tail_ref.shape[0], span, body, carry)
        left = 7.0 - rows8((8, 128))
        for n, rate in enumerate(rates):
            total = (8.0 * lag[n] + left * acc[n]) * jnp.exp(-rate * left)
            p_ref[n : n + 1, span] = jnp.sum(total, axis=0, keepdims=True)


def carry_kernel(near_ref, first_ref, decay_ref, y_ref):
    for span, rates, jump in groups(decay_ref):
        ahead = rows8((8, 128)) + 1.0
        modes = tuple(
            jnp.broadcast_to(first_ref[n : n + 1, span], (8, 128)) * jnp.exp(-rate * ahead)
            for n, rate in enumerate(rates)
        )

        def step(i, modes):
            for k in range(UNROLL):
                base = pl.multiple_of((i * UNROLL + k) * 8, 8)
                y_ref[pl.ds(base, 8), span] = near_ref[pl.ds(base, 8), span] + tree(modes)
                modes = tuple(j * m for j, m in zip(jump, modes))
            return modes

        lax.fori_loop(0, y_ref.shape[0] // (8 * UNROLL), step, modes)


def spread_kernel(first_ref, decay_ref, tail_ref, y_ref):
    for span, rates, jump in groups(decay_ref):
        ahead = 8.0 - rows8((8, 128))
        modes = tuple(
            jnp.broadcast_to(first_ref[n : n + 1, span], (8, 128)) * jnp.exp(-rate * ahead)
            for n, rate in enumerate(rates)
        )

        def run(ref, modes):
            count = ref.shape[0] // 8

            def step(i, modes):
                for k in range(UNROLL):
                    base = pl.multiple_of((count - 1 - i * UNROLL - k) * 8, 8)
                    ref[pl.ds(base, 8), span] = tree(modes)
                    modes = tuple(j * m for j, m in zip(jump, modes))
                return modes

            return lax.fori_loop(0, count // UNROLL, step, modes)

        run(tail_ref, run(y_ref, modes))


def near_kernel(x_ref, fade_ref, gate_ref, skip_ref, y_ref):
    fade, gate, skip = fade_ref[...], gate_ref[...], skip_ref[...]

    def octet(i, u):
        base = pl.multiple_of(i * 8, 8)
        tile = x_ref[pl.ds(base, 8), :]
        rows = []
        for r in range(8):
            row = tile[r : r + 1, :]
            u = fade * u + gate * jnp.broadcast_to(row, fade.shape)
            rows.append(jnp.sum(u, axis=0, keepdims=True) + skip * row)
        y_ref[pl.ds(base, 8), :] = jnp.concatenate(rows, 0)
        return u

    lax.fori_loop(0, x_ref.shape[0] // 8, octet, jnp.zeros(fade.shape, jnp.float32))


def tail_back_kernel(
    x_ref, d_ref, fade_ref, gate_ref, skip_ref, q_ref, r_ref, dh_ref, dp_ref, dskip_ref, dx_ref
):
    fade, gate, skip = fade_ref[...], gate_ref[...], skip_ref[...]
    octets = x_ref.shape[0] // 8
    zero = jnp.zeros(fade.shape, jnp.float32)

    def forward(i, carry):
        h, p, dh, dp = carry
        base = pl.multiple_of(i * 8, 8)
        tile, grads = x_ref[pl.ds(base, 8), :], d_ref[pl.ds(base, 8), :]
        for r in range(8):
            p = fade * (p + h)
            h = fade * h + jnp.broadcast_to(tile[r : r + 1, :], fade.shape)
            grad = jnp.broadcast_to(grads[r : r + 1, :], fade.shape)
            dh = dh + grad * h
            dp = dp + grad * p
        return h, p, dh, dp

    _, _, dh, dp = lax.fori_loop(0, octets, forward, (zero, zero, zero, zero))
    dh_ref[...] = dh
    dp_ref[...] = dp
    dskip_ref[...] = jnp.sum(x_ref[...] * d_ref[...], axis=0, keepdims=True)

    def backward(k, carry):
        q, r_sum = carry
        base = pl.multiple_of((octets - 1 - k) * 8, 8)
        grads = d_ref[pl.ds(base, 8), :]
        rows = [None] * 8
        for r in reversed(range(8)):
            r_sum = fade * (r_sum + q)
            grad = grads[r : r + 1, :]
            q = fade * q + jnp.broadcast_to(grad, fade.shape)
            rows[r] = jnp.sum(gate * q, axis=0, keepdims=True) + skip * grad
        dx_ref[pl.ds(base, 8), :] = jnp.concatenate(rows, 0)
        return q, r_sum

    q, r_sum = lax.fori_loop(0, octets, backward, (zero, zero))
    q_ref[...] = q
    r_ref[...] = r_sum


def by_channels(kernel, ins, outs, cut=512):
    width = ins[0].shape[1]
    cut = cut if width % cut == 0 else width

    def spec(rows):
        return pl.BlockSpec((rows, cut), lambda i: (0, i))

    return pl.pallas_call(
        kernel,
        grid=(width // cut,),
        in_specs=[spec(a.shape[0]) for a in ins],
        out_specs=[spec(r) for r in outs],
        out_shape=[jax.ShapeDtypeStruct((r, width), jnp.float32) for r in outs],
        cost_estimate=pl.CostEstimate(flops=0, bytes_accessed=COST, transcendentals=0),
    )(*ins)


def cut(value):
    top = value.astype(jnp.bfloat16)
    return top, (value - top.astype(jnp.float32)).astype(jnp.bfloat16)


def dot3(left, right, dims):
    def one(a, b):
        return lax.dot_general(a, b, (dims, ((), ())), preferred_element_type=jnp.float32)

    return one(left[0], right[1]) + one(left[1], right[0]) + one(left[0], right[0])


NT = ((1,), (1,))
NN = ((1,), (0,))
TN = ((0,), (0,))
TILE = 256
LATE = 4
COST = 1024
SCALE = HDIM ** (-0.5)


def causal(shape, first_row):
    row = lax.broadcasted_iota(jnp.int32, shape, 0) + first_row
    return lax.broadcasted_iota(jnp.int32, shape, 1) <= row


def self_kernel(q_ref, k_ref, v_ref, acc_ref, top_ref, sum_ref):
    rows = q_ref.shape[0]
    k, v = cut(k_ref[...]), cut(v_ref[...])
    for first in range(0, rows, TILE):
        span = slice(first, first + TILE)
        seen = first + TILE
        q = cut(q_ref[span, :] * SCALE)
        scores = dot3(q, (k[0][:seen], k[1][:seen]), NT)
        scores = jnp.where(causal(scores.shape, first), scores, -1e30)
        top = jnp.max(scores, axis=1, keepdims=True)
        weight = jnp.exp(scores - top)
        acc_ref[span, :] = dot3(cut(weight), (v[0][:seen], v[1][:seen]), NN)
        top_ref[span, :] = jnp.broadcast_to(top, (TILE, HDIM))
        sum_ref[span, :] = jnp.broadcast_to(jnp.sum(weight, axis=1, keepdims=True), (TILE, HDIM))


def ctx_kernel(ok_ref, q_ref, k_ref, v_ref, acc_ref, top_ref, sum_ref, out_ref, log_ref):
    ok = ok_ref[0] > 0
    q = cut(q_ref[...] * SCALE)
    scores = dot3(q, cut(k_ref[...]), NT)
    scores = jnp.where(ok, scores, -1e30)
    top = jnp.maximum(top_ref[...], jnp.max(scores, axis=1, keepdims=True))
    weight = jnp.where(ok, jnp.exp(scores - top[:, :1]), 0.0)
    ease = jnp.exp(top_ref[...] - top)
    total = sum_ref[...] * ease + jnp.sum(weight, axis=1, keepdims=True)
    out_ref[...] = (acc_ref[...] * ease + dot3(cut(weight), cut(v_ref[...]), NN)) / total
    log_ref[...] = top + jnp.log(total)


def back_kernel(ok_ref, q_ref, k_ref, v_ref, kc_ref, vc_ref, o_ref, l_ref, g_ref, d_ref):
    ok = ok_ref[0] > 0
    rows = q_ref.shape[0]
    k, v, kc, vc = cut(k_ref[...]), cut(v_ref[...]), cut(kc_ref[...]), cut(vc_ref[...])
    d_ref[0, :CTX, :] = jnp.zeros((CTX, HDIM), jnp.float32)
    for first in reversed(range(0, rows, TILE)):
        seen = first + TILE
        span = slice(first, seen)
        grad = g_ref[span, :]
        q = cut(q_ref[span, :] * SCALE)
        grad2 = cut(grad)
        inner = jnp.sum(grad * o_ref[span, :], axis=1, keepdims=True)
        mark = l_ref[span, :][:, :1]
        ks, vs = (k[0][:seen], k[1][:seen]), (v[0][:seen], v[1][:seen])
        probs = dot3(q, ks, NT)
        probs = jnp.where(causal(probs.shape, first), jnp.exp(probs - mark), 0.0)
        probs_c = jnp.where(ok, jnp.exp(dot3(q, kc, NT) - mark), 0.0)
        ds = cut(probs * (dot3(grad2, vs, NT) - inner))
        ds_c = cut(probs_c * (dot3(grad2, vc, NT) - inner))
        probs, probs_c = cut(probs), cut(probs_c)
        d_ref[0, CTX + first : CTX + seen, :] = (dot3(ds, ks, NN) + dot3(ds_c, kc, NN)) * SCALE
        for at, (own, ctx, other) in enumerate([(ds, ds_c, q), (probs, probs_c, grad2)]):
            near, back = dot3(own, other, TN), dot3(ctx, other, TN)
            if seen == rows:
                d_ref[1 + at, CTX:, :] = near
                d_ref[1 + at, :CTX, :] = back
            else:
                d_ref[1 + at, CTX : CTX + seen, :] += near
                d_ref[1 + at, :CTX, :] += back


def by_heads(kernel, ins, outs, scalars=()):
    heads = ins[0][0].shape[1] // HDIM
    specs = [pl.BlockSpec(memory_space=pltpu.SMEM) for _ in scalars]
    for _, rows, at in ins:
        specs.append(pl.BlockSpec((rows, HDIM), lambda h, at=at: (at, h)))
    return pl.pallas_call(
        kernel,
        grid=(heads,),
        in_specs=specs,
        out_specs=[
            pl.BlockSpec(lead + (HDIM,), lambda h, n=len(lead): (0,) * n + (h,)) for lead in outs
        ],
        out_shape=[jax.ShapeDtypeStruct(lead + (heads * HDIM,), jnp.float32) for lead in outs],
        cost_estimate=pl.CostEstimate(flops=0, bytes_accessed=COST, transcendentals=0),
        compiler_params=pltpu.CompilerParams(vmem_limit_bytes=40 << 20),
    )(*scalars, *[a for a, _, _ in ins])


def per_device(
    tokens,
    window_state,
    norm1_gain,
    norm1_bias,
    in_coef,
    out_coef,
    decay_rate,
    skip_gain,
    qkv_weight,
    out_weight,
    norm2_gain,
    norm2_bias,
    up_weight,
    up_bias,
    down_weight,
    down_bias,
    cotangent,
):
    place_seq = lax.axis_index("seq")
    core = place_seq % 2
    rows, width = tokens.shape
    states = in_coef.shape[1]
    windows = window_state.shape[0]
    per_window = LEN // rows
    block = place_seq % per_window
    window = place_seq // per_window
    has_ctx = block > 0
    ok = has_ctx.astype(jnp.int32).reshape(1)
    half = rows // 2

    qkv = qkv_weight.astype(jnp.float32)
    out_own = out_weight.astype(jnp.float32)
    up = up_weight.astype(jnp.float32)
    down = down_weight.astype(jnp.float32)

    packed = jnp.concatenate(
        [jnp.transpose(a) for a in (decay_rate, in_coef, out_coef)]
        + [jnp.transpose(window_state[w]) for w in range(windows)]
        + [skip_gain[None]],
        0,
    )
    coefs, rounds = gather_all(packed)
    decay, c_in, c_out = (coefs[i * states : (i + 1) * states] for i in range(3))
    carried = lax.dynamic_slice_in_dim(coefs, (3 + window) * states, states, 0)
    skip = coefs[(3 + windows) * states :]
    gate = c_in * c_out
    fade = jnp.exp(-decay)

    def faded(steps):
        return jnp.exp(-decay * steps)

    inner = out_own.shape[0]
    sent = lax.dynamic_slice_in_dim(out_own, core * (inner // 2), inner // 2, 0)
    across = swap_bit(after(sent, rounds[1]), "mp", 0)
    beside = swap_bit(across, "seq", 0)
    out_far = jnp.where(
        core == 0, jnp.concatenate([across, beside], 0), jnp.concatenate([beside, across], 0)
    )

    unit1, rate1 = norm_parts(tokens)
    normed = after(unit1 * norm1_gain + norm1_bias)
    tail = shift_in_window(normed[rows - CTX :], 1, per_window)
    query = mm(normed, qkv[0])
    key = mm(normed, qkv[1])
    value = mm(normed, qkv[2])
    acc, top, total = by_heads(
        self_kernel,
        [(after(query, rounds[1]), rows, 0), (key, rows, 0), (value, rows, 0)],
        [(rows,)] * 3,
    )

    length = float(rows)
    chips = per_window // 2
    chip = block // 2
    (sum_h,) = by_channels(
        summary_kernel,
        [tail, after(normed, acc), decay],
        [states],
    )

    def pair_order(value):
        other = swap_bit(value, "seq", 0)
        return jnp.where(core == 0, value, other), jnp.where(core == 0, other, value)

    first_h, second_h = pair_order(sum_h)
    both_h = faded(length) * first_h + second_h
    far_h = [trade_chips(both_h, d) for d in range(1, chips)]
    (near,) = by_channels(
        near_kernel, [after(tail, sum_h), fade, gate, skip], [CTX]
    )
    far_h = [after(h, near) for h in far_h]
    past_h = jnp.zeros_like(sum_h)
    for d in range(1, chips):
        there = chip ^ d
        gap = jnp.maximum(chip - 1 - there, 0).astype(jnp.float32) * (2.0 * length)
        past_h = past_h + jnp.where(there < chip, faded(gap) * far_h[d - 1], 0.0)
    chip_h = past_h
    past_h = jnp.where(core == 0, past_h, faded(length) * past_h + first_h)

    start_t = jnp.maximum(block * rows - CTX, 0).astype(jnp.float32)
    first = c_out * (c_in * past_h + carried * faded(start_t))

    (context,) = by_channels(
        carry_kernel, [near, first, decay], [CTX]
    )
    key_ctx = mm(context, qkv[1])
    value_ctx = mm(context, qkv[2])
    heads, logs, far = [], [], []
    for part in range(2):
        o, l = by_heads(
            ctx_kernel,
            [(query, half, part), (key_ctx, CTX, 0), (after(value_ctx, *heads), CTX, 0)]
            + [(a, half, part) for a in (acc, top, total)],
            [(half,)] * 2,
            scalars=(ok,),
        )
        heads.append(o)
        logs.append(l)
        far.append(swap_bit(o, "mp", 0))
    grad_hidden = mm(after(cotangent, *heads), down, NT)
    seen = jnp.concatenate([after(context, *heads), normed], 0)
    outs = jnp.concatenate(heads, 0)
    log = jnp.concatenate(logs, 0)

    hidden, grad_pre = unset((rows, up.shape[1])), unset((rows, up.shape[1]))
    normed2 = unset((rows, width))
    mixed, part2 = [], []
    for part in range(2):
        span = slice(part * half, (part + 1) * half)
        came = after(far[part], part2[0]) if part else after(far[0], seen, outs, log, grad_hidden)
        m = tokens[span] + (mm(heads[part], out_own) + mm(came, out_far))
        n = norm_parts(m)[0] * norm2_gain + norm2_bias
        pre = mm(n, up) + up_bias
        cdf = 0.5 + 0.5 * lax.erf(pre * (0.5**0.5))
        bell = jnp.exp(-0.5 * pre * pre) * (1.0 / math.sqrt(2.0 * math.pi))
        hidden = lax.dynamic_update_slice(hidden, pre * cdf, (part * half, 0))
        slope = grad_hidden[span] * (cdf + pre * bell)
        grad_pre = lax.dynamic_update_slice(grad_pre, slope, (part * half, 0))
        normed2 = lax.dynamic_update_slice(normed2, n, (part * half, 0))
        mixed.append(m)
        if part == 0:
            part2.append(mm(grad_pre[span], up, NT))

    clock = Clock()
    give = mm(core_half(after(hidden, part2[0]), 1 - core), cotangent, TN)
    keep = mm(core_half(after(hidden, give), core), cotangent, TN)
    down_ring = Ring([[keep, swap_bit(give, "seq", 0)]], (1,))
    clock.set(down_ring.held)
    part2.append(mm(clock.hold(grad_pre)[half:], up, NT))
    clock.set(part2[1])
    gots2 = [swap_bit(p, "mp", 0) for p in part2]
    down_ring.turn(clock)
    give = mm(core_half(clock.hold(normed2), 1 - core), grad_pre, TN)
    clock.set(give)
    down_ring.turn(clock)
    keep = mm(core_half(clock.hold(normed2), core), grad_pre, TN) + swap_bit(give, "seq", 0)
    up_ring = Ring([[keep]], (1,))
    clock.set(up_ring.held)
    hops = down_ring.count - 1
    down_ring.turn(clock)
    (sum_p,) = by_channels(moment_kernel, [tail, clock.hold(normed), decay], [states])
    clock.set(sum_p)
    up_ring.turn(clock)
    down_ring.turn(clock)

    grad2 = jnp.concatenate([p + clock.hold(g) for p, g in zip(part2, gots2)], 0)
    mixed = jnp.concatenate(mixed, 0)
    unit2, rate2 = norm_parts(after(mixed, grad2))
    gain2 = jnp.sum(grad2 * unit2, axis=0)
    bias2 = jnp.sum(grad2, axis=0)
    grad_mixed = cotangent + norm_back(grad2, unit2, rate2, norm2_gain)
    clock.set(grad_mixed, gain2, bias2)
    up_ring.turn(clock)
    down_ring.turn(clock)
    grad_heads = mm(clock.hold(grad_mixed), out_own, NT)
    clock.set(grad_heads)

    (grads,) = by_heads(
        back_kernel,
        [(query, rows, 0), (key, rows, 0), (value, rows, 0), (key_ctx, CTX, 0), (value_ctx, CTX, 0)]
        + [(a, rows, 0) for a in (outs, log, clock.hold(grad_heads))],
        [(3, CTX + rows)],
        scalars=(ok,),
    )
    clock.set(grads)
    up_ring.turn(clock)
    down_ring.turn(clock)
    gives = [mm(core_half(clock.hold(seen), 1 - core), grads[i], TN) for i in range(3)]
    gives.append(mm(core_half(clock.hold(grad_mixed), 1 - core), outs, TN))
    gots = [swap_bit(g, "seq", 0) for g in gives]
    clock.set(*gives)
    up_ring.turn(clock)
    down_ring.turn(clock)
    feed = mm(clock.hold(hidden), down)
    clock.set(feed)
    feed = lax.psum(feed, "mp")
    up_ring.turn(clock)
    down_ring.turn(clock)
    keeps = [mm(core_half(clock.hold(seen), core), grads[i], TN) + gots[i] for i in range(3)]
    keeps.append(mm(core_half(clock.hold(grad_mixed), core), outs, TN) + gots[3])
    attn_ring = Ring([[k] for k in keeps], (3, 1))
    clock.set(attn_ring.held)
    while up_ring.step < hops:
        up_ring.turn(clock)
        if down_ring.step < hops + 2:
            down_ring.turn(clock)

    left_down, left_up = 2 * hops - down_ring.step, 2 * hops - up_ring.step
    queue = [up_ring] * (left_up - left_down) + [down_ring, up_ring] * left_down

    def next_turn():
        if attn_ring.step < attn_ring.count * 2 - 2:
            attn_ring.turn(clock)
        if queue:
            queue.pop(0).turn(clock)

    held = clock.hold(grads)
    grad_seen = sum(mm(held[i], qkv[i], NT) for i in range(3))
    grad_context = jnp.where(has_ctx, grad_seen[:CTX], 0.0)
    clock.set(grad_seen)
    next_turn()

    sum_q, sum_r, part_h, part_p, part_skip, grad_tail = by_channels(
        tail_back_kernel,
        [tail, clock.hold(grad_context), fade, gate, skip],
        [states, states, states, states, 1, CTX],
    )
    clock.set(sum_q)
    next_turn()
    other = swap_bit(jnp.concatenate([sum_p, sum_q], 0), "seq", 0)
    other_p, other_q = other[:states], other[states:]
    first_p, second_p = jnp.where(core == 0, sum_p, other_p), jnp.where(core == 0, other_p, sum_p)
    first_q, second_q = jnp.where(core == 0, sum_q, other_q), jnp.where(core == 0, other_q, sum_q)
    both_p = faded(length) * (first_p + length * first_h) + second_p
    both_q = first_q + faded(length) * second_q
    both = jnp.concatenate([both_p, both_q], 0)
    clock.set(both)
    past_p = jnp.zeros_like(sum_p)
    later = jnp.zeros_like(sum_q)
    came = [trade_chips(both, d) for d in range(1, chips)]
    next_turn()
    for d in range(1, chips):
        there = chip ^ d
        gap = (jnp.maximum(jnp.abs(chip - there) - 1, 0)).astype(jnp.float32) * (2.0 * length)
        near_p, near_q = came[d - 1][:states], came[d - 1][states:]
        fading = faded(gap)
        past_p = past_p + jnp.where(there < chip, fading * (near_p + gap * far_h[d - 1]), 0.0)
        later = later + jnp.where(there > chip, fading * near_q, 0.0)
    past_p = jnp.where(core == 0, past_p, faded(length) * (past_p + length * chip_h) + first_p)
    later = jnp.where(core == 1, later, second_q + faded(length) * later)
    far_tail, grad_rows = by_channels(
        spread_kernel,
        [clock.hold(gate * later), decay],
        [CTX, rows - CTX],
    )
    to_last = far_tail + grad_tail
    clock.set(to_last)
    from_next = shift_in_window(to_last, -1, per_window)
    next_turn()
    along_h = fade * past_h * sum_q + part_h
    along_p = fade * (past_h * (sum_r + sum_q) + past_p * sum_q) + part_p
    gone = faded(start_t + 1.0)
    part_in = c_out * along_h
    part_out = c_in * along_h + carried * gone * sum_q
    part_decay = -gate * along_p - c_out * carried * gone * ((start_t + 1.0) * sum_q + sum_r)
    stacked = jnp.concatenate([part_in, part_out, part_decay, part_skip], 0)
    clock.set(stacked)
    grad_normed = grad_seen[CTX:] + jnp.concatenate([grad_rows, clock.hold(from_next)], 0)
    result = mixed + clock.hold(feed) + down_bias
    grad_normed = after(grad_normed, result)
    clock.set(grad_normed)
    grad_normed = lax.psum(grad_normed, "mp")
    next_turn()
    far_stacked = swap_bit(stacked, "mp", 0)
    grad_up_bias = jnp.sum(clock.hold(grad_pre), axis=0)
    clock.set(grad_up_bias)
    next_turn()
    grad_down_bias = jnp.sum(clock.hold(cotangent), axis=0)
    ups = grad_up_bias.reshape(-1, width)
    small = jnp.concatenate(
        [stacked + clock.hold(far_stacked), jnp.stack([gain2, bias2, grad_down_bias]), ups], 0
    )
    clock.set(small)
    for bit in range(bits_of(lax.axis_size("seq"))):
        other = swap_bit(small, "seq", bit)
        next_turn()
        small = small + clock.hold(other)
        clock.set(small)
    while attn_ring.step < attn_ring.count * 2 - 2 - LATE:
        next_turn()
    last = clock.hold(grad_normed)
    grad_gain1 = jnp.sum(last * unit1, axis=0)
    grad_bias1 = jnp.sum(last, axis=0)
    grad_tokens = grad_mixed + norm_back(last, unit1, rate1, norm1_gain)
    late = jnp.stack([grad_gain1, grad_bias1])
    clock.set(grad_tokens, late)
    for bit in range(bits_of(lax.axis_size("seq"))):
        other = swap_bit(late, "seq", bit)
        next_turn()
        late = late + clock.hold(other)
        clock.set(late)
    while attn_ring.step < attn_ring.count * 2 - 2:
        next_turn()
    grad_down = down_ring.results()[0][0]
    grad_up = up_ring.results()[0][0]
    grad_qkv, grad_out = attn_ring.results()
    grad_out = jnp.transpose(grad_out[0])

    channels = in_coef.shape[0]
    at = (place_seq * lax.axis_size("mp") + lax.axis_index("mp")) * channels
    own = jnp.transpose(lax.dynamic_slice_in_dim(small[: 3 * states + 1], at, channels, 1))
    grad_in = own[:, :states]
    grad_out_coef = own[:, states : 2 * states]
    grad_decay = own[:, 2 * states : 3 * states]
    grad_skip = own[:, 3 * states]
    small = small[3 * states + 1 :]
    return (
        result,
        grad_tokens,
        late[0],
        late[1],
        grad_in,
        grad_out_coef,
        grad_decay,
        grad_skip,
        grad_qkv,
        grad_out,
        small[0],
        small[1],
        grad_up,
        small[3:].reshape(-1),
        grad_down,
        small[2],
    )


def solution(mesh):
    owner = P(("seq", "mp"), None)
    return jax.shard_map(
        per_device,
        mesh=mesh,
        in_specs=(
            P("seq", None),
            P(None, ("seq", "mp"), None),
            P(),
            P(),
            owner,
            owner,
            owner,
            P(("seq", "mp")),
            P(None, None, "mp"),
            P("mp", None),
            P(),
            P(),
            P(None, "mp"),
            P("mp"),
            P("mp", None),
            P(),
            P("seq", None),
        ),
        out_specs=(
            P("seq", None),
            P("seq", None),
            P(),
            P(),
            owner,
            owner,
            owner,
            P(("seq", "mp")),
            P(None, None, "mp"),
            P("mp", None),
            P(),
            P(),
            P(None, "mp"),
            P("mp"),
            P("mp", None),
            P(),
        ),
        check_vma=False,
    )
```

```python
import functools
import math

import jax
import jax.numpy as jnp
from jax import lax
from jax.experimental import pallas as pl
from jax.experimental.pallas import tpu as pltpu
from jax.sharding import PartitionSpec as P

HDIM = 128
BLOCK = 512
CTX = 128
LEN = 4096
EPS = 1e-05
HIGH = lax.Precision.HIGH


def mm(left, right, dims=((1,), (0,))):
    return lax.dot_general(
        left, right, (dims, ((), ())), precision=HIGH, preferred_element_type=jnp.float32
    )


def norm_parts(value):
    center = value - jnp.mean(value, axis=-1, keepdims=True)
    spread = jnp.mean(center * center, axis=-1, keepdims=True)
    rate = lax.rsqrt(spread + EPS)
    return center * rate, rate


def norm_back(grad, unit, rate, gain):
    scaled = grad * gain
    inner = jnp.mean(scaled * unit, axis=-1, keepdims=True)
    return rate * (scaled - jnp.mean(scaled, axis=-1, keepdims=True) - unit * inner)


def swap_bit(value, axis, bit):
    size = lax.axis_size(axis)
    return lax.ppermute(value, axis, [(i, i ^ (1 << bit)) for i in range(size)])


def bits_of(count):
    return count.bit_length() - 1


def shift_in_window(value, distance, per_window):
    size = lax.axis_size("seq")
    route = [(i, i + distance) for i in range(size)]
    inside = [(a, b) for a, b in route if 0 <= b < size and a // per_window == b // per_window]
    return lax.ppermute(value, "seq", inside)


def after(value, *others):
    return lax.optimization_barrier((value,) + others)[0]


def gather_all(piece, gates=()):
    mp_size, seq_size = lax.axis_size("mp"), lax.axis_size("seq")
    me = lax.axis_index("seq") * mp_size + lax.axis_index("mp")
    block, seen = piece, []
    for bit in range(bits_of(mp_size * seq_size)):
        axis, own = ("mp", bit) if bit < bits_of(mp_size) else ("seq", bit - bits_of(mp_size))
        if gates:
            block = after(block, gates[bit])
        other = swap_bit(block, axis, own)
        upper = (me >> bit) & 1
        block = jnp.where(
            upper == 1, jnp.concatenate([other, block], 1), jnp.concatenate([block, other], 1)
        )
        seen.append(block)
    return block, seen


def trade_chips(value, distance):
    size = lax.axis_size("seq")
    return lax.ppermute(value, "seq", [(i, i ^ (2 * distance)) for i in range(size)])


def chip_order(count):
    if count <= 2:
        return list(range(count))
    return list(range(0, count, 2)) + list(range(count - 1 - count % 2, 0, -2))


def ring_route(count):
    order = chip_order(count)
    route = []
    for i in range(count):
        here, there = order[i], order[(i + 1) % count]
        route.append((2 * here, 2 * there))
        route.append((2 * there + 1, 2 * here + 1))
    return route


def ring_spot():
    count = lax.axis_size("seq") // 2
    places = [0] * count
    for i, chip in enumerate(chip_order(count)):
        places[chip] = i
    me = lax.axis_index("seq")
    here = jnp.array(places, jnp.int32)[me // 2]
    return jnp.where(me % 2 == 0, here, (count - here) % count)


def unset(shape):
    return pl.pallas_call(
        lambda out: None,
        out_shape=jax.ShapeDtypeStruct(shape, jnp.float32),
        out_specs=pl.BlockSpec(memory_space=pl.ANY),
    )()


def pick(value, index):
    return lax.dynamic_index_in_dim(value, index, 0, keepdims=False)


class Clock:
    def __init__(self):
        self.last = ()

    def hold(self, value):
        return after(value, *self.last) if self.last else value

    def set(self, *values):
        self.last = values


def assemble_kernel(count, cuts, where_ref, *refs):
    parts, outs, sems = refs[: 2 * count], refs[2 * count : -1], refs[-1]
    copies = []
    for n in range(2 * count):
        which, spot = where_ref[0, n], where_ref[1, n]
        for out, (low, high) in zip(outs, cuts):
            copies.append(
                pltpu.make_async_copy(
                    parts[n].at[low:high], out.at[:, which, spot], sems.at[len(copies)]
                )
            )
    for copy in copies:
        copy.start()
    for copy in copies:
        copy.wait()


class Ring:
    def __init__(self, pieces, outs):
        self.count = lax.axis_size("seq") // 2
        self.place, self.route = ring_spot(), ring_route(self.count)
        self.core = lax.axis_index("seq") % 2
        self.mirror = (self.count - self.place) % self.count
        self.rows, self.cols = pieces[0][0].shape[0] // self.count, pieces[0][0].shape[1]
        self.pieces = [
            [a.reshape(self.count, self.rows, self.cols) for a in addends] for addends in pieces
        ]
        self.outs = outs
        self.step, self.own, self.far = 0, [], []
        self.held = self.chunk(self.place)

    def chunk(self, spot):
        return jnp.stack([sum(pick(a, spot) for a in addends) for addends in self.pieces])

    def turn(self, clock, kept=()):
        got = lax.ppermute(self.held, "seq", self.route)
        got, *kept = lax.optimization_barrier((got, *kept, *clock.last))[: 1 + len(kept)]
        self.step += 1
        if self.step < self.count:
            got = got + self.chunk((self.place + 2 * self.count - self.step) % self.count)
        self.held = got
        if self.step >= self.count - 1:
            self.own.append(got)
            self.far.append(swap_bit(got, "seq", 0))
        clock.set(got)
        return kept

    def results(self):
        count = self.count
        hops = jnp.arange(count, dtype=jnp.int32)
        spots = jnp.concatenate([self.place + 1 - hops, self.mirror + 1 - hops]) + count
        which = jnp.repeat(jnp.stack([self.core, 1 - self.core]), count)
        where = jnp.stack([which, spots % count]).astype(jnp.int32)
        cuts, low = [], 0
        for size in self.outs:
            cuts.append((low, low + size))
            low += size
        shapes = [(size, 2, count, self.rows, self.cols) for size in self.outs]
        outs = pl.pallas_call(
            functools.partial(assemble_kernel, count, cuts),
            in_specs=[pl.BlockSpec(memory_space=pltpu.SMEM)]
            + [pl.BlockSpec(memory_space=pltpu.VMEM)] * (2 * count),
            out_specs=[pl.BlockSpec(memory_space=pl.ANY)] * len(shapes),
            out_shape=[jax.ShapeDtypeStruct(shape, jnp.float32) for shape in shapes],
            scratch_shapes=[pltpu.SemaphoreType.DMA((2 * count * len(shapes),))],
            cost_estimate=pl.CostEstimate(flops=0, bytes_accessed=COST, transcendentals=0),
        )(where, *self.own, *self.far)
        return [out.reshape(out.shape[0], -1, self.cols) for out in outs]


def core_half(value, which):
    size = value.shape[1] // 2
    return lax.dynamic_slice_in_dim(value, which * size, size, 1)


def rows8(shape):
    return lax.broadcasted_iota(jnp.int32, shape, 0).astype(jnp.float32)


def tree(values):
    values = list(values)
    while len(values) > 1:
        values = [sum(values[i : i + 2]) for i in range(0, len(values), 2)]
    return values[0]


def groups(decay_ref):
    states, lanes = decay_ref.shape
    for low in range(0, lanes, 128):
        span = slice(low, low + 128)
        rates = [jnp.broadcast_to(decay_ref[n : n + 1, span], (8, 128)) for n in range(states)]
        yield span, rates, [jnp.exp(-8.0 * rate) for rate in rates]


UNROLL = 4


def over_rows(ref, count, span, body, carry):
    def step(i, carry):
        for k in range(UNROLL):
            base = pl.multiple_of((i * UNROLL + k) * 8, 8)
            carry = body(ref[pl.ds(base, 8), span], carry)
        return carry

    return lax.fori_loop(0, count // (8 * UNROLL), step, carry)


def summary_kernel(tail_ref, x_ref, decay_ref, h_ref):
    for span, rates, jump in groups(decay_ref):

        def body(tile, acc):
            return tuple(j * a + tile for j, a in zip(jump, acc))

        acc = (tail_ref[:8, span] * 0.0,) * len(rates)
        acc = over_rows(tail_ref, tail_ref.shape[0], span, body, acc)
        acc = over_rows(x_ref, x_ref.shape[0] - tail_ref.shape[0], span, body, acc)
        left = 7.0 - rows8((8, 128))
        for n, rate in enumerate(rates):
            h_ref[n : n + 1, span] = jnp.sum(acc[n] * jnp.exp(-rate * left), axis=0, keepdims=True)


def moment_kernel(tail_ref, x_ref, decay_ref, p_ref):
    for span, rates, jump in groups(decay_ref):

        def body(tile, carry):
            acc, lag = carry
            lag = tuple(j * (b + a) for j, a, b in zip(jump, acc, lag))
            return tuple(j * a + tile for j, a in zip(jump, acc)), lag

        zeros = (tail_ref[:8, span] * 0.0,) * len(rates)
        carry = over_rows(tail_ref, tail_ref.shape[0], span, body, (zeros, zeros))
        acc, lag = over_rows(x_ref, x_ref.shape[0] - tail_ref.shape[0], span, body, carry)
        left = 7.0 - rows8((8, 128))
        for n, rate in enumerate(rates):
            total = (8.0 * lag[n] + left * acc[n]) * jnp.exp(-rate * left)
            p_ref[n : n + 1, span] = jnp.sum(total, axis=0, keepdims=True)


def carry_kernel(near_ref, first_ref, decay_ref, y_ref):
    for span, rates, jump in groups(decay_ref):
        ahead = rows8((8, 128)) + 1.0
        modes = tuple(
            jnp.broadcast_to(first_ref[n : n + 1, span], (8, 128)) * jnp.exp(-rate * ahead)
            for n, rate in enumerate(rates)
        )

        def step(i, modes):
            for k in range(UNROLL):
                base = pl.multiple_of((i * UNROLL + k) * 8, 8)
                y_ref[pl.ds(base, 8), span] = near_ref[pl.ds(base, 8), span] + tree(modes)
                modes = tuple(j * m for j, m in zip(jump, modes))
            return modes

        lax.fori_loop(0, y_ref.shape[0] // (8 * UNROLL), step, modes)


def spread_kernel(first_ref, decay_ref, tail_ref, y_ref):
    for span, rates, jump in groups(decay_ref):
        ahead = 8.0 - rows8((8, 128))
        modes = tuple(
            jnp.broadcast_to(first_ref[n : n + 1, span], (8, 128)) * jnp.exp(-rate * ahead)
            for n, rate in enumerate(rates)
        )

        def run(ref, modes):
            count = ref.shape[0] // 8

            def step(i, modes):
                for k in range(UNROLL):
                    base = pl.multiple_of((count - 1 - i * UNROLL - k) * 8, 8)
                    ref[pl.ds(base, 8), span] = tree(modes)
                    modes = tuple(j * m for j, m in zip(jump, modes))
                return modes

            return lax.fori_loop(0, count // UNROLL, step, modes)

        run(tail_ref, run(y_ref, modes))


def near_kernel(x_ref, fade_ref, gate_ref, skip_ref, y_ref):
    fade, gate, skip = fade_ref[...], gate_ref[...], skip_ref[...]

    def octet(i, u):
        base = pl.multiple_of(i * 8, 8)
        tile = x_ref[pl.ds(base, 8), :]
        rows = []
        for r in range(8):
            row = tile[r : r + 1, :]
            u = fade * u + gate * jnp.broadcast_to(row, fade.shape)
            rows.append(jnp.sum(u, axis=0, keepdims=True) + skip * row)
        y_ref[pl.ds(base, 8), :] = jnp.concatenate(rows, 0)
        return u

    lax.fori_loop(0, x_ref.shape[0] // 8, octet, jnp.zeros(fade.shape, jnp.float32))


def tail_back_kernel(
    x_ref, d_ref, fade_ref, gate_ref, skip_ref, q_ref, r_ref, dh_ref, dp_ref, dskip_ref, dx_ref
):
    fade, gate, skip = fade_ref[...], gate_ref[...], skip_ref[...]
    octets = x_ref.shape[0] // 8
    zero = jnp.zeros(fade.shape, jnp.float32)

    def forward(i, carry):
        h, p, dh, dp = carry
        base = pl.multiple_of(i * 8, 8)
        tile, grads = x_ref[pl.ds(base, 8), :], d_ref[pl.ds(base, 8), :]
        for r in range(8):
            p = fade * (p + h)
            h = fade * h + jnp.broadcast_to(tile[r : r + 1, :], fade.shape)
            grad = jnp.broadcast_to(grads[r : r + 1, :], fade.shape)
            dh = dh + grad * h
            dp = dp + grad * p
        return h, p, dh, dp

    _, _, dh, dp = lax.fori_loop(0, octets, forward, (zero, zero, zero, zero))
    dh_ref[...] = dh
    dp_ref[...] = dp
    dskip_ref[...] = jnp.sum(x_ref[...] * d_ref[...], axis=0, keepdims=True)

    def backward(k, carry):
        q, r_sum = carry
        base = pl.multiple_of((octets - 1 - k) * 8, 8)
        grads = d_ref[pl.ds(base, 8), :]
        rows = [None] * 8
        for r in reversed(range(8)):
            r_sum = fade * (r_sum + q)
            grad = grads[r : r + 1, :]
            q = fade * q + jnp.broadcast_to(grad, fade.shape)
            rows[r] = jnp.sum(gate * q, axis=0, keepdims=True) + skip * grad
        dx_ref[pl.ds(base, 8), :] = jnp.concatenate(rows, 0)
        return q, r_sum

    q, r_sum = lax.fori_loop(0, octets, backward, (zero, zero))
    q_ref[...] = q
    r_ref[...] = r_sum


def by_channels(kernel, ins, outs, cut=512):
    width = ins[0].shape[1]
    cut = cut if width % cut == 0 else width

    def spec(rows):
        return pl.BlockSpec((rows, cut), lambda i: (0, i))

    return pl.pallas_call(
        kernel,
        grid=(width // cut,),
        in_specs=[spec(a.shape[0]) for a in ins],
        out_specs=[spec(r) for r in outs],
        out_shape=[jax.ShapeDtypeStruct((r, width), jnp.float32) for r in outs],
        cost_estimate=pl.CostEstimate(flops=0, bytes_accessed=COST, transcendentals=0),
    )(*ins)


def cut(value):
    top = value.astype(jnp.bfloat16)
    return top, (value - top.astype(jnp.float32)).astype(jnp.bfloat16)


def dot3(left, right, dims):
    def one(a, b):
        return lax.dot_general(a, b, (dims, ((), ())), preferred_element_type=jnp.float32)

    return one(left[0], right[1]) + one(left[1], right[0]) + one(left[0], right[0])


NT = ((1,), (1,))
NN = ((1,), (0,))
TN = ((0,), (0,))
TILE = 256
COST = 1024
SCALE = HDIM ** (-0.5)


def causal(shape, first_row):
    row = lax.broadcasted_iota(jnp.int32, shape, 0) + first_row
    return lax.broadcasted_iota(jnp.int32, shape, 1) <= row


def self_kernel(q_ref, k_ref, v_ref, acc_ref, top_ref, sum_ref):
    rows = q_ref.shape[0]
    k, v = cut(k_ref[...]), cut(v_ref[...])
    for first in range(0, rows, TILE):
        span = slice(first, first + TILE)
        seen = first + TILE
        q = cut(q_ref[span, :] * SCALE)
        scores = dot3(q, (k[0][:seen], k[1][:seen]), NT)
        scores = jnp.where(causal(scores.shape, first), scores, -1e30)
        top = jnp.max(scores, axis=1, keepdims=True)
        weight = jnp.exp(scores - top)
        acc_ref[span, :] = dot3(cut(weight), (v[0][:seen], v[1][:seen]), NN)
        top_ref[span, :] = jnp.broadcast_to(top, (TILE, HDIM))
        sum_ref[span, :] = jnp.broadcast_to(jnp.sum(weight, axis=1, keepdims=True), (TILE, HDIM))


def ctx_kernel(ok_ref, q_ref, k_ref, v_ref, acc_ref, top_ref, sum_ref, out_ref, log_ref):
    ok = ok_ref[0] > 0
    q = cut(q_ref[...] * SCALE)
    scores = dot3(q, cut(k_ref[...]), NT)
    scores = jnp.where(ok, scores, -1e30)
    top = jnp.maximum(top_ref[...], jnp.max(scores, axis=1, keepdims=True))
    weight = jnp.where(ok, jnp.exp(scores - top[:, :1]), 0.0)
    ease = jnp.exp(top_ref[...] - top)
    total = sum_ref[...] * ease + jnp.sum(weight, axis=1, keepdims=True)
    out_ref[...] = (acc_ref[...] * ease + dot3(cut(weight), cut(v_ref[...]), NN)) / total
    log_ref[...] = top + jnp.log(total)


def back_kernel(ok_ref, q_ref, k_ref, v_ref, kc_ref, vc_ref, o_ref, l_ref, g_ref, d_ref):
    ok = ok_ref[0] > 0
    rows = q_ref.shape[0]
    k, v, kc, vc = cut(k_ref[...]), cut(v_ref[...]), cut(kc_ref[...]), cut(vc_ref[...])
    d_ref[0, :CTX, :] = jnp.zeros((CTX, HDIM), jnp.float32)
    for first in reversed(range(0, rows, TILE)):
        seen = first + TILE
        span = slice(first, seen)
        grad = g_ref[span, :]
        q = cut(q_ref[span, :] * SCALE)
        grad2 = cut(grad)
        inner = jnp.sum(grad * o_ref[span, :], axis=1, keepdims=True)
        mark = l_ref[span, :][:, :1]
        ks, vs = (k[0][:seen], k[1][:seen]), (v[0][:seen], v[1][:seen])
        probs = dot3(q, ks, NT)
        probs = jnp.where(causal(probs.shape, first), jnp.exp(probs - mark), 0.0)
        probs_c = jnp.where(ok, jnp.exp(dot3(q, kc, NT) - mark), 0.0)
        ds = cut(probs * (dot3(grad2, vs, NT) - inner))
        ds_c = cut(probs_c * (dot3(grad2, vc, NT) - inner))
        probs, probs_c = cut(probs), cut(probs_c)
        d_ref[0, CTX + first : CTX + seen, :] = (dot3(ds, ks, NN) + dot3(ds_c, kc, NN)) * SCALE
        for at, (own, ctx, other) in enumerate([(ds, ds_c, q), (probs, probs_c, grad2)]):
            near, back = dot3(own, other, TN), dot3(ctx, other, TN)
            if seen == rows:
                d_ref[1 + at, CTX:, :] = near
                d_ref[1 + at, :CTX, :] = back
            else:
                d_ref[1 + at, CTX : CTX + seen, :] += near
                d_ref[1 + at, :CTX, :] += back


def by_heads(kernel, ins, outs, scalars=()):
    heads = ins[0][0].shape[-1] // HDIM
    specs = [pl.BlockSpec(memory_space=pltpu.SMEM) for _ in scalars]
    for _, rows, *at in ins:
        if len(at) == 2:
            specs.append(pl.BlockSpec((None, rows, HDIM), lambda h, at=at: (at[1], at[0], h)))
        else:
            specs.append(pl.BlockSpec((rows, HDIM), lambda h, at=at: (at[0], h)))
    return pl.pallas_call(
        kernel,
        grid=(heads,),
        in_specs=specs,
        out_specs=[
            pl.BlockSpec(lead + (HDIM,), lambda h, n=len(lead): (0,) * n + (h,)) for lead in outs
        ],
        out_shape=[jax.ShapeDtypeStruct(lead + (heads * HDIM,), jnp.float32) for lead in outs],
        cost_estimate=pl.CostEstimate(flops=0, bytes_accessed=COST, transcendentals=0),
        compiler_params=pltpu.CompilerParams(vmem_limit_bytes=40 << 20),
    )(*scalars, *[a[0] for a in ins])


def project_kernel(x_ref, w_ref, out_ref, high_ref, low_ref):
    @pl.when(pl.program_id(0) == 0)
    def _():
        high_ref[...], low_ref[...] = cut(x_ref[...])

    def one(part):
        return lax.dot_general(
            part, w_ref[...], (NN, ((), ())), preferred_element_type=jnp.float32
        )

    out_ref[...] = one(low_ref[...]) + one(high_ref[...])


def project(x, weights, first, count):
    rows, depth = x.shape
    width = weights.shape[2]
    return pl.pallas_call(
        project_kernel,
        grid=(count,),
        in_specs=[
            pl.BlockSpec((rows, depth), lambda i: (0, 0)),
            pl.BlockSpec((None, depth, width), lambda i: (first + i, 0, 0)),
        ],
        out_specs=pl.BlockSpec((None, rows, width), lambda i: (i, 0, 0)),
        out_shape=jax.ShapeDtypeStruct((count, rows, width), jnp.float32),
        scratch_shapes=[pltpu.VMEM((rows, depth), jnp.bfloat16)] * 2,
        cost_estimate=pl.CostEstimate(flops=0, bytes_accessed=COST, transcendentals=0),
        compiler_params=pltpu.CompilerParams(vmem_limit_bytes=40 << 20),
    )(x, weights)


def per_device(
    tokens,
    window_state,
    norm1_gain,
    norm1_bias,
    in_coef,
    out_coef,
    decay_rate,
    skip_gain,
    qkv_weight,
    out_weight,
    norm2_gain,
    norm2_bias,
    up_weight,
    up_bias,
    down_weight,
    down_bias,
    cotangent,
):
    place_seq = lax.axis_index("seq")
    core = place_seq % 2
    rows, width = tokens.shape
    states = in_coef.shape[1]
    windows = window_state.shape[0]
    per_window = LEN // rows
    block = place_seq % per_window
    window = place_seq // per_window
    has_ctx = block > 0
    ok = has_ctx.astype(jnp.int32).reshape(1)
    half = rows // 2

    qkv = qkv_weight.astype(jnp.float32)
    out_own = out_weight.astype(jnp.float32)
    up = up_weight.astype(jnp.float32)
    down = down_weight.astype(jnp.float32)

    packed = jnp.concatenate(
        [jnp.transpose(a) for a in (decay_rate, in_coef, out_coef)]
        + [jnp.transpose(window_state[w]) for w in range(windows)]
        + [skip_gain[None]],
        0,
    )
    coefs, rounds = gather_all(packed)
    decay, c_in, c_out = (coefs[i * states : (i + 1) * states] for i in range(3))
    carried = lax.dynamic_slice_in_dim(coefs, (3 + window) * states, states, 0)
    skip = coefs[(3 + windows) * states :]
    gate = c_in * c_out
    fade = jnp.exp(-decay)

    def faded(steps):
        return jnp.exp(-decay * steps)

    inner = out_own.shape[0]
    sent = lax.dynamic_slice_in_dim(out_own, core * (inner // 2), inner // 2, 0)
    across = swap_bit(after(sent, rounds[1]), "mp", 0)
    beside = swap_bit(across, "seq", 0)
    out_far = jnp.where(
        core == 0, jnp.concatenate([across, beside], 0), jnp.concatenate([beside, across], 0)
    )

    unit1, rate1 = norm_parts(tokens)
    normed = after(unit1 * norm1_gain + norm1_bias)
    tail = shift_in_window(normed[rows - CTX :], 1, per_window)
    qkv_rows = project(normed, qkv_weight, 0, 3)
    acc, top, total = by_heads(
        self_kernel,
        [(qkv_rows, rows, 0, i) for i in range(3)],
        [(rows,)] * 3,
    )

    length = float(rows)
    chips = per_window // 2
    chip = block // 2
    (sum_h,) = by_channels(
        summary_kernel,
        [tail, after(normed, acc), decay],
        [states],
    )

    def pair_order(value):
        other = swap_bit(value, "seq", 0)
        return jnp.where(core == 0, value, other), jnp.where(core == 0, other, value)

    first_h, second_h = pair_order(sum_h)
    both_h = faded(length) * first_h + second_h
    far_h = [trade_chips(both_h, d) for d in range(1, chips)]
    (near,) = by_channels(
        near_kernel, [after(tail, sum_h), fade, gate, skip], [CTX]
    )
    far_h = [after(h, near) for h in far_h]
    past_h = jnp.zeros_like(sum_h)
    for d in range(1, chips):
        there = chip ^ d
        gap = jnp.maximum(chip - 1 - there, 0).astype(jnp.float32) * (2.0 * length)
        past_h = past_h + jnp.where(there < chip, faded(gap) * far_h[d - 1], 0.0)
    chip_h = past_h
    past_h = jnp.where(core == 0, past_h, faded(length) * past_h + first_h)

    start_t = jnp.maximum(block * rows - CTX, 0).astype(jnp.float32)
    first = c_out * (c_in * past_h + carried * faded(start_t))

    (context,) = by_channels(
        carry_kernel, [near, first, decay], [CTX]
    )
    kv_ctx = project(context, qkv_weight, 1, 2)
    heads, logs, far = [], [], []
    for part in range(2):
        o, l = by_heads(
            ctx_kernel,
            [(qkv_rows, half, part, 0), (after(kv_ctx, *heads), CTX, 0, 0), (kv_ctx, CTX, 0, 1)]
            + [(a, half, part) for a in (acc, top, total)],
            [(half,)] * 2,
            scalars=(ok,),
        )
        heads.append(o)
        logs.append(l)
        far.append(swap_bit(o, "mp", 0))
    grad_hidden = mm(after(cotangent, *heads), down, NT)
    seen = jnp.concatenate([after(context, *heads), normed], 0)
    outs = jnp.concatenate(heads, 0)
    log = jnp.concatenate(logs, 0)

    hidden, grad_pre = unset((rows, up.shape[1])), unset((rows, up.shape[1]))
    normed2 = unset((rows, width))
    mixed, part2 = [], []
    for part in range(2):
        span = slice(part * half, (part + 1) * half)
        came = after(far[part], part2[0]) if part else after(far[0], seen, outs, log, grad_hidden)
        m = tokens[span] + (mm(heads[part], out_own) + mm(came, out_far))
        n = norm_parts(m)[0] * norm2_gain + norm2_bias
        pre = mm(n, up) + up_bias
        cdf = 0.5 + 0.5 * lax.erf(pre * (0.5**0.5))
        bell = jnp.exp(-0.5 * pre * pre) * (1.0 / math.sqrt(2.0 * math.pi))
        hidden = lax.dynamic_update_slice(hidden, pre * cdf, (part * half, 0))
        slope = grad_hidden[span] * (cdf + pre * bell)
        grad_pre = lax.dynamic_update_slice(grad_pre, slope, (part * half, 0))
        normed2 = lax.dynamic_update_slice(normed2, n, (part * half, 0))
        mixed.append(m)
        if part == 0:
            part2.append(mm(grad_pre[span], up, NT))

    clock = Clock()
    give = mm(core_half(after(hidden, part2[0]), 1 - core), cotangent, TN)
    keep = mm(core_half(after(hidden, give), core), cotangent, TN)
    down_ring = Ring([[keep, swap_bit(give, "seq", 0)]], (1,))
    clock.set(down_ring.held)
    part2.append(mm(clock.hold(grad_pre)[half:], up, NT))
    clock.set(part2[1])
    gots2 = [swap_bit(p, "mp", 0) for p in part2]
    mixed = jnp.concatenate(mixed, 0)
    grad_mixed, grad_heads = unset((rows, width)), []
    gain2, bias2 = 0.0, 0.0

    def norm2_half(part, grad_mixed, gain2, bias2):
        span = slice(part * half, (part + 1) * half)
        grad2 = part2[part] + after(gots2[part], *clock.last)
        unit2, rate2 = norm_parts(after(mixed, grad2)[span])
        gain2 = gain2 + jnp.sum(grad2 * unit2, axis=0)
        bias2 = bias2 + jnp.sum(grad2, axis=0)
        new = cotangent[span] + norm_back(grad2, unit2, rate2, norm2_gain)
        grad_mixed = lax.dynamic_update_slice(grad_mixed, new, (part * half, 0))
        clock.set(grad_mixed, gain2, bias2)
        return grad_mixed, gain2, bias2

    hops = down_ring.count - 1

    def turn(*rings, kept=()):
        rings = [ring for ring in rings if ring.step < 2 * hops]
        for ring in rings[:-1]:
            ring.turn(clock)
        return rings[-1].turn(clock, kept)

    (gots2[0],) = turn(down_ring, kept=(gots2[0],))
    grad_mixed, gain2, bias2 = norm2_half(0, grad_mixed, gain2, bias2)
    give = mm(core_half(clock.hold(normed2), 1 - core), grad_pre, TN)
    clock.set(give)
    turn(down_ring)
    keep = mm(core_half(clock.hold(normed2), core), grad_pre, TN) + swap_bit(give, "seq", 0)
    up_ring = Ring([[keep]], (1,))
    clock.set(up_ring.held)
    (gots2[1],) = turn(down_ring, kept=(gots2[1],))
    grad_mixed, gain2, bias2 = norm2_half(1, grad_mixed, gain2, bias2)
    grad_heads = mm(clock.hold(grad_mixed), out_own, NT)
    clock.set(grad_heads)
    turn(down_ring, up_ring)

    (grads,) = by_heads(
        back_kernel,
        [(qkv_rows, rows, 0, i) for i in range(3)]
        + [(kv_ctx, CTX, 0, i) for i in range(2)]
        + [(a, rows, 0) for a in (outs, log, clock.hold(grad_heads))],
        [(3, CTX + rows)],
        scalars=(ok,),
    )
    clock.set(grads)
    turn(down_ring, up_ring)
    gives = [mm(core_half(clock.hold(seen), 1 - core), grads[i], TN) for i in range(3)]
    gives.append(mm(core_half(clock.hold(grad_mixed), 1 - core), outs, TN))
    gots = [swap_bit(g, "seq", 0) for g in gives]
    clock.set(*gives)
    turn(down_ring, up_ring)
    keeps = [mm(core_half(clock.hold(seen), core), grads[i], TN) + gots[i] for i in range(3)]
    keeps.append(mm(core_half(clock.hold(grad_mixed), core), outs, TN) + gots[3])
    attn_ring = Ring([[k] for k in keeps], (3, 1))
    clock.set(attn_ring.held)
    turn(down_ring, up_ring)

    feed = mm(clock.hold(hidden), down)
    clock.set(feed)
    turn(attn_ring, down_ring, up_ring)
    grad_seen = sum(mm(clock.hold(grads)[i], qkv[i], NT) for i in range(3))
    grad_context = jnp.where(has_ctx, grad_seen[:CTX], 0.0)
    clock.set(grad_seen)
    quarter = rows // 4
    result, grad_tokens = unset((rows, width)), unset((rows, width))

    def across(source, k, into, base):
        span = slice(k * quarter, (k + 1) * quarter)
        got = swap_bit(source[span], "mp", 0)
        (got,) = turn(attn_ring, down_ring, up_ring, kept=(got,))
        return lax.dynamic_update_slice(into, base(span) + (source[span] + got), (k * quarter, 0))

    def result_base(span):
        return mixed[span] + down_bias

    result = across(feed, 0, result, result_base)

    sum_q, sum_r, part_h, part_p, part_skip, grad_tail = by_channels(
        tail_back_kernel,
        [tail, clock.hold(grad_context), fade, gate, skip],
        [states, states, states, states, 1, CTX],
    )
    clock.set(sum_q)
    result = across(feed, 1, result, result_base)
    (sum_p,) = by_channels(moment_kernel, [tail, clock.hold(normed), decay], [states])
    clock.set(sum_p)
    other = swap_bit(jnp.concatenate([sum_p, sum_q], 0), "seq", 0)
    other_p, other_q = other[:states], other[states:]
    first_p, second_p = jnp.where(core == 0, sum_p, other_p), jnp.where(core == 0, other_p, sum_p)
    first_q, second_q = jnp.where(core == 0, sum_q, other_q), jnp.where(core == 0, other_q, sum_q)
    both_p = faded(length) * (first_p + length * first_h) + second_p
    both_q = first_q + faded(length) * second_q
    both = jnp.concatenate([both_p, both_q], 0)
    clock.set(both)
    past_p = jnp.zeros_like(sum_p)
    later = jnp.zeros_like(sum_q)
    came = [trade_chips(both, d) for d in range(1, chips)]
    result = across(feed, 2, result, result_base)
    came[0] = clock.hold(came[0])
    for d in range(1, chips):
        there = chip ^ d
        gap = (jnp.maximum(jnp.abs(chip - there) - 1, 0)).astype(jnp.float32) * (2.0 * length)
        near_p, near_q = came[d - 1][:states], came[d - 1][states:]
        fading = faded(gap)
        past_p = past_p + jnp.where(there < chip, fading * (near_p + gap * far_h[d - 1]), 0.0)
        later = later + jnp.where(there > chip, fading * near_q, 0.0)
    past_p = jnp.where(core == 0, past_p, faded(length) * (past_p + length * chip_h) + first_p)
    later = jnp.where(core == 1, later, second_q + faded(length) * later)
    far_tail, grad_rows = by_channels(
        spread_kernel,
        [gate * later, decay],
        [CTX, rows - CTX],
    )
    to_last = far_tail + grad_tail
    clock.set(to_last)
    from_next = shift_in_window(to_last, -1, per_window)
    result = across(feed, 3, result, result_base)
    along_h = fade * clock.hold(past_h) * sum_q + part_h
    along_p = fade * (past_h * (sum_r + sum_q) + past_p * sum_q) + part_p
    gone = faded(start_t + 1.0)
    part_in = c_out * along_h
    part_out = c_in * along_h + carried * gone * sum_q
    part_decay = -gate * along_p - c_out * carried * gone * ((start_t + 1.0) * sum_q + sum_r)
    clock.set(part_in, part_out, part_decay)

    grad_normed = grad_seen[CTX:] + jnp.concatenate([grad_rows, clock.hold(from_next)], 0)
    part_gain1 = jnp.sum(grad_normed * unit1, axis=0, keepdims=True)
    part_bias1 = jnp.sum(grad_normed, axis=0, keepdims=True)
    part_tokens = norm_back(grad_normed, unit1, rate1, norm1_gain)
    clock.set(part_tokens, part_gain1, part_bias1)
    turn(attn_ring, down_ring, up_ring)
    stacked = jnp.concatenate([part_in, part_out, part_decay, part_skip, part_gain1, part_bias1], 0)
    for k in range(4):
        if k == 1:
            grad_up_bias = jnp.sum(clock.hold(grad_pre), axis=0)
            grad_down_bias = jnp.sum(clock.hold(cotangent), axis=0)
            clock.set(grad_up_bias, grad_down_bias)
        grad_tokens = across(part_tokens, k, grad_tokens, lambda span: grad_mixed[span])

    (stacked_far,) = turn(attn_ring, down_ring, up_ring, kept=(swap_bit(stacked, "mp", 0),))
    while up_ring.step < 2 * hops or down_ring.step < 2 * hops:
        turn(attn_ring, down_ring, up_ring)
    ups = grad_up_bias.reshape(-1, width)
    small = jnp.concatenate(
        [stacked + stacked_far, jnp.stack([gain2, bias2, grad_down_bias]), ups], 0
    )
    todo = [down_ring, up_ring]
    whole = {}
    for bit in range(bits_of(lax.axis_size("seq"))):
        other = swap_bit(small, "seq", bit)
        kept = [other]
        if todo:
            ring = todo.pop(0)
            ring.own[0] = clock.hold(ring.own[0])
            whole[ring] = len(kept)
            kept.append(ring.results()[0])
        if attn_ring.step < 2 * hops:
            other, *made = turn(attn_ring, kept=kept)
        else:
            other, *made = kept
        for ring, at in list(whole.items()):
            if isinstance(at, int):
                whole[ring] = made[at - 1]
        small = small + other
    while attn_ring.step < 2 * hops:
        turn(attn_ring)
    grad_down, grad_up = whole[down_ring][0], whole[up_ring][0]
    grad_qkv, grad_out = attn_ring.results()
    grad_out = jnp.transpose(grad_out[0])

    channels = in_coef.shape[0]
    at = (place_seq * lax.axis_size("mp") + lax.axis_index("mp")) * channels
    own = jnp.transpose(lax.dynamic_slice_in_dim(small[: 3 * states + 1], at, channels, 1))
    grad_in = own[:, :states]
    grad_out_coef = own[:, states : 2 * states]
    grad_decay = own[:, 2 * states : 3 * states]
    grad_skip = own[:, 3 * states]
    small = small[3 * states + 1 :]
    return (
        result,
        grad_tokens,
        small[0],
        small[1],
        grad_in,
        grad_out_coef,
        grad_decay,
        grad_skip,
        grad_qkv,
        grad_out,
        small[2],
        small[3],
        grad_up,
        small[5:].reshape(-1),
        grad_down,
        small[4],
    )


def solution(mesh):
    owner = P(("seq", "mp"), None)
    return jax.shard_map(
        per_device,
        mesh=mesh,
        in_specs=(
            P("seq", None),
            P(None, ("seq", "mp"), None),
            P(),
            P(),
            owner,
            owner,
            owner,
            P(("seq", "mp")),
            P(None, None, "mp"),
            P("mp", None),
            P(),
            P(),
            P(None, "mp"),
            P("mp"),
            P("mp", None),
            P(),
            P("seq", None),
        ),
        out_specs=(
            P("seq", None),
            P("seq", None),
            P(),
            P(),
            owner,
            owner,
            owner,
            P(("seq", "mp")),
            P(None, None, "mp"),
            P("mp", None),
            P(),
            P(),
            P(None, "mp"),
            P("mp"),
            P("mp", None),
            P(),
        ),
        check_vma=False,
    )
```

```python
import functools
import math

import jax
import jax.numpy as jnp
from jax import lax
from jax.experimental import pallas as pl
from jax.experimental.pallas import tpu as pltpu
from jax.sharding import PartitionSpec as P

HDIM = 128
BLOCK = 512
CTX = 128
LEN = 4096
EPS = 1e-05
HIGH = lax.Precision.HIGH


def mm(left, right, dims=((1,), (0,))):
    return lax.dot_general(
        left, right, (dims, ((), ())), precision=HIGH, preferred_element_type=jnp.float32
    )


def norm_parts(value):
    center = value - jnp.mean(value, axis=-1, keepdims=True)
    spread = jnp.mean(center * center, axis=-1, keepdims=True)
    rate = lax.rsqrt(spread + EPS)
    return center * rate, rate


def norm_back(grad, unit, rate, gain):
    scaled = grad * gain
    inner = jnp.mean(scaled * unit, axis=-1, keepdims=True)
    return rate * (scaled - jnp.mean(scaled, axis=-1, keepdims=True) - unit * inner)


def swap_bit(value, axis, bit):
    size = lax.axis_size(axis)
    return lax.ppermute(value, axis, [(i, i ^ (1 << bit)) for i in range(size)])


def bits_of(count):
    return count.bit_length() - 1


def shift_in_window(value, distance, per_window):
    size = lax.axis_size("seq")
    route = [(i, i + distance) for i in range(size)]
    inside = [(a, b) for a, b in route if 0 <= b < size and a // per_window == b // per_window]
    return lax.ppermute(value, "seq", inside)


def after(value, *others):
    return lax.optimization_barrier((value,) + others)[0]


def gather_all(piece, gates=()):
    mp_size, seq_size = lax.axis_size("mp"), lax.axis_size("seq")
    me = lax.axis_index("seq") * mp_size + lax.axis_index("mp")
    block, seen = piece, []
    for bit in range(bits_of(mp_size * seq_size)):
        axis, own = ("mp", bit) if bit < bits_of(mp_size) else ("seq", bit - bits_of(mp_size))
        if gates:
            block = after(block, gates[bit])
        other = swap_bit(block, axis, own)
        upper = (me >> bit) & 1
        block = jnp.where(
            upper == 1, jnp.concatenate([other, block], 1), jnp.concatenate([block, other], 1)
        )
        seen.append(block)
    return block, seen


def trade_chips(value, distance):
    size = lax.axis_size("seq")
    return lax.ppermute(value, "seq", [(i, i ^ (2 * distance)) for i in range(size)])


def chip_order(count):
    if count <= 2:
        return list(range(count))
    return list(range(0, count, 2)) + list(range(count - 1 - count % 2, 0, -2))


def ring_route(count):
    order = chip_order(count)
    route = []
    for i in range(count):
        here, there = order[i], order[(i + 1) % count]
        route.append((2 * here, 2 * there))
        route.append((2 * there + 1, 2 * here + 1))
    return route


def ring_spot():
    count = lax.axis_size("seq") // 2
    places = [0] * count
    for i, chip in enumerate(chip_order(count)):
        places[chip] = i
    me = lax.axis_index("seq")
    here = jnp.array(places, jnp.int32)[me // 2]
    return jnp.where(me % 2 == 0, here, (count - here) % count)


def unset(shape):
    return pl.pallas_call(
        lambda out: None,
        out_shape=jax.ShapeDtypeStruct(shape, jnp.float32),
        out_specs=pl.BlockSpec(memory_space=pl.ANY),
        compiler_params=pltpu.CompilerParams(vmem_limit_bytes=1 << 20),
    )()


def pack_kernel(*refs):
    low = 0
    for ref in refs[:-1]:
        refs[-1][low : low + ref.shape[0], :] = ref[...]
        low += ref.shape[0]


def pack(parts):
    rows, cols = sum(part.shape[0] for part in parts), parts[0].shape[1]
    return pl.pallas_call(
        pack_kernel,
        out_shape=jax.ShapeDtypeStruct((rows, cols), jnp.float32),
        compiler_params=pltpu.CompilerParams(vmem_limit_bytes=1 << 20),
    )(*parts)


def pick(value, index):
    return lax.dynamic_index_in_dim(value, index, 0, keepdims=False)


class Clock:
    def __init__(self):
        self.last = ()

    def hold(self, value):
        return after(value, *self.last) if self.last else value

    def set(self, *values):
        self.last = values


def assemble_kernel(count, cuts, where_ref, *refs):
    parts, outs, sems = refs[: 2 * count], refs[2 * count : -1], refs[-1]
    copies = []
    for n in range(2 * count):
        which, spot = where_ref[0, n], where_ref[1, n]
        for out, (low, high) in zip(outs, cuts):
            copies.append(
                pltpu.make_async_copy(
                    parts[n].at[low:high], out.at[:, which, spot], sems.at[len(copies)]
                )
            )
    for copy in copies:
        copy.start()
    for copy in copies:
        copy.wait()


class Ring:
    def __init__(self, pieces, outs):
        self.count = lax.axis_size("seq") // 2
        self.place, self.route = ring_spot(), ring_route(self.count)
        self.core = lax.axis_index("seq") % 2
        self.mirror = (self.count - self.place) % self.count
        self.rows, self.cols = pieces[0][0].shape[0] // self.count, pieces[0][0].shape[1]
        self.pieces = [
            [a.reshape(self.count, self.rows, self.cols) for a in addends] for addends in pieces
        ]
        self.outs = outs
        self.step, self.own, self.far, self.extras = 0, [], [], []
        self.held = self.chunk(self.place)

    def chunk(self, spot):
        return jnp.stack([sum(pick(a, spot) for a in addends) for addends in self.pieces])

    def take(self, extra):
        self.extras = [extra]
        self.held = jnp.concatenate([self.held, extra], 0)

    def extra_sum(self):
        count = self.count
        seen = jnp.stack(self.extras)
        return sum(
            lax.dynamic_index_in_dim(seen, (self.place - i + count) % count, 0, keepdims=False)
            for i in range(count)
        )

    def turn(self, clock, kept=()):
        got = lax.ppermute(self.held, "seq", self.route)
        got, *kept = lax.optimization_barrier((got, *kept, *clock.last))[: 1 + len(kept)]
        self.step += 1
        if self.step < self.count:
            got = got + self.chunk((self.place + 2 * self.count - self.step) % self.count)
        self.held = got
        if self.step >= self.count - 1:
            self.own.append(got)
            self.far.append(swap_bit(got, "seq", 0))
        if self.extras:
            self.extras.append(got[-self.extras[0].shape[0] :])
        clock.set(got)
        return kept

    def results(self):
        count = self.count
        hops = jnp.arange(count, dtype=jnp.int32)
        spots = jnp.concatenate([self.place + 1 - hops, self.mirror + 1 - hops]) + count
        which = jnp.repeat(jnp.stack([self.core, 1 - self.core]), count)
        where = jnp.stack([which, spots % count]).astype(jnp.int32)
        cuts, low = [], 0
        for size in self.outs:
            cuts.append((low, low + size))
            low += size
        shapes = [(size, 2, count, self.rows, self.cols) for size in self.outs]
        outs = pl.pallas_call(
            functools.partial(assemble_kernel, count, cuts),
            in_specs=[pl.BlockSpec(memory_space=pltpu.SMEM)]
            + [pl.BlockSpec(memory_space=pltpu.VMEM)] * (2 * count),
            out_specs=[pl.BlockSpec(memory_space=pl.ANY)] * len(shapes),
            out_shape=[jax.ShapeDtypeStruct(shape, jnp.float32) for shape in shapes],
            scratch_shapes=[pltpu.SemaphoreType.DMA((2 * count * len(shapes),))],
            cost_estimate=pl.CostEstimate(flops=0, bytes_accessed=COST, transcendentals=0),
        )(where, *self.own, *self.far)
        return [out.reshape(out.shape[0], -1, self.cols) for out in outs]


def core_half(value, which):
    size = value.shape[1] // 2
    return lax.dynamic_slice_in_dim(value, which * size, size, 1)


def rows8(shape):
    return lax.broadcasted_iota(jnp.int32, shape, 0).astype(jnp.float32)


def tree(values):
    values = list(values)
    while len(values) > 1:
        values = [sum(values[i : i + 2]) for i in range(0, len(values), 2)]
    return values[0]


def groups(decay_ref):
    states, lanes = decay_ref.shape
    for low in range(0, lanes, 128):
        span = slice(low, low + 128)
        rates = [jnp.broadcast_to(decay_ref[n : n + 1, span], (8, 128)) for n in range(states)]
        yield span, rates, [jnp.exp(-8.0 * rate) for rate in rates]


UNROLL = 4


def over_rows(ref, count, span, body, carry):
    def step(i, carry):
        for k in range(UNROLL):
            base = pl.multiple_of((i * UNROLL + k) * 8, 8)
            carry = body(ref[pl.ds(base, 8), span], carry)
        return carry

    return lax.fori_loop(0, count // (8 * UNROLL), step, carry)


def summary_kernel(tail_ref, x_ref, decay_ref, h_ref):
    for span, rates, jump in groups(decay_ref):

        def body(tile, acc):
            return tuple(j * a + tile for j, a in zip(jump, acc))

        acc = (tail_ref[:8, span] * 0.0,) * len(rates)
        acc = over_rows(tail_ref, tail_ref.shape[0], span, body, acc)
        acc = over_rows(x_ref, x_ref.shape[0] - tail_ref.shape[0], span, body, acc)
        left = 7.0 - rows8((8, 128))
        for n, rate in enumerate(rates):
            h_ref[n : n + 1, span] = jnp.sum(acc[n] * jnp.exp(-rate * left), axis=0, keepdims=True)


def moment_kernel(tail_ref, x_ref, decay_ref, p_ref):
    for span, rates, jump in groups(decay_ref):

        def body(tile, carry):
            acc, lag = carry
            lag = tuple(j * (b + a) for j, a, b in zip(jump, acc, lag))
            return tuple(j * a + tile for j, a in zip(jump, acc)), lag

        zeros = (tail_ref[:8, span] * 0.0,) * len(rates)
        carry = over_rows(tail_ref, tail_ref.shape[0], span, body, (zeros, zeros))
        acc, lag = over_rows(x_ref, x_ref.shape[0] - tail_ref.shape[0], span, body, carry)
        left = 7.0 - rows8((8, 128))
        for n, rate in enumerate(rates):
            total = (8.0 * lag[n] + left * acc[n]) * jnp.exp(-rate * left)
            p_ref[n : n + 1, span] = jnp.sum(total, axis=0, keepdims=True)


def carry_kernel(near_ref, first_ref, decay_ref, y_ref):
    for span, rates, jump in groups(decay_ref):
        ahead = rows8((8, 128)) + 1.0
        modes = tuple(
            jnp.broadcast_to(first_ref[n : n + 1, span], (8, 128)) * jnp.exp(-rate * ahead)
            for n, rate in enumerate(rates)
        )

        def step(i, modes):
            for k in range(UNROLL):
                base = pl.multiple_of((i * UNROLL + k) * 8, 8)
                y_ref[pl.ds(base, 8), span] = near_ref[pl.ds(base, 8), span] + tree(modes)
                modes = tuple(j * m for j, m in zip(jump, modes))
            return modes

        lax.fori_loop(0, y_ref.shape[0] // (8 * UNROLL), step, modes)


def spread_kernel(first_ref, decay_ref, tail_ref, y_ref):
    for span, rates, jump in groups(decay_ref):
        ahead = 8.0 - rows8((8, 128))
        modes = tuple(
            jnp.broadcast_to(first_ref[n : n + 1, span], (8, 128)) * jnp.exp(-rate * ahead)
            for n, rate in enumerate(rates)
        )

        def run(ref, modes):
            count = ref.shape[0] // 8

            def step(i, modes):
                for k in range(UNROLL):
                    base = pl.multiple_of((count - 1 - i * UNROLL - k) * 8, 8)
                    ref[pl.ds(base, 8), span] = tree(modes)
                    modes = tuple(j * m for j, m in zip(jump, modes))
                return modes

            return lax.fori_loop(0, count // UNROLL, step, modes)

        run(tail_ref, run(y_ref, modes))


def near_kernel(x_ref, fade_ref, gate_ref, skip_ref, y_ref):
    fade, gate, skip = fade_ref[...], gate_ref[...], skip_ref[...]

    def octet(i, u):
        base = pl.multiple_of(i * 8, 8)
        tile = x_ref[pl.ds(base, 8), :]
        rows = []
        for r in range(8):
            row = tile[r : r + 1, :]
            u = fade * u + gate * jnp.broadcast_to(row, fade.shape)
            rows.append(jnp.sum(u, axis=0, keepdims=True) + skip * row)
        y_ref[pl.ds(base, 8), :] = jnp.concatenate(rows, 0)
        return u

    lax.fori_loop(0, x_ref.shape[0] // 8, octet, jnp.zeros(fade.shape, jnp.float32))


def tail_back_kernel(
    x_ref, d_ref, fade_ref, gate_ref, skip_ref, q_ref, r_ref, dh_ref, dp_ref, dskip_ref, dx_ref
):
    fade, gate, skip = fade_ref[...], gate_ref[...], skip_ref[...]
    octets = x_ref.shape[0] // 8
    zero = jnp.zeros(fade.shape, jnp.float32)

    def forward(i, carry):
        h, p, dh, dp = carry
        base = pl.multiple_of(i * 8, 8)
        tile, grads = x_ref[pl.ds(base, 8), :], d_ref[pl.ds(base, 8), :]
        for r in range(8):
            p = fade * (p + h)
            h = fade * h + jnp.broadcast_to(tile[r : r + 1, :], fade.shape)
            grad = jnp.broadcast_to(grads[r : r + 1, :], fade.shape)
            dh = dh + grad * h
            dp = dp + grad * p
        return h, p, dh, dp

    _, _, dh, dp = lax.fori_loop(0, octets, forward, (zero, zero, zero, zero))
    dh_ref[...] = dh
    dp_ref[...] = dp
    dskip_ref[...] = jnp.sum(x_ref[...] * d_ref[...], axis=0, keepdims=True)

    def backward(k, carry):
        q, r_sum = carry
        base = pl.multiple_of((octets - 1 - k) * 8, 8)
        grads = d_ref[pl.ds(base, 8), :]
        rows = [None] * 8
        for r in reversed(range(8)):
            r_sum = fade * (r_sum + q)
            grad = grads[r : r + 1, :]
            q = fade * q + jnp.broadcast_to(grad, fade.shape)
            rows[r] = jnp.sum(gate * q, axis=0, keepdims=True) + skip * grad
        dx_ref[pl.ds(base, 8), :] = jnp.concatenate(rows, 0)
        return q, r_sum

    q, r_sum = lax.fori_loop(0, octets, backward, (zero, zero))
    q_ref[...] = q
    r_ref[...] = r_sum


def by_channels(kernel, ins, outs, cut=512):
    width = ins[0].shape[1]
    cut = cut if width % cut == 0 else width

    def spec(rows):
        return pl.BlockSpec((rows, cut), lambda i: (0, i))

    return pl.pallas_call(
        kernel,
        grid=(width // cut,),
        in_specs=[spec(a.shape[0]) for a in ins],
        out_specs=[spec(r) for r in outs],
        out_shape=[jax.ShapeDtypeStruct((r, width), jnp.float32) for r in outs],
        cost_estimate=pl.CostEstimate(flops=0, bytes_accessed=COST, transcendentals=0),
        compiler_params=pltpu.CompilerParams(vmem_limit_bytes=12 << 20),
    )(*ins)


def cut(value):
    top = value.astype(jnp.bfloat16)
    return top, (value - top.astype(jnp.float32)).astype(jnp.bfloat16)


def dot3(left, right, dims):
    def one(a, b):
        return lax.dot_general(a, b, (dims, ((), ())), preferred_element_type=jnp.float32)

    return one(left[0], right[1]) + one(left[1], right[0]) + one(left[0], right[0])


NT = ((1,), (1,))
NN = ((1,), (0,))
TN = ((0,), (0,))
TILE = 256
COST = 1024
SCALE = HDIM ** (-0.5)


def causal(shape, first_row):
    row = lax.broadcasted_iota(jnp.int32, shape, 0) + first_row
    return lax.broadcasted_iota(jnp.int32, shape, 1) <= row


def self_kernel(q_ref, k_ref, v_ref, acc_ref, top_ref):
    rows = q_ref.shape[0]
    k, v = cut(k_ref[...]), cut(v_ref[...])
    for first in range(0, rows, TILE):
        span = slice(first, first + TILE)
        seen = first + TILE
        q = cut(q_ref[span, :] * SCALE)
        scores = dot3(q, (k[0][:seen], k[1][:seen]), NT)
        scores = jnp.where(causal(scores.shape, first), scores, -1e30)
        top = jnp.max(scores, axis=1, keepdims=True)
        weight = jnp.exp(scores - top)
        acc_ref[span, :] = dot3(cut(weight), (v[0][:seen], v[1][:seen]), NN)
        total = jnp.sum(weight, axis=1, keepdims=True)
        lane = lax.broadcasted_iota(jnp.int32, (TILE, HDIM), 1)
        top_ref[span, :] = jnp.where(lane < HDIM // 2, top, total)


def ctx_kernel(ok_ref, q_ref, k_ref, v_ref, acc_ref, top_ref, out_ref, log_ref):
    ok = ok_ref[0] > 0
    q = cut(q_ref[...] * SCALE)
    scores = dot3(q, cut(k_ref[...]), NT)
    scores = jnp.where(ok, scores, -1e30)
    near, near_sum = top_ref[:, :1], top_ref[:, HDIM // 2 : HDIM // 2 + 1]
    top = jnp.maximum(near, jnp.max(scores, axis=1, keepdims=True))
    weight = jnp.where(ok, jnp.exp(scores - top), 0.0)
    ease = jnp.exp(near - top)
    total = near_sum * ease + jnp.sum(weight, axis=1, keepdims=True)
    out_ref[...] = (acc_ref[...] * ease + dot3(cut(weight), cut(v_ref[...]), NN)) / total
    log_ref[...] = jnp.broadcast_to(top + jnp.log(total), log_ref.shape)


def back_kernel(ok_ref, q_ref, k_ref, v_ref, kc_ref, vc_ref, o_ref, l_ref, g_ref, d_ref):
    ok = ok_ref[0] > 0
    rows = q_ref.shape[0]
    k, v, kc, vc = cut(k_ref[...]), cut(v_ref[...]), cut(kc_ref[...]), cut(vc_ref[...])
    d_ref[0, :CTX, :] = jnp.zeros((CTX, HDIM), jnp.float32)
    for first in reversed(range(0, rows, TILE)):
        seen = first + TILE
        span = slice(first, seen)
        grad = g_ref[span, :]
        q = cut(q_ref[span, :] * SCALE)
        grad2 = cut(grad)
        inner = jnp.sum(grad * o_ref[span, :], axis=1, keepdims=True)
        mark = l_ref[span, :][:, :1]
        ks, vs = (k[0][:seen], k[1][:seen]), (v[0][:seen], v[1][:seen])
        probs = dot3(q, ks, NT)
        probs = jnp.where(causal(probs.shape, first), jnp.exp(probs - mark), 0.0)
        probs_c = jnp.where(ok, jnp.exp(dot3(q, kc, NT) - mark), 0.0)
        ds = cut(probs * (dot3(grad2, vs, NT) - inner))
        ds_c = cut(probs_c * (dot3(grad2, vc, NT) - inner))
        probs, probs_c = cut(probs), cut(probs_c)
        d_ref[0, CTX + first : CTX + seen, :] = (dot3(ds, ks, NN) + dot3(ds_c, kc, NN)) * SCALE
        for at, (own, ctx, other) in enumerate([(ds, ds_c, q), (probs, probs_c, grad2)]):
            near, back = dot3(own, other, TN), dot3(ctx, other, TN)
            if seen == rows:
                d_ref[1 + at, CTX:, :] = near
                d_ref[1 + at, :CTX, :] = back
            else:
                d_ref[1 + at, CTX : CTX + seen, :] += near
                d_ref[1 + at, :CTX, :] += back


def by_heads(kernel, ins, outs, scalars=()):
    heads = ins[0][0].shape[-1] // HDIM
    specs = [pl.BlockSpec(memory_space=pltpu.SMEM) for _ in scalars]
    for _, rows, *at in ins:
        if len(at) == 2:
            specs.append(pl.BlockSpec((None, rows, HDIM), lambda h, at=at: (at[1], at[0], h)))
        else:
            specs.append(pl.BlockSpec((rows, HDIM), lambda h, at=at: (at[0], h)))
    return pl.pallas_call(
        kernel,
        grid=(heads,),
        in_specs=specs,
        out_specs=[
            pl.BlockSpec(lead + (HDIM,), lambda h, n=len(lead): (0,) * n + (h,)) for lead in outs
        ],
        out_shape=[jax.ShapeDtypeStruct(lead + (heads * HDIM,), jnp.float32) for lead in outs],
        cost_estimate=pl.CostEstimate(flops=0, bytes_accessed=COST, transcendentals=0),
        compiler_params=pltpu.CompilerParams(vmem_limit_bytes=16 << 20),
    )(*scalars, *[a[0] for a in ins])


def project_kernel(x_ref, w_ref, out_ref, high_ref, low_ref):
    @pl.when(pl.program_id(0) == 0)
    def _():
        high_ref[...], low_ref[...] = cut(x_ref[...])

    def one(part):
        return lax.dot_general(
            part, w_ref[...], (NN, ((), ())), preferred_element_type=jnp.float32
        )

    out_ref[...] = one(low_ref[...]) + one(high_ref[...])


def project(x, weights, first, count):
    rows, depth = x.shape
    width = weights.shape[2]
    return pl.pallas_call(
        project_kernel,
        grid=(count,),
        in_specs=[
            pl.BlockSpec((rows, depth), lambda i: (0, 0)),
            pl.BlockSpec((None, depth, width), lambda i: (first + i, 0, 0)),
        ],
        out_specs=pl.BlockSpec((None, rows, width), lambda i: (i, 0, 0)),
        out_shape=jax.ShapeDtypeStruct((count, rows, width), jnp.float32),
        scratch_shapes=[pltpu.VMEM((rows, depth), jnp.bfloat16)] * 2,
        cost_estimate=pl.CostEstimate(flops=0, bytes_accessed=COST, transcendentals=0),
        compiler_params=pltpu.CompilerParams(vmem_limit_bytes=16 << 20),
    )(x, weights)


def per_device(
    tokens,
    window_state,
    norm1_gain,
    norm1_bias,
    in_coef,
    out_coef,
    decay_rate,
    skip_gain,
    qkv_weight,
    out_weight,
    norm2_gain,
    norm2_bias,
    up_weight,
    up_bias,
    down_weight,
    down_bias,
    cotangent,
):
    place_seq = lax.axis_index("seq")
    core = place_seq % 2
    rows, width = tokens.shape
    states = in_coef.shape[1]
    windows = window_state.shape[0]
    per_window = LEN // rows
    block = place_seq % per_window
    window = place_seq // per_window
    has_ctx = block > 0
    ok = has_ctx.astype(jnp.int32).reshape(1)
    half = rows // 2

    qkv = qkv_weight.astype(jnp.float32)
    out_own = out_weight.astype(jnp.float32)
    up = up_weight.astype(jnp.float32)
    down = down_weight.astype(jnp.float32)

    coefs, rounds = gather_all(
        pack(
            [jnp.transpose(a) for a in (decay_rate, in_coef, out_coef)]
            + [jnp.transpose(window_state[w]) for w in range(windows)]
            + [skip_gain[None]]
        )
    )
    decay, c_in, c_out = (coefs[i * states : (i + 1) * states] for i in range(3))
    carried = lax.dynamic_slice_in_dim(coefs, (3 + window) * states, states, 0)
    skip = coefs[(3 + windows) * states :]
    gate = c_in * c_out
    fade = jnp.exp(-decay)

    def faded(steps):
        return jnp.exp(-decay * steps)

    inner = out_own.shape[0]
    sent = pick(out_weight.reshape(2, inner // 2, width), core).astype(jnp.float32)
    across = swap_bit(after(sent, rounds[1]), "mp", 0)
    beside = swap_bit(across, "seq", 0)
    out_far = jnp.where(
        core == 0, jnp.concatenate([across, beside], 0), jnp.concatenate([beside, across], 0)
    )

    unit1, rate1 = norm_parts(tokens)
    normed = after(unit1 * norm1_gain + norm1_bias)
    tail = shift_in_window(normed[rows - CTX :], 1, per_window)
    qkv_rows = project(normed, qkv_weight, 0, 3)
    acc, top = by_heads(
        self_kernel,
        [(qkv_rows, rows, 0, i) for i in range(3)],
        [(rows,)] * 2,
    )

    length = float(rows)
    chips = per_window // 2
    chip = block // 2
    (sum_h,) = by_channels(
        summary_kernel,
        [tail, after(normed, acc), decay],
        [states],
    )

    def pair_order(value):
        other = swap_bit(value, "seq", 0)
        return jnp.where(core == 0, value, other), jnp.where(core == 0, other, value)

    first_h, second_h = pair_order(sum_h)
    both_h = faded(length) * first_h + second_h
    far_h = [trade_chips(both_h, d) for d in range(1, chips)]
    (near,) = by_channels(
        near_kernel, [after(tail, sum_h), fade, gate, skip], [CTX]
    )
    far_h = [after(h, near) for h in far_h]
    past_h = jnp.zeros_like(sum_h)
    for d in range(1, chips):
        there = chip ^ d
        gap = jnp.maximum(chip - 1 - there, 0).astype(jnp.float32) * (2.0 * length)
        past_h = past_h + jnp.where(there < chip, faded(gap) * far_h[d - 1], 0.0)
    chip_h = past_h
    past_h = jnp.where(core == 0, past_h, faded(length) * past_h + first_h)

    start_t = jnp.maximum(block * rows - CTX, 0).astype(jnp.float32)
    first = c_out * (c_in * past_h + carried * faded(start_t))

    (context,) = by_channels(
        carry_kernel, [near, first, decay], [CTX]
    )
    kv_ctx = project(context, qkv_weight, 1, 2)
    heads, logs, far = [], [], []
    for part in range(2):
        o, l = by_heads(
            ctx_kernel,
            [(qkv_rows, half, part, 0), (after(kv_ctx, *heads), CTX, 0, 0), (kv_ctx, CTX, 0, 1)]
            + [(a, half, part) for a in (acc, top)],
            [(half,)] * 2,
            scalars=(ok,),
        )
        heads.append(o)
        logs.append(l)
        far.append(swap_bit(o, "mp", 0))
    grad_hidden = mm(after(cotangent, *heads), down, NT)
    seen = jnp.concatenate([after(context, *heads), normed], 0)
    outs = jnp.concatenate(heads, 0)
    log = jnp.concatenate(logs, 0)

    hidden, grad_pre = unset((rows, up.shape[1])), unset((rows, up.shape[1]))
    normed2 = unset((rows, width))
    mixed, part2 = [], []
    for part in range(2):
        span = slice(part * half, (part + 1) * half)
        came = after(far[part], part2[0]) if part else after(far[0], seen, outs, log, grad_hidden)
        m = tokens[span] + (mm(heads[part], out_own) + mm(came, out_far))
        n = norm_parts(m)[0] * norm2_gain + norm2_bias
        pre = mm(n, up) + up_bias
        cdf = 0.5 + 0.5 * lax.erf(pre * (0.5**0.5))
        bell = jnp.exp(-0.5 * pre * pre) * (1.0 / math.sqrt(2.0 * math.pi))
        hidden = lax.dynamic_update_slice(hidden, pre * cdf, (part * half, 0))
        slope = grad_hidden[span] * (cdf + pre * bell)
        grad_pre = lax.dynamic_update_slice(grad_pre, slope, (part * half, 0))
        normed2 = lax.dynamic_update_slice(normed2, n, (part * half, 0))
        mixed.append(m)
        if part == 0:
            part2.append(mm(grad_pre[span], up, NT))

    clock = Clock()
    give = mm(core_half(after(hidden, part2[0]), 1 - core), cotangent, TN)
    keep = mm(core_half(after(hidden, give), core), cotangent, TN)
    down_ring = Ring([[keep, swap_bit(give, "seq", 0)]], (1,))
    clock.set(down_ring.held)
    part2.append(mm(clock.hold(grad_pre)[half:], up, NT))
    clock.set(part2[1])
    gots2 = [swap_bit(p, "mp", 0) for p in part2]
    mixed = jnp.concatenate(mixed, 0)
    grad_mixed, grad_heads = unset((rows, width)), []
    gain2, bias2 = 0.0, 0.0

    def norm2_half(part, grad_mixed, gain2, bias2):
        span = slice(part * half, (part + 1) * half)
        grad2 = part2[part] + after(gots2[part], *clock.last)
        unit2, rate2 = norm_parts(after(mixed, grad2)[span])
        gain2 = gain2 + jnp.sum(grad2 * unit2, axis=0)
        bias2 = bias2 + jnp.sum(grad2, axis=0)
        new = cotangent[span] + norm_back(grad2, unit2, rate2, norm2_gain)
        grad_mixed = lax.dynamic_update_slice(grad_mixed, new, (part * half, 0))
        clock.set(grad_mixed, gain2, bias2)
        return grad_mixed, gain2, bias2

    hops = down_ring.count - 1

    def turn(*rings, kept=()):
        rings = [ring for ring in rings if ring.step < 2 * hops]
        for ring in rings[:-1]:
            ring.turn(clock)
        return rings[-1].turn(clock, kept)

    (gots2[0],) = turn(down_ring, kept=(gots2[0],))
    grad_mixed, gain2, bias2 = norm2_half(0, grad_mixed, gain2, bias2)
    give = mm(core_half(clock.hold(normed2), 1 - core), grad_pre, TN)
    clock.set(give)
    turn(down_ring)
    keep = mm(core_half(clock.hold(normed2), core), grad_pre, TN) + swap_bit(give, "seq", 0)
    up_ring = Ring([[keep]], (1,))
    clock.set(up_ring.held)
    (gots2[1],) = turn(down_ring, kept=(gots2[1],))
    grad_mixed, gain2, bias2 = norm2_half(1, grad_mixed, gain2, bias2)
    grad_heads = mm(clock.hold(grad_mixed), out_own, NT)
    clock.set(grad_heads)
    turn(down_ring, up_ring)

    (grads,) = by_heads(
        back_kernel,
        [(qkv_rows, rows, 0, i) for i in range(3)]
        + [(kv_ctx, CTX, 0, i) for i in range(2)]
        + [(a, rows, 0) for a in (outs, log, clock.hold(grad_heads))],
        [(3, CTX + rows)],
        scalars=(ok,),
    )
    clock.set(grads)
    turn(down_ring, up_ring)
    gives = [mm(core_half(clock.hold(seen), 1 - core), grads[i], TN) for i in range(3)]
    gives.append(mm(core_half(clock.hold(grad_mixed), 1 - core), outs, TN))
    gots = [swap_bit(g, "seq", 0) for g in gives]
    clock.set(*gives)
    turn(down_ring, up_ring)
    keeps = [mm(core_half(clock.hold(seen), core), grads[i], TN) + gots[i] for i in range(3)]
    keeps.append(mm(core_half(clock.hold(grad_mixed), core), outs, TN) + gots[3])
    attn_ring = Ring([[k] for k in keeps], (3, 1))
    clock.set(attn_ring.held)
    turn(down_ring, up_ring)

    feed = mm(clock.hold(hidden), down)
    clock.set(feed)
    turn(attn_ring, down_ring, up_ring)
    grad_seen = sum(mm(clock.hold(grads)[i], qkv[i], NT) for i in range(3))
    grad_context = jnp.where(has_ctx, grad_seen[:CTX], 0.0)
    clock.set(grad_seen)
    quarter = rows // 4
    result, grad_tokens = unset((rows, width)), unset((rows, width))

    def across(source, k, into, base, kept=()):
        span = slice(k * quarter, (k + 1) * quarter)
        got = swap_bit(source[span], "mp", 0)
        got, into, *kept = turn(attn_ring, down_ring, up_ring, kept=(got, into, *kept))
        new = base(span) + (source[span] + got)
        return [lax.dynamic_update_slice(into, new, (k * quarter, 0)), *kept]

    def result_base(span):
        return mixed[span] + down_bias

    (result,) = across(feed, 0, result, result_base)

    sum_q, sum_r, part_h, part_p, part_skip, grad_tail = by_channels(
        tail_back_kernel,
        [tail, clock.hold(grad_context), fade, gate, skip],
        [states, states, states, states, 1, CTX],
    )
    clock.set(sum_q)
    (result,) = across(feed, 1, result, result_base)
    (sum_p,) = by_channels(moment_kernel, [tail, clock.hold(normed), decay], [states])
    clock.set(sum_p)
    other = swap_bit(jnp.concatenate([sum_p, sum_q], 0), "seq", 0)
    other_p, other_q = other[:states], other[states:]
    first_p, second_p = jnp.where(core == 0, sum_p, other_p), jnp.where(core == 0, other_p, sum_p)
    first_q, second_q = jnp.where(core == 0, sum_q, other_q), jnp.where(core == 0, other_q, sum_q)
    both_p = faded(length) * (first_p + length * first_h) + second_p
    both_q = first_q + faded(length) * second_q
    both = jnp.concatenate([both_p, both_q], 0)
    clock.set(both)
    past_p = jnp.zeros_like(sum_p)
    later = jnp.zeros_like(sum_q)
    came = [trade_chips(both, d) for d in range(1, chips)]
    (result,) = across(feed, 2, result, result_base)
    came[0] = clock.hold(came[0])
    for d in range(1, chips):
        there = chip ^ d
        gap = (jnp.maximum(jnp.abs(chip - there) - 1, 0)).astype(jnp.float32) * (2.0 * length)
        near_p, near_q = came[d - 1][:states], came[d - 1][states:]
        fading = faded(gap)
        past_p = past_p + jnp.where(there < chip, fading * (near_p + gap * far_h[d - 1]), 0.0)
        later = later + jnp.where(there > chip, fading * near_q, 0.0)
    past_p = jnp.where(core == 0, past_p, faded(length) * (past_p + length * chip_h) + first_p)
    later = jnp.where(core == 1, later, second_q + faded(length) * later)
    far_tail, grad_rows = by_channels(
        spread_kernel,
        [gate * later, decay],
        [CTX, rows - CTX],
    )
    to_last = far_tail + grad_tail
    clock.set(to_last)
    from_next = shift_in_window(to_last, -1, per_window)
    (result,) = across(feed, 3, result, result_base)
    along_h = fade * clock.hold(past_h) * sum_q + part_h
    along_p = fade * (past_h * (sum_r + sum_q) + past_p * sum_q) + part_p
    gone = faded(start_t + 1.0)
    part_in = c_out * along_h
    part_out = c_in * along_h + carried * gone * sum_q
    part_decay = -gate * along_p - c_out * carried * gone * ((start_t + 1.0) * sum_q + sum_r)
    clock.set(part_in, part_out, part_decay)

    grad_normed = grad_seen[CTX:] + jnp.concatenate([grad_rows, clock.hold(from_next)], 0)
    part_gain1 = jnp.sum(grad_normed * unit1, axis=0, keepdims=True)
    part_bias1 = jnp.sum(grad_normed, axis=0, keepdims=True)
    part_tokens = norm_back(grad_normed, unit1, rate1, norm1_gain)
    clock.set(part_tokens, part_gain1, part_bias1)
    turn(attn_ring, down_ring, up_ring)
    stacked = jnp.concatenate([part_in, part_out, part_decay, part_skip, part_gain1, part_bias1], 0)
    whole = {}

    def gather_done():
        made = []
        for ring in (down_ring, up_ring):
            if ring.step == 2 * hops and ring not in whole:
                ring.own[0] = clock.hold(ring.own[0])
                whole[ring] = ring.results()[0]
                made.append(ring)
        return made

    def tokens_turn(k, grad_tokens, *kept):
        made = gather_done()
        kept = [*kept, *[whole[ring] for ring in made]]
        if k < 4:
            grad_tokens, *kept = across(
                part_tokens, k, grad_tokens, lambda span: grad_mixed[span], kept
            )
        else:
            grad_tokens, *kept = turn(
                attn_ring, down_ring, up_ring, kept=(grad_tokens, *kept)
            )
        for ring, out in zip(made, kept[len(kept) - len(made) :]):
            whole[ring] = out
        return [grad_tokens, *kept[: len(kept) - len(made)]]

    grad_tokens, stacked_far, result = tokens_turn(
        0, grad_tokens, swap_bit(stacked, "mp", 0), result
    )
    grad_up_bias = jnp.sum(clock.hold(grad_pre), axis=0)
    grad_down_bias = jnp.sum(clock.hold(cotangent), axis=0)
    ups = grad_up_bias.reshape(-1, width)
    small = jnp.concatenate(
        [stacked + stacked_far, jnp.stack([gain2, bias2, grad_down_bias]), ups], 0
    )
    thin = attn_ring.rows
    extra = -(-small.shape[0] * width // (2 * thin * inner))
    side = extra * thin * inner // width
    small = jnp.pad(small, ((0, 2 * side - small.shape[0]), (0, 0)))
    small = small + swap_bit(small, "seq", 0)
    small = lax.dynamic_slice_in_dim(small, core * side, side, 0)
    turns = 1
    while attn_ring.step < hops:
        (grad_tokens,) = tokens_turn(turns, grad_tokens)
        turns += 1
    attn_ring.take(small.reshape(extra, thin, inner))
    while attn_ring.step < 2 * hops:
        (grad_tokens,) = tokens_turn(turns, grad_tokens)
        turns += 1
    gather_done()
    grad_down, grad_up = whole[down_ring][0], whole[up_ring][0]
    small = attn_ring.extra_sum().reshape(side, width)
    other = swap_bit(small, "seq", 0)
    attn_ring.own[0] = after(attn_ring.own[0], small)
    grad_qkv, grad_out = attn_ring.results()
    grad_out = jnp.transpose(grad_out[0])
    small = jnp.where(
        core == 0, jnp.concatenate([small, other], 0), jnp.concatenate([other, small], 0)
    )

    channels = in_coef.shape[0]
    at = (place_seq * lax.axis_size("mp") + lax.axis_index("mp")) * channels
    own = jnp.transpose(lax.dynamic_slice_in_dim(small[: 3 * states + 1], at, channels, 1))
    grad_in = own[:, :states]
    grad_out_coef = own[:, states : 2 * states]
    grad_decay = own[:, 2 * states : 3 * states]
    grad_skip = own[:, 3 * states]
    small = small[3 * states + 1 :]
    return (
        result,
        grad_tokens,
        small[0],
        small[1],
        grad_in,
        grad_out_coef,
        grad_decay,
        grad_skip,
        grad_qkv,
        grad_out,
        small[2],
        small[3],
        grad_up,
        small[5 : 5 + ups.shape[0]].reshape(-1),
        grad_down,
        small[4],
    )


def solution(mesh):
    owner = P(("seq", "mp"), None)
    return jax.shard_map(
        per_device,
        mesh=mesh,
        in_specs=(
            P("seq", None),
            P(None, ("seq", "mp"), None),
            P(),
            P(),
            owner,
            owner,
            owner,
            P(("seq", "mp")),
            P(None, None, "mp"),
            P("mp", None),
            P(),
            P(),
            P(None, "mp"),
            P("mp"),
            P("mp", None),
            P(),
            P("seq", None),
        ),
        out_specs=(
            P("seq", None),
            P("seq", None),
            P(),
            P(),
            owner,
            owner,
            owner,
            P(("seq", "mp")),
            P(None, None, "mp"),
            P("mp", None),
            P(),
            P(),
            P(None, "mp"),
            P("mp"),
            P("mp", None),
            P(),
        ),
        check_vma=False,
    )
```

```python
import functools
import math

import jax
import jax.numpy as jnp
from jax import lax
from jax.experimental import pallas as pl
from jax.experimental.pallas import tpu as pltpu
from jax.sharding import PartitionSpec as P

HDIM = 128
BLOCK = 512
CTX = 128
LEN = 4096
EPS = 1e-05
HIGH = lax.Precision.HIGH


def mm(left, right, dims=((1,), (0,))):
    return lax.dot_general(
        left, right, (dims, ((), ())), precision=HIGH, preferred_element_type=jnp.float32
    )


def norm_parts(value):
    center = value - jnp.mean(value, axis=-1, keepdims=True)
    spread = jnp.mean(center * center, axis=-1, keepdims=True)
    rate = lax.rsqrt(spread + EPS)
    return center * rate, rate


def norm_back(grad, unit, rate, gain):
    scaled = grad * gain
    inner = jnp.mean(scaled * unit, axis=-1, keepdims=True)
    return rate * (scaled - jnp.mean(scaled, axis=-1, keepdims=True) - unit * inner)


def swap_bit(value, axis, bit):
    size = lax.axis_size(axis)
    return lax.ppermute(value, axis, [(i, i ^ (1 << bit)) for i in range(size)])


def bits_of(count):
    return count.bit_length() - 1


def shift_in_window(value, distance, per_window):
    size = lax.axis_size("seq")
    route = [(i, i + distance) for i in range(size)]
    inside = [(a, b) for a, b in route if 0 <= b < size and a // per_window == b // per_window]
    return lax.ppermute(value, "seq", inside)


def after(value, *others):
    return lax.optimization_barrier((value,) + others)[0]


def gather_all(piece, gates=()):
    mp_size, seq_size = lax.axis_size("mp"), lax.axis_size("seq")
    me = lax.axis_index("seq") * mp_size + lax.axis_index("mp")
    block, seen = piece, []
    for bit in range(bits_of(mp_size * seq_size)):
        axis, own = ("mp", bit) if bit < bits_of(mp_size) else ("seq", bit - bits_of(mp_size))
        if gates:
            block = after(block, gates[bit])
        other = swap_bit(block, axis, own)
        upper = (me >> bit) & 1
        block = jnp.where(
            upper == 1, jnp.concatenate([other, block], 1), jnp.concatenate([block, other], 1)
        )
        seen.append(block)
    return block, seen


def trade_chips(value, distance):
    size = lax.axis_size("seq")
    return lax.ppermute(value, "seq", [(i, i ^ (2 * distance)) for i in range(size)])


def chip_order(count):
    if count <= 2:
        return list(range(count))
    return list(range(0, count, 2)) + list(range(count - 1 - count % 2, 0, -2))


def ring_route(count):
    order = chip_order(count)
    route = []
    for i in range(count):
        here, there = order[i], order[(i + 1) % count]
        route.append((2 * here, 2 * there))
        route.append((2 * there + 1, 2 * here + 1))
    return route


def ring_spot():
    count = lax.axis_size("seq") // 2
    places = [0] * count
    for i, chip in enumerate(chip_order(count)):
        places[chip] = i
    me = lax.axis_index("seq")
    here = jnp.array(places, jnp.int32)[me // 2]
    return jnp.where(me % 2 == 0, here, (count - here) % count)


def unset(shape):
    return pl.pallas_call(
        lambda out: None,
        out_shape=jax.ShapeDtypeStruct(shape, jnp.float32),
        out_specs=pl.BlockSpec(memory_space=pl.ANY),
        compiler_params=pltpu.CompilerParams(vmem_limit_bytes=1 << 20),
    )()


def pack_kernel(*refs):
    low = 0
    for ref in refs[:-1]:
        refs[-1][low : low + ref.shape[0], :] = ref[...]
        low += ref.shape[0]


def pack(parts):
    rows, cols = sum(part.shape[0] for part in parts), parts[0].shape[1]
    return pl.pallas_call(
        pack_kernel,
        out_shape=jax.ShapeDtypeStruct((rows, cols), jnp.float32),
        compiler_params=pltpu.CompilerParams(vmem_limit_bytes=1 << 20),
    )(*parts)


def pick(value, index):
    return lax.dynamic_index_in_dim(value, index, 0, keepdims=False)


class Clock:
    def __init__(self):
        self.last = ()

    def hold(self, value):
        return after(value, *self.last) if self.last else value

    def set(self, *values):
        self.last = values


def assemble_kernel(count, cuts, where_ref, *refs):
    parts, outs, sems = refs[: 2 * count], refs[2 * count : -1], refs[-1]
    copies = []
    for n in range(2 * count):
        which, spot = where_ref[0, n], where_ref[1, n]
        for out, (low, high) in zip(outs, cuts):
            copies.append(
                pltpu.make_async_copy(
                    parts[n].at[low:high], out.at[:, which, spot], sems.at[len(copies)]
                )
            )
    for copy in copies:
        copy.start()
    for copy in copies:
        copy.wait()


class Ring:
    def __init__(self, pieces, outs):
        self.count = lax.axis_size("seq") // 2
        self.place, self.route = ring_spot(), ring_route(self.count)
        self.core = lax.axis_index("seq") % 2
        self.mirror = (self.count - self.place) % self.count
        self.rows, self.cols = pieces[0][0].shape[0] // self.count, pieces[0][0].shape[1]
        self.pieces = [
            [a.reshape(self.count, self.rows, self.cols) for a in addends] for addends in pieces
        ]
        self.outs = outs
        self.step, self.own, self.far, self.extras = 0, [], [], []
        self.held = self.chunk(self.place)

    def chunk(self, spot):
        return jnp.stack([sum(pick(a, spot) for a in addends) for addends in self.pieces])

    def take(self, extra):
        self.extras = [extra]
        self.held = jnp.concatenate([self.held, extra], 0)

    def extra_sum(self):
        count = self.count
        seen = jnp.stack(self.extras)
        return sum(
            lax.dynamic_index_in_dim(seen, (self.place - i + count) % count, 0, keepdims=False)
            for i in range(count)
        )

    def turn(self, clock, kept=()):
        got = lax.ppermute(self.held, "seq", self.route)
        got, *kept = lax.optimization_barrier((got, *kept, *clock.last))[: 1 + len(kept)]
        self.step += 1
        if self.step < self.count:
            got = got + self.chunk((self.place + 2 * self.count - self.step) % self.count)
        self.held = got
        if self.step >= self.count - 1:
            self.own.append(got)
            self.far.append(swap_bit(got, "seq", 0))
        if self.extras:
            self.extras.append(got[-self.extras[0].shape[0] :])
        clock.set(got)
        return kept

    def results(self):
        count = self.count
        hops = jnp.arange(count, dtype=jnp.int32)
        spots = jnp.concatenate([self.place + 1 - hops, self.mirror + 1 - hops]) + count
        which = jnp.repeat(jnp.stack([self.core, 1 - self.core]), count)
        where = jnp.stack([which, spots % count]).astype(jnp.int32)
        cuts, low = [], 0
        for size in self.outs:
            cuts.append((low, low + size))
            low += size
        shapes = [(size, 2, count, self.rows, self.cols) for size in self.outs]
        outs = pl.pallas_call(
            functools.partial(assemble_kernel, count, cuts),
            in_specs=[pl.BlockSpec(memory_space=pltpu.SMEM)]
            + [pl.BlockSpec(memory_space=pltpu.VMEM)] * (2 * count),
            out_specs=[pl.BlockSpec(memory_space=pl.ANY)] * len(shapes),
            out_shape=[jax.ShapeDtypeStruct(shape, jnp.float32) for shape in shapes],
            scratch_shapes=[pltpu.SemaphoreType.DMA((2 * count * len(shapes),))],
            cost_estimate=pl.CostEstimate(flops=0, bytes_accessed=COST, transcendentals=0),
        )(where, *self.own, *self.far)
        return [out.reshape(out.shape[0], -1, self.cols) for out in outs]


def core_half(value, which):
    size = value.shape[1] // 2
    return lax.dynamic_slice_in_dim(value, which * size, size, 1)


def rows8(shape):
    return lax.broadcasted_iota(jnp.int32, shape, 0).astype(jnp.float32)


def tree(values):
    values = list(values)
    while len(values) > 1:
        values = [sum(values[i : i + 2]) for i in range(0, len(values), 2)]
    return values[0]


def groups(decay_ref):
    states, lanes = decay_ref.shape
    for low in range(0, lanes, 128):
        span = slice(low, low + 128)
        rates = [jnp.broadcast_to(decay_ref[n : n + 1, span], (8, 128)) for n in range(states)]
        yield span, rates, [jnp.exp(-8.0 * rate) for rate in rates]


UNROLL = 4


def over_rows(ref, count, span, body, carry):
    def step(i, carry):
        for k in range(UNROLL):
            base = pl.multiple_of((i * UNROLL + k) * 8, 8)
            carry = body(ref[pl.ds(base, 8), span], carry)
        return carry

    return lax.fori_loop(0, count // (8 * UNROLL), step, carry)


def summary_kernel(tail_ref, x_ref, decay_ref, h_ref):
    for span, rates, jump in groups(decay_ref):

        def body(tile, acc):
            return tuple(j * a + tile for j, a in zip(jump, acc))

        acc = (tail_ref[:8, span] * 0.0,) * len(rates)
        acc = over_rows(tail_ref, tail_ref.shape[0], span, body, acc)
        acc = over_rows(x_ref, x_ref.shape[0] - tail_ref.shape[0], span, body, acc)
        left = 7.0 - rows8((8, 128))
        for n, rate in enumerate(rates):
            h_ref[n : n + 1, span] = jnp.sum(acc[n] * jnp.exp(-rate * left), axis=0, keepdims=True)


def moment_kernel(tail_ref, x_ref, decay_ref, p_ref):
    for span, rates, jump in groups(decay_ref):

        def body(tile, carry):
            acc, lag = carry
            lag = tuple(j * (b + a) for j, a, b in zip(jump, acc, lag))
            return tuple(j * a + tile for j, a in zip(jump, acc)), lag

        zeros = (tail_ref[:8, span] * 0.0,) * len(rates)
        carry = over_rows(tail_ref, tail_ref.shape[0], span, body, (zeros, zeros))
        acc, lag = over_rows(x_ref, x_ref.shape[0] - tail_ref.shape[0], span, body, carry)
        left = 7.0 - rows8((8, 128))
        for n, rate in enumerate(rates):
            total = (8.0 * lag[n] + left * acc[n]) * jnp.exp(-rate * left)
            p_ref[n : n + 1, span] = jnp.sum(total, axis=0, keepdims=True)


def carry_kernel(near_ref, first_ref, decay_ref, y_ref):
    for span, rates, jump in groups(decay_ref):
        ahead = rows8((8, 128)) + 1.0
        modes = tuple(
            jnp.broadcast_to(first_ref[n : n + 1, span], (8, 128)) * jnp.exp(-rate * ahead)
            for n, rate in enumerate(rates)
        )

        def step(i, modes):
            for k in range(UNROLL):
                base = pl.multiple_of((i * UNROLL + k) * 8, 8)
                y_ref[pl.ds(base, 8), span] = near_ref[pl.ds(base, 8), span] + tree(modes)
                modes = tuple(j * m for j, m in zip(jump, modes))
            return modes

        lax.fori_loop(0, y_ref.shape[0] // (8 * UNROLL), step, modes)


def spread_kernel(first_ref, decay_ref, tail_ref, y_ref):
    for span, rates, jump in groups(decay_ref):
        ahead = 8.0 - rows8((8, 128))
        modes = tuple(
            jnp.broadcast_to(first_ref[n : n + 1, span], (8, 128)) * jnp.exp(-rate * ahead)
            for n, rate in enumerate(rates)
        )

        def run(ref, modes):
            count = ref.shape[0] // 8

            def step(i, modes):
                for k in range(UNROLL):
                    base = pl.multiple_of((count - 1 - i * UNROLL - k) * 8, 8)
                    ref[pl.ds(base, 8), span] = tree(modes)
                    modes = tuple(j * m for j, m in zip(jump, modes))
                return modes

            return lax.fori_loop(0, count // UNROLL, step, modes)

        run(tail_ref, run(y_ref, modes))


def near_kernel(x_ref, fade_ref, gate_ref, skip_ref, y_ref):
    fade, gate, skip = fade_ref[...], gate_ref[...], skip_ref[...]

    def octet(i, u):
        base = pl.multiple_of(i * 8, 8)
        tile = x_ref[pl.ds(base, 8), :]
        rows = []
        for r in range(8):
            row = tile[r : r + 1, :]
            u = fade * u + gate * jnp.broadcast_to(row, fade.shape)
            rows.append(jnp.sum(u, axis=0, keepdims=True) + skip * row)
        y_ref[pl.ds(base, 8), :] = jnp.concatenate(rows, 0)
        return u

    lax.fori_loop(0, x_ref.shape[0] // 8, octet, jnp.zeros(fade.shape, jnp.float32))


def tail_back_kernel(
    x_ref, d_ref, fade_ref, gate_ref, skip_ref, q_ref, r_ref, dh_ref, dp_ref, dskip_ref, dx_ref
):
    fade, gate, skip = fade_ref[...], gate_ref[...], skip_ref[...]
    octets = x_ref.shape[0] // 8
    zero = jnp.zeros(fade.shape, jnp.float32)

    def forward(i, carry):
        h, p, dh, dp = carry
        base = pl.multiple_of(i * 8, 8)
        tile, grads = x_ref[pl.ds(base, 8), :], d_ref[pl.ds(base, 8), :]
        for r in range(8):
            p = fade * (p + h)
            h = fade * h + jnp.broadcast_to(tile[r : r + 1, :], fade.shape)
            grad = jnp.broadcast_to(grads[r : r + 1, :], fade.shape)
            dh = dh + grad * h
            dp = dp + grad * p
        return h, p, dh, dp

    _, _, dh, dp = lax.fori_loop(0, octets, forward, (zero, zero, zero, zero))
    dh_ref[...] = dh
    dp_ref[...] = dp
    dskip_ref[...] = jnp.sum(x_ref[...] * d_ref[...], axis=0, keepdims=True)

    def backward(k, carry):
        q, r_sum = carry
        base = pl.multiple_of((octets - 1 - k) * 8, 8)
        grads = d_ref[pl.ds(base, 8), :]
        rows = [None] * 8
        for r in reversed(range(8)):
            r_sum = fade * (r_sum + q)
            grad = grads[r : r + 1, :]
            q = fade * q + jnp.broadcast_to(grad, fade.shape)
            rows[r] = jnp.sum(gate * q, axis=0, keepdims=True) + skip * grad
        dx_ref[pl.ds(base, 8), :] = jnp.concatenate(rows, 0)
        return q, r_sum

    q, r_sum = lax.fori_loop(0, octets, backward, (zero, zero))
    q_ref[...] = q
    r_ref[...] = r_sum


def by_channels(kernel, ins, outs, cut=512):
    width = ins[0].shape[1]
    cut = cut if width % cut == 0 else width

    def spec(rows):
        return pl.BlockSpec((rows, cut), lambda i: (0, i))

    return pl.pallas_call(
        kernel,
        grid=(width // cut,),
        in_specs=[spec(a.shape[0]) for a in ins],
        out_specs=[spec(r) for r in outs],
        out_shape=[jax.ShapeDtypeStruct((r, width), jnp.float32) for r in outs],
        cost_estimate=pl.CostEstimate(flops=0, bytes_accessed=COST, transcendentals=0),
        compiler_params=pltpu.CompilerParams(vmem_limit_bytes=12 << 20),
    )(*ins)


def cut(value):
    top = value.astype(jnp.bfloat16)
    return top, (value - top.astype(jnp.float32)).astype(jnp.bfloat16)


def dot3(left, right, dims):
    def one(a, b):
        return lax.dot_general(a, b, (dims, ((), ())), preferred_element_type=jnp.float32)

    return one(left[0], right[1]) + one(left[1], right[0]) + one(left[0], right[0])


NT = ((1,), (1,))
NN = ((1,), (0,))
TN = ((0,), (0,))
TILE = 256
COST = 1024
SCALE = HDIM ** (-0.5)


def causal(shape, first_row):
    row = lax.broadcasted_iota(jnp.int32, shape, 0) + first_row
    return lax.broadcasted_iota(jnp.int32, shape, 1) <= row


def self_kernel(q_ref, k_ref, v_ref, acc_ref, top_ref):
    rows = q_ref.shape[0]
    k, v = cut(k_ref[...]), cut(v_ref[...])
    for first in range(0, rows, TILE):
        span = slice(first, first + TILE)
        seen = first + TILE
        q = cut(q_ref[span, :] * SCALE)
        scores = dot3(q, (k[0][:seen], k[1][:seen]), NT)
        scores = jnp.where(causal(scores.shape, first), scores, -1e30)
        top = jnp.max(scores, axis=1, keepdims=True)
        weight = jnp.exp(scores - top)
        acc_ref[span, :] = dot3(cut(weight), (v[0][:seen], v[1][:seen]), NN)
        total = jnp.sum(weight, axis=1, keepdims=True)
        lane = lax.broadcasted_iota(jnp.int32, (TILE, HDIM), 1)
        top_ref[span, :] = jnp.where(lane < HDIM // 2, top, total)


def ctx_kernel(ok_ref, q_ref, k_ref, v_ref, acc_ref, top_ref, out_ref, log_ref):
    ok = ok_ref[0] > 0
    q = cut(q_ref[...] * SCALE)
    scores = dot3(q, cut(k_ref[...]), NT)
    scores = jnp.where(ok, scores, -1e30)
    near, near_sum = top_ref[:, :1], top_ref[:, HDIM // 2 : HDIM // 2 + 1]
    top = jnp.maximum(near, jnp.max(scores, axis=1, keepdims=True))
    weight = jnp.where(ok, jnp.exp(scores - top), 0.0)
    ease = jnp.exp(near - top)
    total = near_sum * ease + jnp.sum(weight, axis=1, keepdims=True)
    out_ref[...] = (acc_ref[...] * ease + dot3(cut(weight), cut(v_ref[...]), NN)) / total
    log_ref[...] = jnp.broadcast_to(top + jnp.log(total), log_ref.shape)


def back_kernel(ok_ref, q_ref, k_ref, v_ref, kc_ref, vc_ref, o_ref, l_ref, g_ref, d_ref):
    ok = ok_ref[0] > 0
    rows = q_ref.shape[0]
    k, v, kc, vc = cut(k_ref[...]), cut(v_ref[...]), cut(kc_ref[...]), cut(vc_ref[...])
    d_ref[0, :CTX, :] = jnp.zeros((CTX, HDIM), jnp.float32)
    for first in reversed(range(0, rows, TILE)):
        seen = first + TILE
        span = slice(first, seen)
        grad = g_ref[span, :]
        q = cut(q_ref[span, :] * SCALE)
        grad2 = cut(grad)
        inner = jnp.sum(grad * o_ref[span, :], axis=1, keepdims=True)
        mark = l_ref[span, :][:, :1]
        ks, vs = (k[0][:seen], k[1][:seen]), (v[0][:seen], v[1][:seen])
        probs = dot3(q, ks, NT)
        probs = jnp.where(causal(probs.shape, first), jnp.exp(probs - mark), 0.0)
        probs_c = jnp.where(ok, jnp.exp(dot3(q, kc, NT) - mark), 0.0)
        ds = cut(probs * (dot3(grad2, vs, NT) - inner))
        ds_c = cut(probs_c * (dot3(grad2, vc, NT) - inner))
        probs, probs_c = cut(probs), cut(probs_c)
        d_ref[0, CTX + first : CTX + seen, :] = (dot3(ds, ks, NN) + dot3(ds_c, kc, NN)) * SCALE
        for at, (own, ctx, other) in enumerate([(ds, ds_c, q), (probs, probs_c, grad2)]):
            near, back = dot3(own, other, TN), dot3(ctx, other, TN)
            if seen == rows:
                d_ref[1 + at, CTX:, :] = near
                d_ref[1 + at, :CTX, :] = back
            else:
                d_ref[1 + at, CTX : CTX + seen, :] += near
                d_ref[1 + at, :CTX, :] += back


def by_heads(kernel, ins, outs, scalars=()):
    heads = ins[0][0].shape[-1] // HDIM
    specs = [pl.BlockSpec(memory_space=pltpu.SMEM) for _ in scalars]
    for _, rows, *at in ins:
        if len(at) == 2:
            specs.append(pl.BlockSpec((None, rows, HDIM), lambda h, at=at: (at[1], at[0], h)))
        else:
            specs.append(pl.BlockSpec((rows, HDIM), lambda h, at=at: (at[0], h)))
    return pl.pallas_call(
        kernel,
        grid=(heads,),
        in_specs=specs,
        out_specs=[
            pl.BlockSpec(lead + (HDIM,), lambda h, n=len(lead): (0,) * n + (h,)) for lead in outs
        ],
        out_shape=[jax.ShapeDtypeStruct(lead + (heads * HDIM,), jnp.float32) for lead in outs],
        cost_estimate=pl.CostEstimate(flops=0, bytes_accessed=COST, transcendentals=0),
        compiler_params=pltpu.CompilerParams(vmem_limit_bytes=16 << 20),
    )(*scalars, *[a[0] for a in ins])


def project_kernel(x_ref, w_ref, out_ref, high_ref, low_ref):
    @pl.when(pl.program_id(0) == 0)
    def _():
        high_ref[...], low_ref[...] = cut(x_ref[...])

    def one(part):
        return lax.dot_general(
            part, w_ref[...], (NN, ((), ())), preferred_element_type=jnp.float32
        )

    out_ref[...] = one(low_ref[...]) + one(high_ref[...])


def project(x, weights, first, count):
    rows, depth = x.shape
    width = weights.shape[2]
    return pl.pallas_call(
        project_kernel,
        grid=(count,),
        in_specs=[
            pl.BlockSpec((rows, depth), lambda i: (0, 0)),
            pl.BlockSpec((None, depth, width), lambda i: (first + i, 0, 0)),
        ],
        out_specs=pl.BlockSpec((None, rows, width), lambda i: (i, 0, 0)),
        out_shape=jax.ShapeDtypeStruct((count, rows, width), jnp.float32),
        scratch_shapes=[pltpu.VMEM((rows, depth), jnp.bfloat16)] * 2,
        cost_estimate=pl.CostEstimate(flops=0, bytes_accessed=COST, transcendentals=0),
        compiler_params=pltpu.CompilerParams(vmem_limit_bytes=16 << 20),
    )(x, weights)


def per_device(
    tokens,
    window_state,
    norm1_gain,
    norm1_bias,
    in_coef,
    out_coef,
    decay_rate,
    skip_gain,
    qkv_weight,
    out_weight,
    norm2_gain,
    norm2_bias,
    up_weight,
    up_bias,
    down_weight,
    down_bias,
    cotangent,
):
    place_seq = lax.axis_index("seq")
    core = place_seq % 2
    rows, width = tokens.shape
    states = in_coef.shape[1]
    windows = window_state.shape[0]
    per_window = LEN // rows
    block = place_seq % per_window
    window = place_seq // per_window
    has_ctx = block > 0
    ok = has_ctx.astype(jnp.int32).reshape(1)
    half = rows // 2

    qkv = qkv_weight.astype(jnp.float32)
    out_own = out_weight.astype(jnp.float32)
    up = up_weight.astype(jnp.float32)
    down = down_weight.astype(jnp.float32)

    coefs, rounds = gather_all(
        pack(
            [jnp.transpose(a) for a in (decay_rate, in_coef, out_coef)]
            + [jnp.transpose(window_state[w]) for w in range(windows)]
            + [skip_gain[None]]
        )
    )
    decay, c_in, c_out = (coefs[i * states : (i + 1) * states] for i in range(3))
    carried = lax.dynamic_slice_in_dim(coefs, (3 + window) * states, states, 0)
    skip = coefs[(3 + windows) * states :]
    gate = c_in * c_out
    fade = jnp.exp(-decay)

    def faded(steps):
        return jnp.exp(-decay * steps)

    inner = out_own.shape[0]
    sent = pick(out_weight.reshape(2, inner // 2, width), core).astype(jnp.float32)
    across = swap_bit(after(sent, rounds[1]), "mp", 0)
    beside = swap_bit(across, "seq", 0)
    out_far = jnp.where(
        core == 0, jnp.concatenate([across, beside], 0), jnp.concatenate([beside, across], 0)
    )

    unit1, rate1 = norm_parts(tokens)
    normed = after(unit1 * norm1_gain + norm1_bias)
    tail = shift_in_window(normed[rows - CTX :], 1, per_window)
    qkv_rows = project(normed, qkv_weight, 0, 3)
    acc, top = by_heads(
        self_kernel,
        [(qkv_rows, rows, 0, i) for i in range(3)],
        [(rows,)] * 2,
    )

    length = float(rows)
    chips = per_window // 2
    chip = block // 2
    (sum_h,) = by_channels(
        summary_kernel,
        [tail, after(normed, acc), decay],
        [states],
    )

    def pair_order(value):
        other = swap_bit(value, "seq", 0)
        return jnp.where(core == 0, value, other), jnp.where(core == 0, other, value)

    first_h, second_h = pair_order(sum_h)
    both_h = faded(length) * first_h + second_h
    far_h = [trade_chips(both_h, d) for d in range(1, chips)]
    (near,) = by_channels(
        near_kernel, [after(tail, sum_h), fade, gate, skip], [CTX]
    )
    far_h = [after(h, near) for h in far_h]
    past_h = jnp.zeros_like(sum_h)
    for d in range(1, chips):
        there = chip ^ d
        gap = jnp.maximum(chip - 1 - there, 0).astype(jnp.float32) * (2.0 * length)
        past_h = past_h + jnp.where(there < chip, faded(gap) * far_h[d - 1], 0.0)
    chip_h = past_h
    past_h = jnp.where(core == 0, past_h, faded(length) * past_h + first_h)

    start_t = jnp.maximum(block * rows - CTX, 0).astype(jnp.float32)
    first = c_out * (c_in * past_h + carried * faded(start_t))

    (context,) = by_channels(
        carry_kernel, [near, first, decay], [CTX]
    )
    kv_ctx = project(context, qkv_weight, 1, 2)
    heads, logs, far = [], [], []
    for part in range(2):
        o, l = by_heads(
            ctx_kernel,
            [(qkv_rows, half, part, 0), (after(kv_ctx, *heads), CTX, 0, 0), (kv_ctx, CTX, 0, 1)]
            + [(a, half, part) for a in (acc, top)],
            [(half,)] * 2,
            scalars=(ok,),
        )
        heads.append(o)
        logs.append(l)
        far.append(swap_bit(o, "mp", 0))
    grad_hidden = mm(after(cotangent, *heads), down, NT)
    seen = jnp.concatenate([after(context, *heads), normed], 0)
    outs = jnp.concatenate(heads, 0)
    log = jnp.concatenate(logs, 0)

    hidden, grad_pre = unset((rows, up.shape[1])), unset((rows, up.shape[1]))
    normed2 = unset((rows, width))
    mixed, part2 = [], []
    for part in range(2):
        span = slice(part * half, (part + 1) * half)
        came = after(far[part], part2[0]) if part else after(far[0], seen, outs, log, grad_hidden)
        m = tokens[span] + (mm(heads[part], out_own) + mm(came, out_far))
        n = norm_parts(m)[0] * norm2_gain + norm2_bias
        pre = mm(n, up) + up_bias
        cdf = 0.5 + 0.5 * lax.erf(pre * (0.5**0.5))
        bell = jnp.exp(-0.5 * pre * pre) * (1.0 / math.sqrt(2.0 * math.pi))
        hidden = lax.dynamic_update_slice(hidden, pre * cdf, (part * half, 0))
        slope = grad_hidden[span] * (cdf + pre * bell)
        grad_pre = lax.dynamic_update_slice(grad_pre, slope, (part * half, 0))
        normed2 = lax.dynamic_update_slice(normed2, n, (part * half, 0))
        mixed.append(m)
        if part == 0:
            part2.append(mm(grad_pre[span], up, NT))

    clock = Clock()
    give = mm(core_half(after(hidden, part2[0]), 1 - core), cotangent, TN)
    keep = mm(core_half(after(hidden, give), core), cotangent, TN)
    down_ring = Ring([[keep, swap_bit(give, "seq", 0)]], (1,))
    clock.set(down_ring.held)
    part2.append(mm(clock.hold(grad_pre)[half:], up, NT))
    clock.set(part2[1])
    gots2 = [swap_bit(p, "mp", 0) for p in part2]
    mixed = jnp.concatenate(mixed, 0)
    grad_mixed, grad_heads = unset((rows, width)), []
    gain2, bias2 = 0.0, 0.0

    def norm2_half(part, grad_mixed, gain2, bias2):
        span = slice(part * half, (part + 1) * half)
        grad2 = part2[part] + after(gots2[part], *clock.last)
        unit2, rate2 = norm_parts(after(mixed, grad2)[span])
        gain2 = gain2 + jnp.sum(grad2 * unit2, axis=0)
        bias2 = bias2 + jnp.sum(grad2, axis=0)
        new = cotangent[span] + norm_back(grad2, unit2, rate2, norm2_gain)
        grad_mixed = lax.dynamic_update_slice(grad_mixed, new, (part * half, 0))
        clock.set(grad_mixed, gain2, bias2)
        return grad_mixed, gain2, bias2

    hops = down_ring.count - 1

    def turn(*rings, kept=()):
        rings = [ring for ring in rings if ring.step < 2 * hops]
        for ring in rings[:-1]:
            ring.turn(clock)
        return rings[-1].turn(clock, kept)

    (gots2[0],) = turn(down_ring, kept=(gots2[0],))
    grad_mixed, gain2, bias2 = norm2_half(0, grad_mixed, gain2, bias2)
    give = mm(core_half(clock.hold(normed2), 1 - core), grad_pre, TN)
    clock.set(give)
    keep = mm(core_half(clock.hold(normed2), core), grad_pre, TN) + swap_bit(give, "seq", 0)
    up_ring = Ring([[keep]], (1,))
    clock.set(up_ring.held)
    (gots2[1],) = turn(down_ring, kept=(gots2[1],))
    grad_mixed, gain2, bias2 = norm2_half(1, grad_mixed, gain2, bias2)
    grad_heads = mm(clock.hold(grad_mixed), out_own, NT)
    clock.set(grad_heads)
    turn(down_ring, up_ring)

    (grads,) = by_heads(
        back_kernel,
        [(qkv_rows, rows, 0, i) for i in range(3)]
        + [(kv_ctx, CTX, 0, i) for i in range(2)]
        + [(a, rows, 0) for a in (outs, log, clock.hold(grad_heads))],
        [(3, CTX + rows)],
        scalars=(ok,),
    )
    clock.set(grads)
    turn(down_ring, up_ring)
    gives = [mm(core_half(clock.hold(seen), 1 - core), grads[i], TN) for i in range(3)]
    gives.append(mm(core_half(clock.hold(grad_mixed), 1 - core), outs, TN))
    gots = [swap_bit(g, "seq", 0) for g in gives]
    clock.set(*gives)
    turn(down_ring, up_ring)
    keeps = [mm(core_half(clock.hold(seen), core), grads[i], TN) + gots[i] for i in range(3)]
    keeps.append(mm(core_half(clock.hold(grad_mixed), core), outs, TN) + gots[3])
    attn_ring = Ring([[k] for k in keeps], (3, 1))
    clock.set(attn_ring.held)

    feed = mm(clock.hold(hidden), down)
    clock.set(feed)
    turn(attn_ring, down_ring, up_ring)
    grad_seen = sum(mm(clock.hold(grads)[i], qkv[i], NT) for i in range(3))
    grad_context = jnp.where(has_ctx, grad_seen[:CTX], 0.0)
    clock.set(grad_seen)
    quarter = rows // 4
    result, grad_tokens = unset((rows, width)), unset((rows, width))

    def across(source, k, into, base, kept=()):
        span = slice(k * quarter, (k + 1) * quarter)
        got = swap_bit(source[span], "mp", 0)
        got, into, *kept = turn(attn_ring, down_ring, up_ring, kept=(got, into, *kept))
        new = base(span) + (source[span] + got)
        return [lax.dynamic_update_slice(into, new, (k * quarter, 0)), *kept]

    def result_base(span):
        return mixed[span] + down_bias

    (result,) = across(feed, 0, result, result_base)

    sum_q, sum_r, part_h, part_p, part_skip, grad_tail = by_channels(
        tail_back_kernel,
        [tail, clock.hold(grad_context), fade, gate, skip],
        [states, states, states, states, 1, CTX],
    )
    clock.set(sum_q)
    (result,) = across(feed, 1, result, result_base)
    (sum_p,) = by_channels(moment_kernel, [tail, clock.hold(normed), decay], [states])
    clock.set(sum_p)
    other = swap_bit(jnp.concatenate([sum_p, sum_q], 0), "seq", 0)
    other_p, other_q = other[:states], other[states:]
    first_p, second_p = jnp.where(core == 0, sum_p, other_p), jnp.where(core == 0, other_p, sum_p)
    first_q, second_q = jnp.where(core == 0, sum_q, other_q), jnp.where(core == 0, other_q, sum_q)
    both_p = faded(length) * (first_p + length * first_h) + second_p
    both_q = first_q + faded(length) * second_q
    both = jnp.concatenate([both_p, both_q], 0)
    clock.set(both)
    past_p = jnp.zeros_like(sum_p)
    later = jnp.zeros_like(sum_q)
    came = [trade_chips(both, d) for d in range(1, chips)]
    (result,) = across(feed, 2, result, result_base)
    came[0] = clock.hold(came[0])
    for d in range(1, chips):
        there = chip ^ d
        gap = (jnp.maximum(jnp.abs(chip - there) - 1, 0)).astype(jnp.float32) * (2.0 * length)
        near_p, near_q = came[d - 1][:states], came[d - 1][states:]
        fading = faded(gap)
        past_p = past_p + jnp.where(there < chip, fading * (near_p + gap * far_h[d - 1]), 0.0)
        later = later + jnp.where(there > chip, fading * near_q, 0.0)
    past_p = jnp.where(core == 0, past_p, faded(length) * (past_p + length * chip_h) + first_p)
    later = jnp.where(core == 1, later, second_q + faded(length) * later)
    far_tail, grad_rows = by_channels(
        spread_kernel,
        [gate * later, decay],
        [CTX, rows - CTX],
    )
    to_last = far_tail + grad_tail
    clock.set(to_last)
    from_next = shift_in_window(to_last, -1, per_window)
    (result,) = across(feed, 3, result, result_base)
    along_h = fade * clock.hold(past_h) * sum_q + part_h
    along_p = fade * (past_h * (sum_r + sum_q) + past_p * sum_q) + part_p
    gone = faded(start_t + 1.0)
    part_in = c_out * along_h
    part_out = c_in * along_h + carried * gone * sum_q
    part_decay = -gate * along_p - c_out * carried * gone * ((start_t + 1.0) * sum_q + sum_r)
    clock.set(part_in, part_out, part_decay)

    grad_normed = grad_seen[CTX:] + jnp.concatenate([grad_rows, clock.hold(from_next)], 0)
    part_gain1 = jnp.sum(grad_normed * unit1, axis=0, keepdims=True)
    part_bias1 = jnp.sum(grad_normed, axis=0, keepdims=True)
    part_tokens = norm_back(grad_normed, unit1, rate1, norm1_gain)
    clock.set(part_tokens, part_gain1, part_bias1)
    turn(attn_ring, down_ring, up_ring)
    stacked = jnp.concatenate([part_in, part_out, part_decay, part_skip, part_gain1, part_bias1], 0)
    whole = {}

    def gather_done():
        made = []
        for ring in (down_ring, up_ring):
            if ring.step == 2 * hops and ring not in whole:
                ring.own[0] = clock.hold(ring.own[0])
                whole[ring] = ring.results()[0]
                made.append(ring)
        return made

    def tokens_turn(k, grad_tokens, *kept):
        made = gather_done()
        kept = [*kept, *[whole[ring] for ring in made]]
        if k < 4:
            grad_tokens, *kept = across(
                part_tokens, k, grad_tokens, lambda span: grad_mixed[span], kept
            )
        else:
            grad_tokens, *kept = turn(
                attn_ring, down_ring, up_ring, kept=(grad_tokens, *kept)
            )
        for ring, out in zip(made, kept[len(kept) - len(made) :]):
            whole[ring] = out
        return [grad_tokens, *kept[: len(kept) - len(made)]]

    grad_tokens, stacked_far, result = tokens_turn(
        0, grad_tokens, swap_bit(stacked, "mp", 0), result
    )
    grad_up_bias = jnp.sum(clock.hold(grad_pre), axis=0)
    grad_down_bias = jnp.sum(clock.hold(cotangent), axis=0)
    ups = grad_up_bias.reshape(-1, width)
    small = jnp.concatenate(
        [stacked + stacked_far, jnp.stack([gain2, bias2, grad_down_bias]), ups], 0
    )
    thin = attn_ring.rows
    extra = -(-small.shape[0] * width // (2 * thin * inner))
    side = extra * thin * inner // width
    small = jnp.pad(small, ((0, 2 * side - small.shape[0]), (0, 0)))
    small = small + swap_bit(small, "seq", 0)
    small = lax.dynamic_slice_in_dim(small, core * side, side, 0)
    turns = 1
    while attn_ring.step < hops:
        (grad_tokens,) = tokens_turn(turns, grad_tokens)
        turns += 1
    attn_ring.take(small.reshape(extra, thin, inner))
    while attn_ring.step < 2 * hops:
        (grad_tokens,) = tokens_turn(turns, grad_tokens)
        turns += 1
    gather_done()
    grad_down, grad_up = whole[down_ring][0], whole[up_ring][0]
    small = attn_ring.extra_sum().reshape(side, width)
    other = swap_bit(small, "seq", 0)
    attn_ring.own[0] = after(attn_ring.own[0], small)
    grad_qkv, grad_out = attn_ring.results()
    grad_out = jnp.transpose(grad_out[0])
    small = jnp.where(
        core == 0, jnp.concatenate([small, other], 0), jnp.concatenate([other, small], 0)
    )

    channels = in_coef.shape[0]
    at = (place_seq * lax.axis_size("mp") + lax.axis_index("mp")) * channels
    own = jnp.transpose(lax.dynamic_slice_in_dim(small[: 3 * states + 1], at, channels, 1))
    grad_in = own[:, :states]
    grad_out_coef = own[:, states : 2 * states]
    grad_decay = own[:, 2 * states : 3 * states]
    grad_skip = own[:, 3 * states]
    small = small[3 * states + 1 :]
    return (
        result,
        grad_tokens,
        small[0],
        small[1],
        grad_in,
        grad_out_coef,
        grad_decay,
        grad_skip,
        grad_qkv,
        grad_out,
        small[2],
        small[3],
        grad_up,
        small[5 : 5 + ups.shape[0]].reshape(-1),
        grad_down,
        small[4],
    )


def solution(mesh):
    owner = P(("seq", "mp"), None)
    return jax.shard_map(
        per_device,
        mesh=mesh,
        in_specs=(
            P("seq", None),
            P(None, ("seq", "mp"), None),
            P(),
            P(),
            owner,
            owner,
            owner,
            P(("seq", "mp")),
            P(None, None, "mp"),
            P("mp", None),
            P(),
            P(),
            P(None, "mp"),
            P("mp"),
            P("mp", None),
            P(),
            P("seq", None),
        ),
        out_specs=(
            P("seq", None),
            P("seq", None),
            P(),
            P(),
            owner,
            owner,
            owner,
            P(("seq", "mp")),
            P(None, None, "mp"),
            P("mp", None),
            P(),
            P(),
            P(None, "mp"),
            P("mp"),
            P("mp", None),
            P(),
        ),
        check_vma=False,
    )
```

```python
import functools
import math

import jax
import jax.numpy as jnp
from jax import lax
from jax.experimental import pallas as pl
from jax.experimental.pallas import tpu as pltpu
from jax.sharding import PartitionSpec as P

HDIM = 128
BLOCK = 512
CTX = 128
LEN = 4096
EPS = 1e-05
HIGH = lax.Precision.HIGH


def mm(left, right, dims=((1,), (0,))):
    return lax.dot_general(
        left, right, (dims, ((), ())), precision=HIGH, preferred_element_type=jnp.float32
    )


def norm_parts(value):
    center = value - jnp.mean(value, axis=-1, keepdims=True)
    spread = jnp.mean(center * center, axis=-1, keepdims=True)
    rate = lax.rsqrt(spread + EPS)
    return center * rate, rate


def norm_back(grad, unit, rate, gain):
    scaled = grad * gain
    inner = jnp.mean(scaled * unit, axis=-1, keepdims=True)
    return rate * (scaled - jnp.mean(scaled, axis=-1, keepdims=True) - unit * inner)


def swap_bit(value, axis, bit):
    size = lax.axis_size(axis)
    return lax.ppermute(value, axis, [(i, i ^ (1 << bit)) for i in range(size)])


def bits_of(count):
    return count.bit_length() - 1


def shift_in_window(value, distance, per_window):
    size = lax.axis_size("seq")
    route = [(i, i + distance) for i in range(size)]
    inside = [(a, b) for a, b in route if 0 <= b < size and a // per_window == b // per_window]
    return lax.ppermute(value, "seq", inside)


def after(value, *others):
    return lax.optimization_barrier((value,) + others)[0]


def gather_all(piece, gates=()):
    mp_size, seq_size = lax.axis_size("mp"), lax.axis_size("seq")
    me = lax.axis_index("seq") * mp_size + lax.axis_index("mp")
    block, seen = piece, []
    for bit in range(bits_of(mp_size * seq_size)):
        axis, own = ("mp", bit) if bit < bits_of(mp_size) else ("seq", bit - bits_of(mp_size))
        if gates:
            block = after(block, gates[bit])
        other = swap_bit(block, axis, own)
        upper = (me >> bit) & 1
        block = jnp.where(
            upper == 1, jnp.concatenate([other, block], 1), jnp.concatenate([block, other], 1)
        )
        seen.append(block)
    return block, seen


def trade_chips(value, distance):
    size = lax.axis_size("seq")
    return lax.ppermute(value, "seq", [(i, i ^ (2 * distance)) for i in range(size)])


def chip_order(count):
    if count <= 2:
        return list(range(count))
    return list(range(0, count, 2)) + list(range(count - 1 - count % 2, 0, -2))


def ring_route(count):
    order = chip_order(count)
    route = []
    for i in range(count):
        here, there = order[i], order[(i + 1) % count]
        route.append((2 * here, 2 * there))
        route.append((2 * there + 1, 2 * here + 1))
    return route


def ring_spot():
    count = lax.axis_size("seq") // 2
    places = [0] * count
    for i, chip in enumerate(chip_order(count)):
        places[chip] = i
    me = lax.axis_index("seq")
    here = jnp.array(places, jnp.int32)[me // 2]
    return jnp.where(me % 2 == 0, here, (count - here) % count)


def unset(shape):
    return pl.pallas_call(
        lambda out: None,
        out_shape=jax.ShapeDtypeStruct(shape, jnp.float32),
        out_specs=pl.BlockSpec(memory_space=pl.ANY),
        compiler_params=pltpu.CompilerParams(vmem_limit_bytes=1 << 20),
    )()


def pack_kernel(*refs):
    low = 0
    for ref in refs[:-1]:
        refs[-1][low : low + ref.shape[0], :] = ref[...]
        low += ref.shape[0]


def pack(parts):
    rows, cols = sum(part.shape[0] for part in parts), parts[0].shape[1]
    return pl.pallas_call(
        pack_kernel,
        out_shape=jax.ShapeDtypeStruct((rows, cols), jnp.float32),
        compiler_params=pltpu.CompilerParams(vmem_limit_bytes=1 << 20),
    )(*parts)


def pick(value, index):
    return lax.dynamic_index_in_dim(value, index, 0, keepdims=False)


class Clock:
    def __init__(self):
        self.last = ()

    def hold(self, value):
        return after(value, *self.last) if self.last else value

    def set(self, *values):
        self.last = values


def assemble_kernel(count, cuts, where_ref, *refs):
    parts, outs, sems = refs[: 2 * count], refs[2 * count : -1], refs[-1]
    copies = []
    for n in range(2 * count):
        which, spot = where_ref[0, n], where_ref[1, n]
        for out, (low, high) in zip(outs, cuts):
            copies.append(
                pltpu.make_async_copy(
                    parts[n].at[low:high], out.at[:, which, spot], sems.at[len(copies)]
                )
            )
    for copy in copies:
        copy.start()
    for copy in copies:
        copy.wait()


class Ring:
    def __init__(self, pieces, outs):
        self.count = lax.axis_size("seq") // 2
        self.place, self.route = ring_spot(), ring_route(self.count)
        self.core = lax.axis_index("seq") % 2
        self.mirror = (self.count - self.place) % self.count
        self.rows, self.cols = pieces[0][0].shape[0] // self.count, pieces[0][0].shape[1]
        self.pieces = [
            [a.reshape(self.count, self.rows, self.cols) for a in addends] for addends in pieces
        ]
        self.outs = outs
        self.step, self.own, self.far, self.extras = 0, [], [], []
        self.held = self.chunk(self.place)

    def chunk(self, spot):
        return jnp.stack([sum(pick(a, spot) for a in addends) for addends in self.pieces])

    def take(self, extra):
        self.extras = [extra]
        self.held = jnp.concatenate([self.held, extra], 0)

    def extra_sum(self):
        count = self.count
        seen = jnp.stack(self.extras)
        return sum(
            lax.dynamic_index_in_dim(seen, (self.place - i + count) % count, 0, keepdims=False)
            for i in range(count)
        )

    def turn(self, clock, kept=()):
        got = lax.ppermute(self.held, "seq", self.route)
        got, *kept = lax.optimization_barrier((got, *kept, *clock.last))[: 1 + len(kept)]
        self.step += 1
        if self.step < self.count:
            got = got + self.chunk((self.place + 2 * self.count - self.step) % self.count)
        self.held = got
        if self.step >= self.count - 1:
            self.own.append(got)
            self.far.append(swap_bit(got, "seq", 0))
        if self.extras:
            self.extras.append(got[-self.extras[0].shape[0] :])
        clock.set(got)
        return kept

    def results(self):
        count = self.count
        hops = jnp.arange(count, dtype=jnp.int32)
        spots = jnp.concatenate([self.place + 1 - hops, self.mirror + 1 - hops]) + count
        which = jnp.repeat(jnp.stack([self.core, 1 - self.core]), count)
        where = jnp.stack([which, spots % count]).astype(jnp.int32)
        cuts, low = [], 0
        for size in self.outs:
            cuts.append((low, low + size))
            low += size
        shapes = [(size, 2, count, self.rows, self.cols) for size in self.outs]
        outs = pl.pallas_call(
            functools.partial(assemble_kernel, count, cuts),
            in_specs=[pl.BlockSpec(memory_space=pltpu.SMEM)]
            + [pl.BlockSpec(memory_space=pltpu.VMEM)] * (2 * count),
            out_specs=[pl.BlockSpec(memory_space=pl.ANY)] * len(shapes),
            out_shape=[jax.ShapeDtypeStruct(shape, jnp.float32) for shape in shapes],
            scratch_shapes=[pltpu.SemaphoreType.DMA((2 * count * len(shapes),))],
            cost_estimate=pl.CostEstimate(flops=0, bytes_accessed=COST, transcendentals=0),
        )(where, *self.own, *self.far)
        return [out.reshape(out.shape[0], -1, self.cols) for out in outs]


def core_half(value, which):
    size = value.shape[1] // 2
    return lax.dynamic_slice_in_dim(value, which * size, size, 1)


def rows8(shape):
    return lax.broadcasted_iota(jnp.int32, shape, 0).astype(jnp.float32)


def tree(values):
    values = list(values)
    while len(values) > 1:
        values = [sum(values[i : i + 2]) for i in range(0, len(values), 2)]
    return values[0]


def groups(decay_ref):
    states, lanes = decay_ref.shape
    for low in range(0, lanes, 128):
        span = slice(low, low + 128)
        rates = [jnp.broadcast_to(decay_ref[n : n + 1, span], (8, 128)) for n in range(states)]
        yield span, rates, [jnp.exp(-8.0 * rate) for rate in rates]


UNROLL = 4


def over_rows(ref, count, span, body, carry):
    def step(i, carry):
        for k in range(UNROLL):
            base = pl.multiple_of((i * UNROLL + k) * 8, 8)
            carry = body(ref[pl.ds(base, 8), span], carry)
        return carry

    return lax.fori_loop(0, count // (8 * UNROLL), step, carry)


def summary_kernel(tail_ref, x_ref, decay_ref, h_ref):
    for span, rates, jump in groups(decay_ref):

        def body(tile, acc):
            return tuple(j * a + tile for j, a in zip(jump, acc))

        acc = (tail_ref[:8, span] * 0.0,) * len(rates)
        acc = over_rows(tail_ref, tail_ref.shape[0], span, body, acc)
        acc = over_rows(x_ref, x_ref.shape[0] - tail_ref.shape[0], span, body, acc)
        left = 7.0 - rows8((8, 128))
        for n, rate in enumerate(rates):
            h_ref[n : n + 1, span] = jnp.sum(acc[n] * jnp.exp(-rate * left), axis=0, keepdims=True)


def moment_kernel(tail_ref, x_ref, decay_ref, p_ref):
    for span, rates, jump in groups(decay_ref):

        def body(tile, carry):
            acc, lag = carry
            lag = tuple(j * (b + a) for j, a, b in zip(jump, acc, lag))
            return tuple(j * a + tile for j, a in zip(jump, acc)), lag

        zeros = (tail_ref[:8, span] * 0.0,) * len(rates)
        carry = over_rows(tail_ref, tail_ref.shape[0], span, body, (zeros, zeros))
        acc, lag = over_rows(x_ref, x_ref.shape[0] - tail_ref.shape[0], span, body, carry)
        left = 7.0 - rows8((8, 128))
        for n, rate in enumerate(rates):
            total = (8.0 * lag[n] + left * acc[n]) * jnp.exp(-rate * left)
            p_ref[n : n + 1, span] = jnp.sum(total, axis=0, keepdims=True)


def carry_kernel(near_ref, first_ref, decay_ref, y_ref):
    for span, rates, jump in groups(decay_ref):
        ahead = rows8((8, 128)) + 1.0
        modes = tuple(
            jnp.broadcast_to(first_ref[n : n + 1, span], (8, 128)) * jnp.exp(-rate * ahead)
            for n, rate in enumerate(rates)
        )

        def step(i, modes):
            for k in range(UNROLL):
                base = pl.multiple_of((i * UNROLL + k) * 8, 8)
                y_ref[pl.ds(base, 8), span] = near_ref[pl.ds(base, 8), span] + tree(modes)
                modes = tuple(j * m for j, m in zip(jump, modes))
            return modes

        lax.fori_loop(0, y_ref.shape[0] // (8 * UNROLL), step, modes)


def spread_kernel(first_ref, decay_ref, tail_ref, y_ref):
    for span, rates, jump in groups(decay_ref):
        ahead = 8.0 - rows8((8, 128))
        modes = tuple(
            jnp.broadcast_to(first_ref[n : n + 1, span], (8, 128)) * jnp.exp(-rate * ahead)
            for n, rate in enumerate(rates)
        )

        def run(ref, modes):
            count = ref.shape[0] // 8

            def step(i, modes):
                for k in range(UNROLL):
                    base = pl.multiple_of((count - 1 - i * UNROLL - k) * 8, 8)
                    ref[pl.ds(base, 8), span] = tree(modes)
                    modes = tuple(j * m for j, m in zip(jump, modes))
                return modes

            return lax.fori_loop(0, count // UNROLL, step, modes)

        run(tail_ref, run(y_ref, modes))


def near_kernel(x_ref, fade_ref, gate_ref, skip_ref, y_ref):
    fade, gate, skip = fade_ref[...], gate_ref[...], skip_ref[...]

    def octet(i, u):
        base = pl.multiple_of(i * 8, 8)
        tile = x_ref[pl.ds(base, 8), :]
        rows = []
        for r in range(8):
            row = tile[r : r + 1, :]
            u = fade * u + gate * jnp.broadcast_to(row, fade.shape)
            rows.append(jnp.sum(u, axis=0, keepdims=True) + skip * row)
        y_ref[pl.ds(base, 8), :] = jnp.concatenate(rows, 0)
        return u

    lax.fori_loop(0, x_ref.shape[0] // 8, octet, jnp.zeros(fade.shape, jnp.float32))


def tail_back_kernel(
    x_ref, d_ref, fade_ref, gate_ref, skip_ref, q_ref, r_ref, dh_ref, dp_ref, dskip_ref, dx_ref
):
    fade, gate, skip = fade_ref[...], gate_ref[...], skip_ref[...]
    octets = x_ref.shape[0] // 8
    zero = jnp.zeros(fade.shape, jnp.float32)

    def forward(i, carry):
        h, p, dh, dp = carry
        base = pl.multiple_of(i * 8, 8)
        tile, grads = x_ref[pl.ds(base, 8), :], d_ref[pl.ds(base, 8), :]
        for r in range(8):
            p = fade * (p + h)
            h = fade * h + jnp.broadcast_to(tile[r : r + 1, :], fade.shape)
            grad = jnp.broadcast_to(grads[r : r + 1, :], fade.shape)
            dh = dh + grad * h
            dp = dp + grad * p
        return h, p, dh, dp

    _, _, dh, dp = lax.fori_loop(0, octets, forward, (zero, zero, zero, zero))
    dh_ref[...] = dh
    dp_ref[...] = dp
    dskip_ref[...] = jnp.sum(x_ref[...] * d_ref[...], axis=0, keepdims=True)

    def backward(k, carry):
        q, r_sum = carry
        base = pl.multiple_of((octets - 1 - k) * 8, 8)
        grads = d_ref[pl.ds(base, 8), :]
        rows = [None] * 8
        for r in reversed(range(8)):
            r_sum = fade * (r_sum + q)
            grad = grads[r : r + 1, :]
            q = fade * q + jnp.broadcast_to(grad, fade.shape)
            rows[r] = jnp.sum(gate * q, axis=0, keepdims=True) + skip * grad
        dx_ref[pl.ds(base, 8), :] = jnp.concatenate(rows, 0)
        return q, r_sum

    q, r_sum = lax.fori_loop(0, octets, backward, (zero, zero))
    q_ref[...] = q
    r_ref[...] = r_sum


def by_channels(kernel, ins, outs, cut=512):
    width = ins[0].shape[1]
    cut = cut if width % cut == 0 else width

    def spec(rows):
        return pl.BlockSpec((rows, cut), lambda i: (0, i))

    return pl.pallas_call(
        kernel,
        grid=(width // cut,),
        in_specs=[spec(a.shape[0]) for a in ins],
        out_specs=[spec(r) for r in outs],
        out_shape=[jax.ShapeDtypeStruct((r, width), jnp.float32) for r in outs],
        cost_estimate=pl.CostEstimate(flops=0, bytes_accessed=COST, transcendentals=0),
        compiler_params=pltpu.CompilerParams(vmem_limit_bytes=12 << 20),
    )(*ins)


def cut(value):
    top = value.astype(jnp.bfloat16)
    return top, (value - top.astype(jnp.float32)).astype(jnp.bfloat16)


def dot3(left, right, dims):
    def one(a, b):
        return lax.dot_general(a, b, (dims, ((), ())), preferred_element_type=jnp.float32)

    return one(left[0], right[1]) + one(left[1], right[0]) + one(left[0], right[0])


NT = ((1,), (1,))
NN = ((1,), (0,))
TN = ((0,), (0,))
TILE = 256
COST = 1024
SCALE = HDIM ** (-0.5)


def causal(shape, first_row):
    row = lax.broadcasted_iota(jnp.int32, shape, 0) + first_row
    return lax.broadcasted_iota(jnp.int32, shape, 1) <= row


def self_kernel(q_ref, k_ref, v_ref, acc_ref, top_ref):
    rows = q_ref.shape[0]
    k, v = cut(k_ref[...]), cut(v_ref[...])
    for first in range(0, rows, TILE):
        span = slice(first, first + TILE)
        seen = first + TILE
        q = cut(q_ref[span, :] * SCALE)
        scores = dot3(q, (k[0][:seen], k[1][:seen]), NT)
        scores = jnp.where(causal(scores.shape, first), scores, -1e30)
        top = jnp.max(scores, axis=1, keepdims=True)
        weight = jnp.exp(scores - top)
        acc_ref[span, :] = dot3(cut(weight), (v[0][:seen], v[1][:seen]), NN)
        total = jnp.sum(weight, axis=1, keepdims=True)
        lane = lax.broadcasted_iota(jnp.int32, (TILE, HDIM), 1)
        top_ref[span, :] = jnp.where(lane < HDIM // 2, top, total)


def ctx_kernel(ok_ref, q_ref, k_ref, v_ref, acc_ref, top_ref, out_ref, log_ref):
    ok = ok_ref[0] > 0
    q = cut(q_ref[...] * SCALE)
    scores = dot3(q, cut(k_ref[...]), NT)
    scores = jnp.where(ok, scores, -1e30)
    near, near_sum = top_ref[:, :1], top_ref[:, HDIM // 2 : HDIM // 2 + 1]
    top = jnp.maximum(near, jnp.max(scores, axis=1, keepdims=True))
    weight = jnp.where(ok, jnp.exp(scores - top), 0.0)
    ease = jnp.exp(near - top)
    total = near_sum * ease + jnp.sum(weight, axis=1, keepdims=True)
    out_ref[...] = (acc_ref[...] * ease + dot3(cut(weight), cut(v_ref[...]), NN)) / total
    log_ref[...] = jnp.broadcast_to(top + jnp.log(total), log_ref.shape)


def back_kernel(ok_ref, q_ref, k_ref, v_ref, kc_ref, vc_ref, o_ref, l_ref, g_ref, d_ref):
    ok = ok_ref[0] > 0
    rows = q_ref.shape[0]
    k, v, kc, vc = cut(k_ref[...]), cut(v_ref[...]), cut(kc_ref[...]), cut(vc_ref[...])
    d_ref[0, :CTX, :] = jnp.zeros((CTX, HDIM), jnp.float32)
    for first in reversed(range(0, rows, TILE)):
        seen = first + TILE
        span = slice(first, seen)
        grad = g_ref[span, :]
        q = cut(q_ref[span, :] * SCALE)
        grad2 = cut(grad)
        inner = jnp.sum(grad * o_ref[span, :], axis=1, keepdims=True)
        mark = l_ref[span, :][:, :1]
        ks, vs = (k[0][:seen], k[1][:seen]), (v[0][:seen], v[1][:seen])
        probs = dot3(q, ks, NT)
        probs = jnp.where(causal(probs.shape, first), jnp.exp(probs - mark), 0.0)
        probs_c = jnp.where(ok, jnp.exp(dot3(q, kc, NT) - mark), 0.0)
        ds = cut(probs * (dot3(grad2, vs, NT) - inner))
        ds_c = cut(probs_c * (dot3(grad2, vc, NT) - inner))
        probs, probs_c = cut(probs), cut(probs_c)
        d_ref[0, CTX + first : CTX + seen, :] = (dot3(ds, ks, NN) + dot3(ds_c, kc, NN)) * SCALE
        for at, (own, ctx, other) in enumerate([(ds, ds_c, q), (probs, probs_c, grad2)]):
            near, back = dot3(own, other, TN), dot3(ctx, other, TN)
            if seen == rows:
                d_ref[1 + at, CTX:, :] = near
                d_ref[1 + at, :CTX, :] = back
            else:
                d_ref[1 + at, CTX : CTX + seen, :] += near
                d_ref[1 + at, :CTX, :] += back


def by_heads(kernel, ins, outs, scalars=()):
    heads = ins[0][0].shape[-1] // HDIM
    specs = [pl.BlockSpec(memory_space=pltpu.SMEM) for _ in scalars]
    for _, rows, *at in ins:
        if len(at) == 2:
            specs.append(pl.BlockSpec((None, rows, HDIM), lambda h, at=at: (at[1], at[0], h)))
        else:
            specs.append(pl.BlockSpec((rows, HDIM), lambda h, at=at: (at[0], h)))
    return pl.pallas_call(
        kernel,
        grid=(heads,),
        in_specs=specs,
        out_specs=[
            pl.BlockSpec(lead + (HDIM,), lambda h, n=len(lead): (0,) * n + (h,)) for lead in outs
        ],
        out_shape=[jax.ShapeDtypeStruct(lead + (heads * HDIM,), jnp.float32) for lead in outs],
        cost_estimate=pl.CostEstimate(flops=0, bytes_accessed=COST, transcendentals=0),
        compiler_params=pltpu.CompilerParams(vmem_limit_bytes=16 << 20),
    )(*scalars, *[a[0] for a in ins])


def project_kernel(x_ref, w_ref, out_ref, high_ref, low_ref):
    @pl.when(pl.program_id(0) == 0)
    def _():
        high_ref[...], low_ref[...] = cut(x_ref[...])

    def one(part):
        return lax.dot_general(
            part, w_ref[...], (NN, ((), ())), preferred_element_type=jnp.float32
        )

    out_ref[...] = one(low_ref[...]) + one(high_ref[...])


def project(x, weights, first, count):
    rows, depth = x.shape
    width = weights.shape[2]
    return pl.pallas_call(
        project_kernel,
        grid=(count,),
        in_specs=[
            pl.BlockSpec((rows, depth), lambda i: (0, 0)),
            pl.BlockSpec((None, depth, width), lambda i: (first + i, 0, 0)),
        ],
        out_specs=pl.BlockSpec((None, rows, width), lambda i: (i, 0, 0)),
        out_shape=jax.ShapeDtypeStruct((count, rows, width), jnp.float32),
        scratch_shapes=[pltpu.VMEM((rows, depth), jnp.bfloat16)] * 2,
        cost_estimate=pl.CostEstimate(flops=0, bytes_accessed=COST, transcendentals=0),
        compiler_params=pltpu.CompilerParams(vmem_limit_bytes=16 << 20),
    )(x, weights)


def per_device(
    tokens,
    window_state,
    norm1_gain,
    norm1_bias,
    in_coef,
    out_coef,
    decay_rate,
    skip_gain,
    qkv_weight,
    out_weight,
    norm2_gain,
    norm2_bias,
    up_weight,
    up_bias,
    down_weight,
    down_bias,
    cotangent,
):
    place_seq = lax.axis_index("seq")
    core = place_seq % 2
    rows, width = tokens.shape
    states = in_coef.shape[1]
    windows = window_state.shape[0]
    per_window = LEN // rows
    block = place_seq % per_window
    window = place_seq // per_window
    has_ctx = block > 0
    ok = has_ctx.astype(jnp.int32).reshape(1)
    half = rows // 2

    qkv = qkv_weight.astype(jnp.float32)
    out_own = out_weight.astype(jnp.float32)
    up = up_weight.astype(jnp.float32)
    down = down_weight.astype(jnp.float32)

    coefs, rounds = gather_all(
        pack(
            [jnp.transpose(a) for a in (decay_rate, in_coef, out_coef)]
            + [jnp.transpose(window_state[w]) for w in range(windows)]
            + [skip_gain[None]]
        )
    )
    decay, c_in, c_out = (coefs[i * states : (i + 1) * states] for i in range(3))
    carried = lax.dynamic_slice_in_dim(coefs, (3 + window) * states, states, 0)
    skip = coefs[(3 + windows) * states :]
    gate = c_in * c_out
    fade = jnp.exp(-decay)

    def faded(steps):
        return jnp.exp(-decay * steps)

    inner = out_own.shape[0]
    sent = pick(out_weight.reshape(2, inner // 2, width), core).astype(jnp.float32)
    across = swap_bit(after(sent, rounds[1]), "mp", 0)
    beside = swap_bit(across, "seq", 0)
    out_far = jnp.where(
        core == 0, jnp.concatenate([across, beside], 0), jnp.concatenate([beside, across], 0)
    )

    unit1, rate1 = norm_parts(tokens)
    normed = after(unit1 * norm1_gain + norm1_bias)
    tail = shift_in_window(normed[rows - CTX :], 1, per_window)
    qkv_rows = project(normed, qkv_weight, 0, 3)
    acc, top = by_heads(
        self_kernel,
        [(qkv_rows, rows, 0, i) for i in range(3)],
        [(rows,)] * 2,
    )

    length = float(rows)
    chips = per_window // 2
    chip = block // 2
    (sum_h,) = by_channels(
        summary_kernel,
        [tail, after(normed, acc), decay],
        [states],
    )

    def pair_order(value):
        other = swap_bit(value, "seq", 0)
        return jnp.where(core == 0, value, other), jnp.where(core == 0, other, value)

    first_h, second_h = pair_order(sum_h)
    both_h = faded(length) * first_h + second_h
    far_h = [trade_chips(both_h, d) for d in range(1, chips)]
    (near,) = by_channels(
        near_kernel, [after(tail, sum_h), fade, gate, skip], [CTX]
    )
    far_h = [after(h, near) for h in far_h]
    past_h = jnp.zeros_like(sum_h)
    for d in range(1, chips):
        there = chip ^ d
        gap = jnp.maximum(chip - 1 - there, 0).astype(jnp.float32) * (2.0 * length)
        past_h = past_h + jnp.where(there < chip, faded(gap) * far_h[d - 1], 0.0)
    chip_h = past_h
    past_h = jnp.where(core == 0, past_h, faded(length) * past_h + first_h)

    start_t = jnp.maximum(block * rows - CTX, 0).astype(jnp.float32)
    first = c_out * (c_in * past_h + carried * faded(start_t))

    (context,) = by_channels(
        carry_kernel, [near, first, decay], [CTX]
    )
    kv_ctx = project(context, qkv_weight, 1, 2)
    heads, logs, far = [], [], []
    for part in range(2):
        o, l = by_heads(
            ctx_kernel,
            [(qkv_rows, half, part, 0), (after(kv_ctx, *heads), CTX, 0, 0), (kv_ctx, CTX, 0, 1)]
            + [(a, half, part) for a in (acc, top)],
            [(half,)] * 2,
            scalars=(ok,),
        )
        heads.append(o)
        logs.append(l)
        far.append(swap_bit(o, "mp", 0))
    grad_hidden = mm(after(cotangent, *heads), down, NT)
    seen = jnp.concatenate([after(context, *heads), normed], 0)
    outs = jnp.concatenate(heads, 0)
    log = jnp.concatenate(logs, 0)

    hidden, grad_pre = unset((rows, up.shape[1])), unset((rows, up.shape[1]))
    normed2 = unset((rows, width))
    mixed, part2 = [], []
    for part in range(2):
        span = slice(part * half, (part + 1) * half)
        came = after(far[part], part2[0]) if part else after(far[0], seen, outs, log, grad_hidden)
        m = tokens[span] + (mm(heads[part], out_own) + mm(came, out_far))
        n = norm_parts(m)[0] * norm2_gain + norm2_bias
        pre = mm(n, up) + up_bias
        cdf = 0.5 + 0.5 * lax.erf(pre * (0.5**0.5))
        bell = jnp.exp(-0.5 * pre * pre) * (1.0 / math.sqrt(2.0 * math.pi))
        hidden = lax.dynamic_update_slice(hidden, pre * cdf, (part * half, 0))
        slope = grad_hidden[span] * (cdf + pre * bell)
        grad_pre = lax.dynamic_update_slice(grad_pre, slope, (part * half, 0))
        normed2 = lax.dynamic_update_slice(normed2, n, (part * half, 0))
        mixed.append(m)
        if part == 0:
            part2.append(mm(grad_pre[span], up, NT))

    clock = Clock()
    give = mm(core_half(after(hidden, part2[0]), 1 - core), cotangent, TN)
    keep = mm(core_half(after(hidden, give), core), cotangent, TN)
    down_ring = Ring([[keep, swap_bit(give, "seq", 0)]], (1,))
    clock.set(down_ring.held)
    part2.append(mm(clock.hold(grad_pre)[half:], up, NT))
    clock.set(part2[1])
    gots2 = [swap_bit(p, "mp", 0) for p in part2]
    mixed = jnp.concatenate(mixed, 0)
    grad_mixed, grad_heads = unset((rows, width)), []
    gain2, bias2 = 0.0, 0.0

    def norm2_half(part, grad_mixed, gain2, bias2):
        span = slice(part * half, (part + 1) * half)
        grad2 = part2[part] + after(gots2[part], *clock.last)
        unit2, rate2 = norm_parts(after(mixed, grad2)[span])
        gain2 = gain2 + jnp.sum(grad2 * unit2, axis=0)
        bias2 = bias2 + jnp.sum(grad2, axis=0)
        new = cotangent[span] + norm_back(grad2, unit2, rate2, norm2_gain)
        grad_mixed = lax.dynamic_update_slice(grad_mixed, new, (part * half, 0))
        clock.set(grad_mixed, gain2, bias2)
        return grad_mixed, gain2, bias2

    hops = down_ring.count - 1

    def turn(*rings, kept=()):
        rings = [ring for ring in rings if ring.step < 2 * hops]
        for ring in rings[:-1]:
            ring.turn(clock)
        return rings[-1].turn(clock, kept)

    (gots2[0],) = turn(down_ring, kept=(gots2[0],))
    give = mm(core_half(clock.hold(normed2), 1 - core), grad_pre, TN)
    clock.set(give)
    grad_mixed, gain2, bias2 = norm2_half(0, grad_mixed, gain2, bias2)
    keep = mm(core_half(clock.hold(normed2), core), grad_pre, TN) + swap_bit(give, "seq", 0)
    up_ring = Ring([[keep]], (1,))
    clock.set(up_ring.held)
    (gots2[1],) = turn(down_ring, kept=(gots2[1],))
    grad_mixed, gain2, bias2 = norm2_half(1, grad_mixed, gain2, bias2)
    grad_heads = mm(clock.hold(grad_mixed), out_own, NT)
    clock.set(grad_heads)
    turn(down_ring, up_ring)

    (grads,) = by_heads(
        back_kernel,
        [(qkv_rows, rows, 0, i) for i in range(3)]
        + [(kv_ctx, CTX, 0, i) for i in range(2)]
        + [(a, rows, 0) for a in (outs, log, clock.hold(grad_heads))],
        [(3, CTX + rows)],
        scalars=(ok,),
    )
    clock.set(grads)
    turn(down_ring, up_ring)
    gives = [mm(core_half(clock.hold(seen), 1 - core), grads[i], TN) for i in range(3)]
    gives.append(mm(core_half(clock.hold(grad_mixed), 1 - core), outs, TN))
    gots = [swap_bit(g, "seq", 0) for g in gives]
    clock.set(*gives)
    turn(down_ring, up_ring)
    keeps = [mm(core_half(clock.hold(seen), core), grads[i], TN) + gots[i] for i in range(3)]
    keeps.append(mm(core_half(clock.hold(grad_mixed), core), outs, TN) + gots[3])
    attn_ring = Ring([[k] for k in keeps], (3, 1))
    clock.set(attn_ring.held)

    feed = mm(clock.hold(hidden), down)
    clock.set(feed)
    turn(attn_ring, down_ring, up_ring)
    grad_seen = sum(mm(clock.hold(grads)[i], qkv[i], NT) for i in range(3))
    grad_context = jnp.where(has_ctx, grad_seen[:CTX], 0.0)
    clock.set(grad_seen)
    quarter = rows // 4
    result, grad_tokens = unset((rows, width)), unset((rows, width))

    def across(source, k, into, base, kept=()):
        span = slice(k * quarter, (k + 1) * quarter)
        got = swap_bit(source[span], "mp", 0)
        got, into, *kept = turn(attn_ring, down_ring, up_ring, kept=(got, into, *kept))
        new = base(span) + (source[span] + got)
        return [lax.dynamic_update_slice(into, new, (k * quarter, 0)), *kept]

    def result_base(span):
        return mixed[span] + down_bias

    (result,) = across(feed, 0, result, result_base)

    sum_q, sum_r, part_h, part_p, part_skip, grad_tail = by_channels(
        tail_back_kernel,
        [tail, clock.hold(grad_context), fade, gate, skip],
        [states, states, states, states, 1, CTX],
    )
    clock.set(sum_q)
    (result,) = across(feed, 1, result, result_base)
    (sum_p,) = by_channels(moment_kernel, [tail, clock.hold(normed), decay], [states])
    clock.set(sum_p)
    other = swap_bit(jnp.concatenate([sum_p, sum_q], 0), "seq", 0)
    other_p, other_q = other[:states], other[states:]
    first_p, second_p = jnp.where(core == 0, sum_p, other_p), jnp.where(core == 0, other_p, sum_p)
    first_q, second_q = jnp.where(core == 0, sum_q, other_q), jnp.where(core == 0, other_q, sum_q)
    both_p = faded(length) * (first_p + length * first_h) + second_p
    both_q = first_q + faded(length) * second_q
    both = jnp.concatenate([both_p, both_q], 0)
    clock.set(both)
    past_p = jnp.zeros_like(sum_p)
    later = jnp.zeros_like(sum_q)
    came = [trade_chips(both, d) for d in range(1, chips)]
    (result,) = across(feed, 2, result, result_base)
    came[0] = clock.hold(came[0])
    for d in range(1, chips):
        there = chip ^ d
        gap = (jnp.maximum(jnp.abs(chip - there) - 1, 0)).astype(jnp.float32) * (2.0 * length)
        near_p, near_q = came[d - 1][:states], came[d - 1][states:]
        fading = faded(gap)
        past_p = past_p + jnp.where(there < chip, fading * (near_p + gap * far_h[d - 1]), 0.0)
        later = later + jnp.where(there > chip, fading * near_q, 0.0)
    past_p = jnp.where(core == 0, past_p, faded(length) * (past_p + length * chip_h) + first_p)
    later = jnp.where(core == 1, later, second_q + faded(length) * later)
    far_tail, grad_rows = by_channels(
        spread_kernel,
        [gate * later, decay],
        [CTX, rows - CTX],
    )
    to_last = far_tail + grad_tail
    clock.set(to_last)
    from_next = shift_in_window(to_last, -1, per_window)
    (result,) = across(feed, 3, result, result_base)
    along_h = fade * clock.hold(past_h) * sum_q + part_h
    along_p = fade * (past_h * (sum_r + sum_q) + past_p * sum_q) + part_p
    gone = faded(start_t + 1.0)
    part_in = c_out * along_h
    part_out = c_in * along_h + carried * gone * sum_q
    part_decay = -gate * along_p - c_out * carried * gone * ((start_t + 1.0) * sum_q + sum_r)
    clock.set(part_in, part_out, part_decay)

    grad_normed = grad_seen[CTX:] + jnp.concatenate([grad_rows, clock.hold(from_next)], 0)
    part_gain1 = jnp.sum(grad_normed * unit1, axis=0, keepdims=True)
    part_bias1 = jnp.sum(grad_normed, axis=0, keepdims=True)
    part_tokens = norm_back(grad_normed, unit1, rate1, norm1_gain)
    clock.set(part_tokens, part_gain1, part_bias1)
    turn(attn_ring, down_ring, up_ring)
    stacked = jnp.concatenate([part_in, part_out, part_decay, part_skip, part_gain1, part_bias1], 0)
    whole = {}

    def gather_done():
        made = []
        for ring in (down_ring, up_ring):
            if ring.step == 2 * hops and ring not in whole:
                ring.own[0] = clock.hold(ring.own[0])
                whole[ring] = ring.results()[0]
                made.append(ring)
        return made

    def tokens_turn(k, grad_tokens, *kept):
        made = gather_done()
        kept = [*kept, *[whole[ring] for ring in made]]
        if k < 4:
            grad_tokens, *kept = across(
                part_tokens, k, grad_tokens, lambda span: grad_mixed[span], kept
            )
        else:
            grad_tokens, *kept = turn(
                attn_ring, down_ring, up_ring, kept=(grad_tokens, *kept)
            )
        for ring, out in zip(made, kept[len(kept) - len(made) :]):
            whole[ring] = out
        return [grad_tokens, *kept[: len(kept) - len(made)]]

    grad_tokens, stacked_far, result = tokens_turn(
        0, grad_tokens, swap_bit(stacked, "mp", 0), result
    )
    grad_up_bias = jnp.sum(clock.hold(grad_pre), axis=0)
    grad_down_bias = jnp.sum(clock.hold(cotangent), axis=0)
    ups = grad_up_bias.reshape(-1, width)
    small = jnp.concatenate(
        [stacked + stacked_far, jnp.stack([gain2, bias2, grad_down_bias]), ups], 0
    )
    thin = attn_ring.rows
    extra = -(-small.shape[0] * width // (2 * thin * inner))
    side = extra * thin * inner // width
    small = jnp.pad(small, ((0, 2 * side - small.shape[0]), (0, 0)))
    small = small + swap_bit(small, "seq", 0)
    small = lax.dynamic_slice_in_dim(small, core * side, side, 0)
    turns = 1
    while attn_ring.step < hops:
        (grad_tokens,) = tokens_turn(turns, grad_tokens)
        turns += 1
    attn_ring.take(small.reshape(extra, thin, inner))
    while attn_ring.step < 2 * hops:
        (grad_tokens,) = tokens_turn(turns, grad_tokens)
        turns += 1
    gather_done()
    grad_down, grad_up = whole[down_ring][0], whole[up_ring][0]
    small = attn_ring.extra_sum().reshape(side, width)
    other = swap_bit(small, "seq", 0)
    attn_ring.own[0] = after(attn_ring.own[0], small)
    grad_qkv, grad_out = attn_ring.results()
    grad_out = jnp.transpose(grad_out[0])
    small = jnp.where(
        core == 0, jnp.concatenate([small, other], 0), jnp.concatenate([other, small], 0)
    )

    channels = in_coef.shape[0]
    at = (place_seq * lax.axis_size("mp") + lax.axis_index("mp")) * channels
    own = jnp.transpose(lax.dynamic_slice_in_dim(small[: 3 * states + 1], at, channels, 1))
    grad_in = own[:, :states]
    grad_out_coef = own[:, states : 2 * states]
    grad_decay = own[:, 2 * states : 3 * states]
    grad_skip = own[:, 3 * states]
    small = small[3 * states + 1 :]
    return (
        result,
        grad_tokens,
        small[0],
        small[1],
        grad_in,
        grad_out_coef,
        grad_decay,
        grad_skip,
        grad_qkv,
        grad_out,
        small[2],
        small[3],
        grad_up,
        small[5 : 5 + ups.shape[0]].reshape(-1),
        grad_down,
        small[4],
    )


def solution(mesh):
    owner = P(("seq", "mp"), None)
    return jax.shard_map(
        per_device,
        mesh=mesh,
        in_specs=(
            P("seq", None),
            P(None, ("seq", "mp"), None),
            P(),
            P(),
            owner,
            owner,
            owner,
            P(("seq", "mp")),
            P(None, None, "mp"),
            P("mp", None),
            P(),
            P(),
            P(None, "mp"),
            P("mp"),
            P("mp", None),
            P(),
            P("seq", None),
        ),
        out_specs=(
            P("seq", None),
            P("seq", None),
            P(),
            P(),
            owner,
            owner,
            owner,
            P(("seq", "mp")),
            P(None, None, "mp"),
            P("mp", None),
            P(),
            P(),
            P(None, "mp"),
            P("mp"),
            P("mp", None),
            P(),
        ),
        check_vma=False,
    )
```
